32 devices in a mesh: rep: 1, ctx: 32 (over z, y, x, core), fsdp: 1.
Axes of the slice: x: 2, y: 2, z: 4, core: 2. Of those that a mesh axis runs over, the one named last changes fastest.
Arguments:
- projected_queries: bfloat16 [4096, 2, 2048], P(('rep', 'ctx'), None, 'fsdp'), may hold values from -5 to 5
- projected_keys: bfloat16 [4096, 2, 256], P(('rep', 'ctx'), None, 'fsdp'), may hold values from -5 to 5
- projected_values: bfloat16 [4096, 2, 256], P(('rep', 'ctx'), None, 'fsdp'), may hold values from -6 to 6
- output_gradient: bfloat16 [4096, 2, 2048], P(('rep', 'ctx'), None, 'fsdp'), may hold values from -24 to 24
- normed_layer_input: bfloat16 [4096, 8192], P(('rep', 'ctx'), 'fsdp'), may hold values from -6 to 6
- segment: int32 [4096], P('rep'), may hold values from 0 to 2, as said below
- query_adapter_down: bfloat16 [16, 8192], P(None, 'fsdp'), may hold values from -0.0625 to 0.0625
- query_adapter_up: bfloat16 [16, 2, 2048], P(None, None, 'fsdp'), may hold values from -1.5 to 1.5
- value_adapter_down: bfloat16 [16, 8192], P(None, 'fsdp'), may hold values from -0.0625 to 0.0625
- value_adapter_up: bfloat16 [16, 2, 256], P(None, None, 'fsdp'), may hold values from -1.5 to 1.5
Outputs:
- grad_query: bfloat16 [4096, 2, 2048], P(('rep', 'ctx'), None, 'fsdp')
- grad_key: bfloat16 [4096, 2, 256], P(('rep', 'ctx'), None, 'fsdp')
- grad_value: bfloat16 [4096, 2, 256], P(('rep', 'ctx'), None, 'fsdp')
- query_down_gradient: float32 [16, 8192], P('rep', 'fsdp')
- query_up_gradient: float32 [16, 2, 2048], P('rep', None, 'fsdp')
- value_down_gradient: float32 [16, 8192], P('rep', 'fsdp')
- value_up_gradient: float32 [16, 2, 256], P('rep', None, 'fsdp')
The draws below stay inside these ranges and needn't reach their ends.
Inputs may be any that keep to these rules, and one draw needn't show every extreme that they name: `segment`: documents are packed cyclically: ids rise by one at each of two boundaries, and a third boundary returns to id 0, whose document continues at the start of the token order; all boundaries lie at least 1024 tokens from both ends.
All inputs are finite; a program needn't handle non-finite values.
Results may differ from the reference program's by a relative error of at most 0.0079.
Values may be sent and summed in bfloat16 or wider, within the bound.
A program may use at most 64 MiB of HBM per device.

```python
import jax
import jax.numpy as jnp
from jax import lax

MODEL_WIDTH = 8192
QUERY_HEADS = 32
KEY_VALUE_HEADS = 4
HEAD_SIZE = 128
ADAPTER_RANK = 16
GROUP = 1024
DOCUMENT_TOKENS = 4096


def unsigned_field(key, array_shape):
    return jnp.clip(jax.random.normal(key, array_shape, jnp.float32), -5.0, 5.0)


def draw_projected_keys(key, part):
    sign_field = unsigned_field(jax.random.fold_in(key, 11), (DOCUMENT_TOKENS, 2, KEY_VALUE_HEADS // 2 * HEAD_SIZE))
    return sign_field.astype(jnp.bfloat16)


def draw_projected_queries(key, part):
    sign_field = unsigned_field(jax.random.fold_in(key, 13), (DOCUMENT_TOKENS, 2, QUERY_HEADS // 2 * HEAD_SIZE))
    return sign_field.astype(jnp.bfloat16)


def draw_segment(key, part):
    span_count = DOCUMENT_TOKENS - 2 * GROUP + 1
    order = jax.random.permutation(jax.random.fold_in(key, 41), span_count)
    cuts = jnp.sort(order[:3].astype(jnp.int32)) + GROUP
    positions = jnp.arange(DOCUMENT_TOKENS, dtype=jnp.int32)
    passed = jnp.sum((positions[:, None] >= cuts[None, :]).astype(jnp.int32), axis=1)
    return jnp.where(passed == 3, 0, passed).astype(jnp.int32)


def levels(rng, extent, cuts, least, largest):
    def one(axis_at, parts):
        heights = jax.random.uniform(jax.random.fold_in(jax.random.fold_in(rng, 6), axis_at), (parts,), jnp.float32, least / len(cuts), largest / len(cuts))
        return jnp.repeat(jnp.exp(heights), extent[axis_at] // parts).reshape((-1,) + (1,) * (len(extent) - axis_at - 1))

    gain = one(*cuts[0])
    for cut in cuts[1:]:
        gain = gain * one(*cut)
    return gain


def centred(rng, extent, width, reach, cuts=(), kind=jnp.bfloat16):
    values = jax.random.normal(rng, extent, jnp.float32) * width
    if len(cuts) > 0:
        values = levels(rng, extent, cuts, -0.22, 0.18) * values
    return jnp.clip(values, min=-reach, max=reach).astype(kind)


def setup_inputs(seed: int = 0, part: int = 0) -> dict:
    seeds = jax.random.split(jax.random.key(seed), 11)
    part_keys = jax.random.split(jax.random.fold_in(seeds[10], part), 11)
    projected_queries = draw_projected_queries(jax.random.fold_in(jax.random.fold_in(seeds[10], part), 71), part)
    projected_keys = draw_projected_keys(jax.random.fold_in(jax.random.fold_in(seeds[10], part), 71), part)
    projected_values = centred(part_keys[2], (DOCUMENT_TOKENS, 2, KEY_VALUE_HEADS // 2 * HEAD_SIZE), 1.0, 6.0, ((0, 32),))
    output_gradient = centred(part_keys[3], (DOCUMENT_TOKENS, 2, QUERY_HEADS // 2 * HEAD_SIZE), 4.0, 24.0, ((0, 32),))
    normed_layer_input = centred(part_keys[4], (DOCUMENT_TOKENS, MODEL_WIDTH), 1.0, 6.0, ((0, 32),))
    segment = draw_segment(jax.random.fold_in(jax.random.fold_in(seeds[10], part), 71), part)
    query_adapter_down = centred(seeds[6], (ADAPTER_RANK, MODEL_WIDTH), MODEL_WIDTH ** -0.5, 0.0625)
    query_adapter_up = centred(seeds[7], (ADAPTER_RANK, 2, QUERY_HEADS // 2 * HEAD_SIZE), ADAPTER_RANK ** -0.5, 1.5)
    value_adapter_down = centred(seeds[8], (ADAPTER_RANK, MODEL_WIDTH), MODEL_WIDTH ** -0.5, 0.0625)
    value_adapter_up = centred(seeds[9], (ADAPTER_RANK, 2, KEY_VALUE_HEADS // 2 * HEAD_SIZE), ADAPTER_RANK ** -0.5, 1.5)
    return dict(projected_queries=projected_queries, projected_keys=projected_keys, projected_values=projected_values, output_gradient=output_gradient, normed_layer_input=normed_layer_input, segment=segment, query_adapter_down=query_adapter_down, query_adapter_up=query_adapter_up, value_adapter_down=value_adapter_down, value_adapter_up=value_adapter_up)


adapter_scale = 2.0


def group_backward(items):
    query_part, grad_part, key_rows, value_rows, doc_ids = items
    scaling = HEAD_SIZE ** -0.5
    query_wide = query_part.astype(jnp.float32)
    grad_wide = grad_part.astype(jnp.float32)
    key_wide = key_rows.astype(jnp.float32)
    value_wide = value_rows.astype(jnp.float32)
    positions = jnp.arange(GROUP, dtype=jnp.int32)
    allowed = (positions[None, :] <= positions[:, None]) & (doc_ids[None, :] == doc_ids[:, None])
    scores = jnp.einsum("tgrd,lgd->tgrl", query_wide, key_wide) * scaling
    scores = jnp.where(allowed[:, None, None, :], scores, -jnp.inf)
    highest = jnp.max(scores, axis=-1, keepdims=True)
    weights = jnp.exp(scores - highest)
    weights = weights / jnp.sum(weights, axis=-1, keepdims=True)
    rounded = lax.optimization_barrier(weights.astype(jnp.bfloat16)).astype(jnp.float32)
    output = jnp.einsum("tgrl,lgd->tgrd", rounded, value_wide)
    row_dot = jnp.sum(grad_wide * output, axis=-1, keepdims=True)
    grad_weights = jnp.einsum("tgrd,lgd->tgrl", grad_wide, value_wide)
    grad_scores = lax.optimization_barrier((weights * (grad_weights - row_dot)).astype(jnp.bfloat16)).astype(jnp.float32)
    query_grad = jnp.einsum("tgrl,lgd->tgrd", grad_scores, key_wide) * scaling
    key_grad = jnp.einsum("tgrl,tgrd->lgd", grad_scores, query_wide) * scaling
    value_grad = jnp.einsum("tgrl,tgrd->lgd", rounded, grad_wide)
    return query_grad, key_grad, value_grad


def reference(projected_queries, projected_keys, projected_values, output_gradient, normed_layer_input, segment, query_adapter_down, query_adapter_up, value_adapter_down, value_adapter_up):
    key_value_heads = KEY_VALUE_HEADS // 2
    head_repeat = QUERY_HEADS // KEY_VALUE_HEADS
    groups = DOCUMENT_TOKENS // GROUP
    query_grads = []
    key_grads = []
    value_grads = []
    for half_index in range(2):
        offset = half_index * (GROUP // 2)
        query_part = jnp.roll(projected_queries[:, half_index], -offset, axis=0).reshape(groups, GROUP, key_value_heads, head_repeat, HEAD_SIZE)
        grad_part = jnp.roll(output_gradient[:, half_index], -offset, axis=0).reshape(groups, GROUP, key_value_heads, head_repeat, HEAD_SIZE)
        key_rows = jnp.roll(projected_keys[:, half_index], -offset, axis=0).reshape(groups, GROUP, key_value_heads, HEAD_SIZE)
        value_rows = jnp.roll(projected_values[:, half_index], -offset, axis=0).reshape(groups, GROUP, key_value_heads, HEAD_SIZE)
        doc_ids = jnp.roll(segment, -offset).reshape(groups, GROUP)
        query_grad, key_grad, value_grad = lax.map(group_backward, (query_part, grad_part, key_rows, value_rows, doc_ids))
        query_grads.append(jnp.roll(query_grad.reshape(DOCUMENT_TOKENS, -1), offset, axis=0))
        key_grads.append(jnp.roll(key_grad.reshape(DOCUMENT_TOKENS, -1), offset, axis=0))
        value_grads.append(jnp.roll(value_grad.reshape(DOCUMENT_TOKENS, -1), offset, axis=0))
    grad_query = jnp.stack(query_grads, axis=1).astype(jnp.bfloat16)
    grad_key = jnp.stack(key_grads, axis=1).astype(jnp.bfloat16)
    grad_value = jnp.stack(value_grads, axis=1).astype(jnp.bfloat16)
    query_flattened_rows = grad_query.reshape(DOCUMENT_TOKENS, -1)
    value_flattened_rows = grad_value.reshape(DOCUMENT_TOKENS, -1)
    query_down_part = jnp.dot(normed_layer_input, query_adapter_down.T, preferred_element_type=jnp.float32).astype(jnp.bfloat16)
    value_down_part = jnp.dot(normed_layer_input, value_adapter_down.T, preferred_element_type=jnp.float32).astype(jnp.bfloat16)
    query_up_part = jnp.dot(query_flattened_rows, query_adapter_up.reshape(ADAPTER_RANK, -1).T, preferred_element_type=jnp.float32).astype(jnp.bfloat16)
    value_up_part = jnp.dot(value_flattened_rows, value_adapter_up.reshape(ADAPTER_RANK, -1).T, preferred_element_type=jnp.float32).astype(jnp.bfloat16)
    query_up_gradient = adapter_scale * jnp.dot(query_down_part.T, query_flattened_rows, preferred_element_type=jnp.float32).reshape(ADAPTER_RANK, 2, -1)
    value_up_gradient = adapter_scale * jnp.dot(value_down_part.T, value_flattened_rows, preferred_element_type=jnp.float32).reshape(ADAPTER_RANK, 2, -1)
    query_down_gradient = adapter_scale * jnp.dot(query_up_part.T, normed_layer_input, preferred_element_type=jnp.float32)
    value_down_gradient = adapter_scale * jnp.dot(value_up_part.T, normed_layer_input, preferred_element_type=jnp.float32)
    return (grad_query, grad_key, grad_value, query_down_gradient, query_up_gradient, value_down_gradient, value_up_gradient)
```

```python
import functools
import math

import jax
import jax.numpy as jnp
from jax import lax
from jax.experimental import pallas as pl
from jax.experimental.pallas import tpu as pltpu
from jax.sharding import PartitionSpec as P

MESH = pl.DeviceIdType.MESH
MASKED = -1e30
UNROLL = 4

QUERY_HEADS = 32
KEY_VALUE_HEADS = 4
HEAD_SIZE = 128
GROUP = 1024


adapter_scale = 2.0


def attention_kernel(
    ctx,
    devs,
    with_adapters,
    q_ref,
    do_ref,
    k_ref,
    v_ref,
    seg_ref,
    *refs,
):
    if with_adapters:
        x_ref, q_down_ref, v_down_ref, q_up_ref, v_up_ref = refs[:5]
        dq_ref, gk_ref, gv_ref, qd_out, qu_out, vd_out, vu_out = refs[5:12]
        refs = refs[12:]
    else:
        dq_ref, gk_ref, gv_ref = refs[:3]
        refs = refs[3:]
    kv_buf, part_send, part_recv, own_part, p_scr, w_scr, bias, g_send, g_recv, r_send, r_recv = (
        refs[:11]
    )
    if with_adapters:
        q_down, v_down, q_up, v_up, q_act = refs[11:16]
        q_bufs, v_bufs = refs[16:26], refs[26:]
    tok = k_ref.shape[1]
    kv_heads = k_ref.shape[2] // HEAD_SIZE
    repeat = q_ref.shape[2] // k_ref.shape[2]
    group_width = repeat * HEAD_SIZE
    mid = devs // 2
    scaling = HEAD_SIZE ** (-0.5)
    exponent = scaling * math.log2(math.e)
    me = lax.axis_index("ctx")
    p0 = lax.rem(me, devs)
    small = p0 // mid
    big = 1 - small
    ps = lax.rem(p0, mid)

    def ahead(d):
        return lax.rem(me + d, ctx)

    def behind(d):
        return lax.rem(me + ctx - d, ctx)

    for h in range(2):
        for g in range(kv_heads):
            lanes = slice(g * HEAD_SIZE, (g + 1) * HEAD_SIZE)
            kv_buf[h, 0, g, :, :HEAD_SIZE] = k_ref[h, :, lanes]
            kv_buf[h, 0, g, :, HEAD_SIZE:] = v_ref[h, :, lanes]

    barrier = pltpu.get_barrier_semaphore()
    for d in range(1, devs):
        pl.semaphore_signal(barrier, inc=1, device_id={"ctx": ahead(d)}, device_id_type=MESH)
        pl.semaphore_signal(barrier, inc=1, device_id={"ctx": behind(d)}, device_id_type=MESH)
    planes = ctx // devs
    plane = me // devs
    far = range(1, planes) if with_adapters else range(0)
    for j in far:
        pl.semaphore_signal(
            barrier,
            inc=1,
            device_id={"ctx": lax.rem(me + j * devs, ctx)},
            device_id_type=MESH,
        )
    pl.semaphore_wait(barrier, 2 * (devs - 1) + len(far))

    def gather_copy(h, d):
        return pltpu.make_async_remote_copy(
            src_ref=kv_buf.at[h, 0],
            dst_ref=kv_buf.at[h, d],
            send_sem=g_send.at[h, d],
            recv_sem=g_recv.at[h, d],
            device_id={"ctx": ahead(d)},
            device_id_type=MESH,
        )

    def return_copy(which, h, g, d):
        return pltpu.make_async_remote_copy(
            src_ref=part_send.at[which, h, g, d],
            dst_ref=part_recv.at[which, h, g, d],
            send_sem=r_send.at[which, h, g, d],
            recv_sem=r_recv.at[which, h, g, d],
            device_id={"ctx": behind(d)},
            device_id_type=MESH,
        )

    for d in range(1, mid):

        @pl.when(ps + d < mid)
        def _():
            gather_copy(small, d).start()

    for d in range(1, devs):

        @pl.when((ps + d >= mid) & (ps + d < devs))
        def _():
            gather_copy(small, d).start()

    for d in range(1, mid):

        @pl.when(ps + d < mid)
        def _():
            gather_copy(big, d).start()

    for d in range(1, mid):

        @pl.when(d > ps)
        def _():
            kv_buf[small, d] = jnp.zeros(kv_buf.shape[2:], kv_buf.dtype)

        @pl.when(d > ps)
        def _():
            kv_buf[big, mid + d] = jnp.zeros(kv_buf.shape[2:], kv_buf.dtype)

    own_ids = jnp.transpose(
        jnp.broadcast_to(seg_ref[pl.ds(me, 1), :].astype(jnp.float32), (tok, tok))
    )
    rows = lax.broadcasted_iota(jnp.int32, (tok, tok), 0)
    columns = lax.broadcasted_iota(jnp.int32, (tok, tok), 1)
    for d in range(devs):
        ids = seg_ref[pl.ds(behind(d), 1), :].astype(jnp.float32)
        block = jnp.where(own_ids == ids, 0.0, MASKED)
        if d == 0:
            block = jnp.where(columns <= rows, block, MASKED)
        bias[1, :, d * tok : (d + 1) * tok] = jnp.where(d <= ps + mid, block, MASKED)
        if d < mid:
            bias[0, :, d * tok : (d + 1) * tok] = jnp.where(d <= ps, block, MASKED)

    def within(j):
        return lax.rem(p0 + j, devs)

    def scatter_copy(bufs, j):
        part, landed, s_send, s_recv = bufs[0], bufs[1], bufs[4], bufs[5]
        return pltpu.make_async_remote_copy(
            src_ref=part.at[within(j)],
            dst_ref=landed.at[j],
            send_sem=s_send.at[j],
            recv_sem=s_recv.at[j],
            device_id={"ctx": plane * devs + within(j)},
            device_id_type=MESH,
        )

    def plane_copy(bufs, j):
        across, s_send, s_recv = bufs[2], bufs[6], bufs[7]
        return pltpu.make_async_remote_copy(
            src_ref=across.at[plane],
            dst_ref=across.at[plane],
            send_sem=s_send.at[j],
            recv_sem=s_recv.at[j],
            device_id={"ctx": lax.rem(me + j * devs, ctx)},
            device_id_type=MESH,
        )

    def spread_copy(bufs, j):
        whole, s_send, s_recv = bufs[3], bufs[8], bufs[9]
        return pltpu.make_async_remote_copy(
            src_ref=whole.at[p0],
            dst_ref=whole.at[p0],
            send_sem=s_send.at[j],
            recv_sem=s_recv.at[j],
            device_id={"ctx": plane * devs + within(j)},
            device_id_type=MESH,
        )

    def start_scatter(bufs):
        for j in range(1, devs):
            scatter_copy(bufs, j).start()

    def start_planes(bufs):
        total = bufs[0][p0].astype(jnp.float32)
        for j in range(1, devs):
            scatter_copy(bufs, j).wait_recv()
            total = total + bufs[1][j].astype(jnp.float32)
        bufs[2][plane] = total.astype(jnp.bfloat16)
        for j in range(1, planes):
            plane_copy(bufs, j).start()

    def start_spread(bufs):
        for j in range(1, planes):
            plane_copy(bufs, j).wait_recv()
        total = bufs[2][0].astype(jnp.float32)
        for j in range(1, planes):
            total = total + bufs[2][j].astype(jnp.float32)
        bufs[3][p0] = total.astype(jnp.bfloat16)
        for j in range(1, devs):
            spread_copy(bufs, j).start()

    def finish(bufs, down_out, up_out, up_pieces):
        for j in range(1, devs):
            spread_copy(bufs, j).wait_recv()
        width = down_out.shape[1] // devs
        up_width = 2 * up_out.shape[2] // up_pieces
        for p in range(devs):
            down_out[:, p * width : (p + 1) * width] = adapter_scale * bufs[3][
                p, :, :width
            ].astype(jnp.float32)
            if p < up_pieces:
                h, at = p // (up_pieces // 2), p % (up_pieces // 2)
                up_out[:, h, at * up_width : (at + 1) * up_width] = adapter_scale * bufs[3][
                    p, :, width:
                ].astype(jnp.float32)
        for j in range(1, devs):
            scatter_copy(bufs, j).wait_send()
            spread_copy(bufs, j).wait_send()
        for j in range(1, planes):
            plane_copy(bufs, j).wait_send()

    def project_down(bufs, act):
        width = x_ref.shape[1] // devs
        for p in range(devs):
            bufs[0][p, :, :width] = jnp.dot(
                act, x_ref[:, p * width : (p + 1) * width], preferred_element_type=jnp.float32
            ).astype(jnp.bfloat16)

    if with_adapters:
        for source, act in ((q_down_ref, q_down), (v_down_ref, v_down)):
            act[...] = lax.dot_general(
                source[...],
                x_ref[...],
                (((1,), (1,)), ((), ())),
                preferred_element_type=jnp.float32,
            ).astype(jnp.bfloat16)
        for h in range(2):
            q_up[h] = q_up_ref[:, h, :]
            v_up[h] = v_up_ref[:, h, :]
        q_act[...] = jnp.zeros_like(q_act)
        rank = q_act.shape[0]
        for p in range(2 * kv_heads, devs):
            v_bufs[0][p, :, x_ref.shape[1] // devs :] = jnp.zeros((rank, HEAD_SIZE), jnp.bfloat16)

    def stacked(ref, h, g):
        return jnp.concatenate(
            [
                ref[h, :, g * group_width + r * HEAD_SIZE : g * group_width + (r + 1) * HEAD_SIZE]
                for r in range(repeat)
            ],
            axis=0,
        )

    def send_parts(which, total, h, g, slots, limit):
        for d in range(slots):
            block = jnp.transpose(total[:, d * tok : (d + 1) * tok])
            if d == 0:
                own_part[which, h, g] = block
            else:
                part_send[which, h, g, d] = block.astype(jnp.bfloat16)
        for d in range(1, slots):

            @pl.when(d < limit)
            def _():
                return_copy(which, h, g, d).start()

    def probabilities(h, g, slots, limit):
        keys = slots * tok
        k = kv_buf[h, :slots, g, :, :HEAD_SIZE].reshape(keys, HEAD_SIZE)

        def one_head(r, inner):
            lanes = pl.ds(pl.multiple_of(g * group_width + r * HEAD_SIZE, HEAD_SIZE), HEAD_SIZE)
            at = pl.ds(pl.multiple_of(r * tok, tok), tok)
            s = lax.dot_general(
                q_ref[h, :, lanes],
                k,
                (((1,), (1,)), ((), ())),
                preferred_element_type=jnp.float32,
            )
            t = s * exponent + bias[int(slots == devs), :, :keys]
            e = jnp.exp2(t - jnp.max(t, axis=1, keepdims=True))
            w = e * (1.0 / jnp.sum(e, axis=1, keepdims=True))
            w_scr[g, at, :keys] = w
            p_scr[at, :keys] = w.astype(jnp.bfloat16)
            return inner

        lax.fori_loop(0, repeat, one_head, 0, unroll=8)
        dv = lax.dot_general(
            stacked(do_ref, h, g),
            p_scr[:, :keys],
            (((0,), (0,)), ((), ())),
            preferred_element_type=jnp.float32,
        )
        send_parts(1, dv, h, g, slots, limit)

    def score_gradients(h, g, slots, limit):
        keys = slots * tok
        k = kv_buf[h, :slots, g, :, :HEAD_SIZE].reshape(keys, HEAD_SIZE)
        v = kv_buf[h, :slots, g, :, HEAD_SIZE:].reshape(keys, HEAD_SIZE)

        def one_head(r, inner):
            lanes = pl.ds(pl.multiple_of(g * group_width + r * HEAD_SIZE, HEAD_SIZE), HEAD_SIZE)
            at = pl.ds(pl.multiple_of(r * tok, tok), tok)
            dp = lax.dot_general(
                do_ref[h, :, lanes],
                v,
                (((1,), (1,)), ((), ())),
                preferred_element_type=jnp.float32,
            )
            w = w_scr[g, at, :keys]
            low = w.astype(jnp.bfloat16).astype(jnp.float32)
            dot = jnp.sum(low * dp, axis=1, keepdims=True)
            ds = (w * (dp - dot)).astype(jnp.bfloat16)
            p_scr[at, :keys] = ds
            dq = jnp.dot(ds, k, preferred_element_type=jnp.float32) * scaling
            dq_ref[h, :, lanes] = dq.astype(jnp.bfloat16)
            return inner

        lax.fori_loop(0, repeat, one_head, 0, unroll=8)
        if with_adapters:
            lanes = slice(g * group_width, (g + 1) * group_width)
            dq_all = dq_ref[h, :, lanes]
            q_act[...] += lax.dot_general(
                q_up[h, :, lanes],
                dq_all,
                (((1,), (1,)), ((), ())),
                preferred_element_type=jnp.float32,
            )
            up = jnp.dot(q_down[...], dq_all, preferred_element_type=jnp.float32)
            up = up.astype(jnp.bfloat16)
            width = x_ref.shape[1] // devs
            each = group_width * 2 * kv_heads // devs
            pieces = group_width // each
            for i in range(pieces):
                q_bufs[0][(h * kv_heads + g) * pieces + i, :, width:] = up[
                    :, i * each : (i + 1) * each
                ]
        dk = lax.dot_general(
            stacked(q_ref, h, g),
            p_scr[:, :keys],
            (((0,), (0,)), ((), ())),
            preferred_element_type=jnp.float32,
        )
        send_parts(0, dk * scaling, h, g, slots, limit)

    def collect(which, out_ref):
        for d in range(1, devs):
            for g in range(kv_heads):

                @pl.when(ps + d < devs)
                def _():
                    return_copy(which, small, g, d).wait_recv()
                    own_part[which, small, g] += part_recv[which, small, g, d].astype(jnp.float32)

        for d in range(1, mid):
            for g in range(kv_heads):

                @pl.when(ps + d < mid)
                def _():
                    return_copy(which, big, g, d).wait_recv()
                    own_part[which, big, g] += part_recv[which, big, g, d].astype(jnp.float32)

        for h in range(2):
            for g in range(kv_heads):
                out_ref[h, :, g * HEAD_SIZE : (g + 1) * HEAD_SIZE] = own_part[which, h, g].astype(
                    jnp.bfloat16
                )

    def value_adapter():
        v_act = jnp.zeros(q_act.shape, jnp.float32)
        for h in range(2):
            v_act = v_act + lax.dot_general(
                v_up[h], gv_ref[h], (((1,), (1,)), ((), ())), preferred_element_type=jnp.float32
            )
            up = jnp.dot(v_down[...], gv_ref[h], preferred_element_type=jnp.float32)
            for g in range(kv_heads):
                v_bufs[0][h * kv_heads + g, :, x_ref.shape[1] // devs :] = up[
                    :, g * HEAD_SIZE : (g + 1) * HEAD_SIZE
                ].astype(jnp.bfloat16)
        project_down(v_bufs, v_act.astype(jnp.bfloat16))
        start_scatter(v_bufs)

    for d in range(1, mid):

        @pl.when(d <= ps)
        def _():
            gather_copy(small, d).wait_recv()

    for g in range(kv_heads):
        probabilities(small, g, mid, ps + 1)
    for g in range(kv_heads):
        score_gradients(small, g, mid, ps + 1)

    for d in range(1, devs):

        @pl.when(d <= ps + mid)
        def _():
            gather_copy(big, d).wait_recv()

    for g in range(kv_heads):
        probabilities(big, g, devs, ps + mid + 1)
    for g in range(kv_heads):
        score_gradients(big, g, devs, ps + mid + 1)
        if g == 0:
            collect(1, gv_ref)
            if with_adapters:
                value_adapter()

    if with_adapters:
        project_down(q_bufs, q_act[...].astype(jnp.bfloat16))
        start_scatter(q_bufs)
        start_planes(v_bufs)
        start_planes(q_bufs)
        start_spread(v_bufs)
        start_spread(q_bufs)
    collect(0, gk_ref)
    if with_adapters:
        finish(v_bufs, vd_out, vu_out, 2 * kv_heads)
        finish(q_bufs, qd_out, qu_out, devs)

    for d in range(1, devs):

        @pl.when(ps + d < devs)
        def _():
            gather_copy(small, d).wait_send()

        @pl.when(d <= ps + mid)
        def _():
            for which in range(2):
                for g in range(kv_heads):
                    return_copy(which, big, g, d).wait_send()

    for d in range(1, mid):

        @pl.when(ps + d < mid)
        def _():
            gather_copy(big, d).wait_send()

        @pl.when(d <= ps)
        def _():
            for which in range(2):
                for g in range(kv_heads):
                    return_copy(which, small, g, d).wait_send()


def attention_backward(q, do, k, v, seg, devs, adapters=None):
    tok, width = q.shape[1], q.shape[2]
    kv_heads = k.shape[2] // HEAD_SIZE
    repeat = width // k.shape[2]
    ctx = lax.axis_size("ctx")
    planes = ctx // devs
    bf16, f32 = jnp.bfloat16, jnp.float32
    vmem = pl.BlockSpec(memory_space=pltpu.VMEM)
    operands = (q, do, k, v, seg)
    results = [jax.ShapeDtypeStruct(a.shape, bf16) for a in (q, k, v)]
    scratch = [
        pltpu.VMEM((2, devs, kv_heads, tok, 2 * HEAD_SIZE), bf16),
        pltpu.VMEM((2, 2, kv_heads, devs, tok, HEAD_SIZE), bf16),
        pltpu.VMEM((2, 2, kv_heads, devs, tok, HEAD_SIZE), bf16),
        pltpu.VMEM((2, 2, kv_heads, tok, HEAD_SIZE), f32),
        pltpu.VMEM((repeat * tok, devs * tok), bf16),
        pltpu.VMEM((kv_heads, repeat * tok, devs * tok), f32),
        pltpu.VMEM((2, tok, devs * tok), f32),
        pltpu.SemaphoreType.DMA((2, devs)),
        pltpu.SemaphoreType.DMA((2, devs)),
        pltpu.SemaphoreType.DMA((2, 2, kv_heads, devs)),
        pltpu.SemaphoreType.DMA((2, 2, kv_heads, devs)),
    ]
    if adapters is not None:
        operands = operands + adapters
        x, q_down, v_down, q_up, v_up = adapters
        rank = q_down.shape[0]
        results += [jax.ShapeDtypeStruct(a.shape, f32) for a in (q_down, q_up, v_down, v_up)]
        scratch += [
            pltpu.VMEM((rank, tok), bf16),
            pltpu.VMEM((rank, tok), bf16),
            pltpu.VMEM((2, rank, q.shape[2]), bf16),
            pltpu.VMEM((2, rank, k.shape[2]), bf16),
            pltpu.VMEM((rank, tok), f32),
        ]
        for columns in ((x.shape[1] + 2 * width) // devs, x.shape[1] // devs + HEAD_SIZE):
            scratch += [
                pltpu.VMEM((n, rank, columns), bf16) for n in (devs, devs, planes, devs)
            ]
            scratch += [
                pltpu.SemaphoreType.DMA((n,)) for n in (devs, devs, planes, planes, devs, devs)
            ]
    return pl.pallas_call(
        functools.partial(attention_kernel, ctx, devs, adapters is not None),
        out_shape=tuple(results),
        in_specs=[vmem] * len(operands),
        out_specs=(vmem,) * len(results),
        scratch_shapes=scratch,
        compiler_params=pltpu.CompilerParams(
            collective_id=0, has_side_effects=True, vmem_limit_bytes=52 * 1024 * 1024
        ),
        name="attention_backward",
    )(*operands)


def paired_kernel(
    chips,
    span,
    q_ref,
    do_ref,
    k_ref,
    v_ref,
    seg_ref,
    x_ref,
    q_down_ref,
    v_down_ref,
    q_up_ref,
    v_up_ref,
    dq_ref,
    gk_ref,
    gv_ref,
    qd_out,
    qu_out,
    vd_out,
    vu_out,
    qb,
    dob,
    kb,
    vb,
    xb,
    dqb,
    p_small,
    p_big,
    bias,
    part_send,
    part_recv,
    acc,
    sib_part,
    down_mine,
    down_theirs,
    act_mine,
    act_theirs,
    mixed_mine,
    mixed_theirs,
    acts,
    q_parts,
    q_land,
    q_sums,
    q_other,
    v_parts,
    v_land,
    v_sums,
    v_other,
    local_sem,
    swap_send,
    swap_recv,
    g_send,
    g_recv,
    r_send,
    r_recv,
    a_send,
    a_recv,
):
    bf16, f32 = jnp.bfloat16, jnp.float32
    tok = k_ref.shape[1]
    pair = 2 * tok
    width = qb.shape[2]
    heads = width // HEAD_SIZE
    columns = xb.shape[1]
    each = columns // chips
    up_each = 2 * width // chips
    rank = acts.shape[1]
    mid = span // 2
    scaling = HEAD_SIZE ** (-0.5)
    exponent = scaling * math.log2(math.e)
    me = lax.axis_index("ctx")
    chip = me // 2
    core = lax.rem(me, 2)
    other = 1 - core
    place = lax.rem(chip, span)
    small = place // mid
    big = 1 - small
    ps = lax.rem(place, mid)

    def ahead(d):
        return lax.rem(chip + d, chips)

    def behind(d):
        return lax.rem(chip + chips - d, chips)

    def device(chip_at, core_at):
        return {"ctx": 2 * chip_at + core_at}

    sibling = device(chip, other)

    def rows(at):
        return pl.ds(pl.multiple_of(at * tok, tok), tok)

    def half_columns(at, size):
        return pl.ds(pl.multiple_of(at * size, size), size)

    barrier = pltpu.get_barrier_semaphore()
    pl.semaphore_signal(barrier, inc=1, device_id=sibling, device_id_type=MESH)
    for d in range(1, chips):
        pl.semaphore_signal(
            barrier, inc=1, device_id=device(ahead(d), core), device_id_type=MESH
        )
    for d in range(1, span):
        pl.semaphore_signal(
            barrier, inc=1, device_id=device(ahead(d), other), device_id_type=MESH
        )
        pl.semaphore_signal(
            barrier, inc=1, device_id=device(behind(d), other), device_id_type=MESH
        )

    own = []
    for h in range(2):
        for i, (src, dst) in enumerate(((q_ref, qb), (do_ref, dob))):
            own.append(
                pltpu.make_async_copy(
                    src.at[h, :, half_columns(core, width)],
                    dst.at[h, rows(core)],
                    local_sem.at[2 * h + i],
                )
            )
    own.append(
        pltpu.make_async_copy(
            x_ref.at[:, half_columns(core, columns)], xb.at[rows(core)], local_sem.at[4]
        )
    )
    for copy in own:
        copy.start()

    def swap_columns(row):
        return pltpu.make_async_remote_copy(
            src_ref=x_ref.at[:, half_columns(other, columns)],
            dst_ref=xb.at[rows(row)],
            send_sem=swap_send.at[4],
            recv_sem=swap_recv.at[4],
            device_id=sibling,
            device_id_type=MESH,
        )

    def swap_half(h, i):
        src, dst = ((q_ref, qb), (do_ref, dob))[i]
        return pltpu.make_async_remote_copy(
            src_ref=src.at[h, :, half_columns(other, width)],
            dst_ref=dst.at[h, rows(core)],
            send_sem=swap_send.at[2 * h + i],
            recv_sem=swap_recv.at[2 * h + i],
            device_id=sibling,
            device_id_type=MESH,
        )

    def gather_copy(which, h, d, to, row):
        src = (k_ref, v_ref)[which].at[h, :, half_columns(to, HEAD_SIZE)]
        return pltpu.make_async_remote_copy(
            src_ref=src,
            dst_ref=(kb, vb)[which].at[h, d, rows(row)],
            send_sem=g_send.at[which, h, d, to],
            recv_sem=g_recv.at[which, h, d, row],
            device_id=device(ahead(d), to),
            device_id_type=MESH,
        )

    def gather_start(which, h, d):
        for to in range(2):
            gather_copy(which, h, d, to, core).start()

    def gather_wait(which, h, d):
        for row in range(2):
            gather_copy(which, h, d, row, row).wait_recv()

    def gather_sent(which, h, d):
        for to in range(2):
            gather_copy(which, h, d, to, core).wait_send()

    @pl.when(ps == 0)
    def _():
        for buf in (kb, vb):
            buf[small, 1] = jnp.zeros(buf.shape[2:], bf16)
            buf[big, span - 1] = jnp.zeros(buf.shape[2:], bf16)

    for h in range(2):
        for src, dst in ((k_ref, kb), (v_ref, vb)):
            dst[h, 0, rows(core)] = src[h, :, half_columns(core, HEAD_SIZE)]

    def chip_ids(at):
        first = seg_ref[pl.ds(2 * at, 1), :]
        second = seg_ref[pl.ds(2 * at + 1, 1), :]
        return jnp.concatenate([first, second], axis=1).astype(f32)

    own_ids = jnp.transpose(jnp.broadcast_to(chip_ids(chip), (pair, pair)))
    row = lax.broadcasted_iota(jnp.int32, (pair, pair), 0)
    column = lax.broadcasted_iota(jnp.int32, (pair, pair), 1)
    for d in range(span):
        block = jnp.where(own_ids == chip_ids(behind(d)), 0.0, MASKED)
        if d == 0:
            block = jnp.where(column <= row, block, MASKED)
        bias[1, :, d * pair : (d + 1) * pair] = jnp.where(d <= ps + mid, block, MASKED)
        if d < mid:
            bias[0, :, d * pair : (d + 1) * pair] = jnp.where(d <= ps, block, MASKED)

    pl.semaphore_wait(barrier, chips + 2 * (span - 1))

    for which in range(2):
        if which == 0:
            gather_copy(0, small, 0, other, core).start()
        for d in range(1, mid):

            @pl.when(ps + d < mid)
            def _():
                gather_start(which, small, d)

        if which == 0:
            swap_half(small, 0).start()
        for d in range(1, span):

            @pl.when((ps + d >= mid) & (ps + d < span))
            def _():
                gather_start(which, small, d)

        for d in range(1, mid):

            @pl.when(ps + d < mid)
            def _():
                gather_start(which, big, d)

        if which == 0:
            swap_half(small, 1).start()
            gather_copy(0, big, 0, other, core).start()
            for i in range(2):
                swap_half(big, i).start()
            for h in range(2):
                gather_copy(1, h, 0, other, core).start()
            swap_columns(core).start()

    def exchange(src, dst, i):
        return pltpu.make_async_remote_copy(
            src_ref=src,
            dst_ref=dst,
            send_sem=swap_send.at[i],
            recv_sem=swap_recv.at[i],
            device_id=sibling,
            device_id_type=MESH,
        )

    down_swap = exchange(down_mine, down_theirs, 5)
    act_swap = exchange(act_mine, act_theirs, 6)
    mixed_swap = exchange(mixed_mine, mixed_theirs, 7)

    def part_swap(which, h):
        return pltpu.make_async_remote_copy(
            src_ref=sib_part.at[which, h],
            dst_ref=acc.at[which, h, core],
            send_sem=swap_send.at[8 + 2 * which + h],
            recv_sem=swap_recv.at[8 + 2 * which + h],
            device_id=sibling,
            device_id_type=MESH,
        )

    def part_wait(which, h):
        return pltpu.make_async_remote_copy(
            src_ref=sib_part.at[which, h],
            dst_ref=acc.at[which, h, other],
            send_sem=swap_send.at[8 + 2 * which + h],
            recv_sem=swap_recv.at[8 + 2 * which + h],
            device_id=sibling,
            device_id_type=MESH,
        )

    def dq_swap(h):
        return pltpu.make_async_remote_copy(
            src_ref=dqb.at[h, rows(other)],
            dst_ref=dq_ref.at[h, :, half_columns(core, width)],
            send_sem=swap_send.at[12 + h],
            recv_sem=swap_recv.at[12 + h],
            device_id=sibling,
            device_id_type=MESH,
        )

    def dq_own(h):
        return pltpu.make_async_copy(
            dqb.at[h, rows(core)], dq_ref.at[h, :, half_columns(core, width)], local_sem.at[5 + h]
        )

    def dq_wait(h):
        return pltpu.make_async_remote_copy(
            src_ref=dqb.at[h, rows(other)],
            dst_ref=dq_ref.at[h, :, half_columns(other, width)],
            send_sem=swap_send.at[12 + h],
            recv_sem=swap_recv.at[12 + h],
            device_id=sibling,
            device_id_type=MESH,
        )

    def scatter_copy(s, parts, land, j):
        return pltpu.make_async_remote_copy(
            src_ref=parts.at[ahead(j)],
            dst_ref=land.at[j],
            send_sem=a_send.at[s, j],
            recv_sem=a_recv.at[s, j],
            device_id=device(ahead(j), core),
            device_id_type=MESH,
        )

    def spread_copy(s, sums, j, source):
        return pltpu.make_async_remote_copy(
            src_ref=sums.at[source],
            dst_ref=sums.at[source],
            send_sem=a_send.at[2 + s, j],
            recv_sem=a_recv.at[2 + s, j],
            device_id=device(ahead(j), core),
            device_id_type=MESH,
        )

    q_set = (0, q_parts, q_land, q_sums, q_other)
    v_set = (1, v_parts, v_land, v_sums, v_other)

    def start_scatter(bufs):
        for j in range(1, chips):
            scatter_copy(bufs[0], bufs[1], bufs[2], j).start()

    def start_spread(bufs):
        total = bufs[1][chip].astype(f32)
        for j in range(1, chips):
            scatter_copy(bufs[0], bufs[1], bufs[2], j).wait_recv()
            total = total + bufs[2][j].astype(f32)
        bufs[3][chip] = total.astype(bf16)
        for j in range(1, chips):
            spread_copy(bufs[0], bufs[3], j, chip).start()

    def hand_copy(bufs):
        return exchange(bufs[3], bufs[4], 14 + bufs[0])

    def start_hand(bufs):
        for j in range(1, chips):
            spread_copy(bufs[0], bufs[3], j, behind(j)).wait_recv()
        hand_copy(bufs).start()

    def finish(bufs, down_out, up_out, up_width, up_pieces):
        def write(source, at):
            for i in range(chips):
                lanes = pl.ds(pl.multiple_of(at * columns + i * each, each), each)
                down_out[:, lanes] = adapter_scale * source[i, :, :each].astype(f32)
                if i < up_pieces:
                    h, step = i // (up_pieces // 2), i % (up_pieces // 2)
                    size = up_width // (up_pieces // 2)
                    lanes = pl.ds(pl.multiple_of(at * up_width + step * size, size), size)
                    up_out[:, h, lanes] = adapter_scale * source[i, :, each:].astype(f32)

        write(bufs[3], core)
        hand_copy(bufs).wait_recv()
        write(bufs[4], other)
        for j in range(1, chips):
            scatter_copy(bufs[0], bufs[1], bufs[2], j).wait_send()
            spread_copy(bufs[0], bufs[3], j, chip).wait_send()
        hand_copy(bufs).wait_send()

    def project_down(parts, act):
        for i in range(chips):
            parts[i, :, :each] = jnp.dot(
                act, xb[:, i * each : (i + 1) * each], preferred_element_type=f32
            ).astype(bf16)

    def return_copy(which, h, d, to, head):
        return pltpu.make_async_remote_copy(
            src_ref=part_send.at[which, h, d, rows(to)],
            dst_ref=part_recv.at[which, h, d, head],
            send_sem=r_send.at[which, h, d, to],
            recv_sem=r_recv.at[which, h, d, head],
            device_id=device(behind(d), to),
            device_id_type=MESH,
        )

    def send_parts(which, total, h, slots, limit):
        for d in reversed(range(slots)):
            block = jnp.transpose(total[:, d * pair : (d + 1) * pair])
            if d == 0:
                acc[which, h, core] = jnp.where(core == 0, block[:tok], block[tok:])
                sib_part[which, h] = jnp.where(core == 0, block[tok:], block[:tok])
                part_swap(which, h).start()
            else:
                part_send[which, h, d] = block.astype(bf16)

                @pl.when(d < limit)
                def _():
                    for to in range(2):
                        return_copy(which, h, d, to, core).start()

    def stacked(ref, h):
        return jnp.concatenate(
            [ref[h, :, j * HEAD_SIZE : (j + 1) * HEAD_SIZE] for j in range(heads)], axis=0
        )

    def head_lanes(j):
        return pl.ds(pl.multiple_of(j * HEAD_SIZE, HEAD_SIZE), HEAD_SIZE)

    def head_rows(j):
        return pl.ds(pl.multiple_of(j * pair, pair), pair)

    def probabilities(h, p_ref, slots, limit):
        keys = slots * pair
        k = kb[h, :slots].reshape(keys, HEAD_SIZE)

        def one_head(j, inner):
            s = lax.dot_general(
                qb[h, :, head_lanes(j)], k, (((1,), (1,)), ((), ())), preferred_element_type=f32
            )
            t = s * exponent + bias[int(slots == span), :, :keys]
            e = jnp.exp2(t - jnp.max(t, axis=1, keepdims=True))
            w = e * (1.0 / jnp.sum(e, axis=1, keepdims=True))
            p_ref[head_rows(j)] = w.astype(bf16)
            return inner

        lax.fori_loop(0, heads, one_head, 0, unroll=UNROLL)

    def value_part(h, p_ref, slots, limit):
        dv = lax.dot_general(
            stacked(dob, h), p_ref[...], (((0,), (0,)), ((), ())), preferred_element_type=f32
        )
        send_parts(1, dv, h, slots, limit)

    def score_gradients(h, p_ref, slots):
        keys = slots * pair
        k = kb[h, :slots].reshape(keys, HEAD_SIZE)
        v = vb[h, :slots].reshape(keys, HEAD_SIZE)

        def one_head(j, inner):
            dp = lax.dot_general(
                dob[h, :, head_lanes(j)], v, (((1,), (1,)), ((), ())), preferred_element_type=f32
            )
            w = p_ref[head_rows(j)].astype(f32)
            dot = jnp.sum(w * dp, axis=1, keepdims=True)
            ds = (w * (dp - dot)).astype(bf16)
            p_ref[head_rows(j)] = ds
            dq = jnp.dot(ds, k, preferred_element_type=f32) * scaling
            dqb[h, :, head_lanes(j)] = dq.astype(bf16)
            return inner

        lax.fori_loop(0, heads, one_head, 0, unroll=UNROLL)
        dq_own(h).start()
        dq_swap(h).start()

    def query_adapter(h):
        dq = dqb[h]
        up_rows = q_up_ref[:, h, half_columns(core, width)]
        up = jnp.dot(acts[0], dq, preferred_element_type=f32).astype(bf16)
        return lax.dot_general(
            up_rows, dq, (((1,), (1,)), ((), ())), preferred_element_type=f32
        ), up

    def key_part(h, p_ref, slots, limit):
        dk = lax.dot_general(
            stacked(qb, h), p_ref[...], (((0,), (0,)), ((), ())), preferred_element_type=f32
        )
        send_parts(0, dk * scaling, h, slots, limit)

    def collect(which, out_ref):
        for h in range(2):
            part_wait(which, h).wait_recv()
        for d in range(1, span):

            @pl.when(ps + d < span)
            def _():
                for head in range(2):
                    return_copy(which, small, d, head, head).wait_recv()
                    acc[which, small, head] += part_recv[which, small, d, head].astype(f32)

        for d in range(1, mid):

            @pl.when(ps + d < mid)
            def _():
                for head in range(2):
                    return_copy(which, big, d, head, head).wait_recv()
                    acc[which, big, head] += part_recv[which, big, d, head].astype(f32)

        for h in range(2):
            for head in range(2):
                out_ref[h, :, head * HEAD_SIZE : (head + 1) * HEAD_SIZE] = acc[
                    which, h, head
                ].astype(bf16)

    def wait_swap(h, i):
        src, dst = ((q_ref, qb), (do_ref, dob))[i]
        pltpu.make_async_remote_copy(
            src_ref=src.at[h, :, half_columns(other, width)],
            dst_ref=dst.at[h, rows(other)],
            send_sem=swap_send.at[2 * h + i],
            recv_sem=swap_recv.at[2 * h + i],
            device_id=sibling,
            device_id_type=MESH,
        ).wait_recv()

    for i in (0, 2):
        own[i].wait()
    wait_swap(small, 0)
    gather_copy(0, small, 0, other, other).wait_recv()
    for d in range(1, mid):

        @pl.when(d <= ps)
        def _():
            gather_wait(0, small, d)

    probabilities(small, p_small, mid, ps + 1)
    for i in (1, 3):
        own[i].wait()
    wait_swap(small, 1)
    value_part(small, p_small, mid, ps + 1)

    own[4].wait()
    swap_columns(other).wait_recv()
    for i, source in enumerate((q_down_ref, v_down_ref)):
        down_mine[i] = lax.dot_general(
            source[:, half_columns(core, columns)],
            xb[...],
            (((1,), (1,)), ((), ())),
            preferred_element_type=f32,
        )
    down_swap.start()

    wait_swap(big, 0)
    gather_copy(0, big, 0, other, other).wait_recv()
    for d in range(1, span):

        @pl.when(d <= ps + mid)
        def _():
            gather_wait(0, big, d)

    probabilities(big, p_big, span, ps + mid + 1)
    wait_swap(big, 1)
    value_part(big, p_big, span, ps + mid + 1)

    down_swap.wait()
    for i in range(2):
        acts[i] = (down_mine[i] + down_theirs[i]).astype(bf16)

    for h in (small, big):
        gather_copy(1, h, 0, other, other).wait_recv()
    for d in range(1, mid):

        @pl.when(d <= ps)
        def _():
            gather_wait(1, small, d)

    for d in range(1, span):

        @pl.when(d <= ps + mid)
        def _():
            gather_wait(1, big, d)

    score_gradients(small, p_small, mid)

    collect(1, gv_ref)
    v_act = jnp.zeros((rank, tok), f32)
    own_lanes = half_columns(core, tok)
    for h in range(2):
        v_act = v_act + lax.dot_general(
            v_up_ref[:, h, :], gv_ref[h], (((1,), (1,)), ((), ())), preferred_element_type=f32
        )
        up = jnp.dot(acts[1, :, own_lanes], gv_ref[h], preferred_element_type=f32)
        first, second = up[:, :HEAD_SIZE], up[:, HEAD_SIZE:]
        mixed_mine[1 + h] = jnp.where(core == 0, second, first)
        mixed_mine[3 + h] = jnp.where(core == 0, first, second)
    mixed_mine[0] = v_act
    mixed_swap.start()

    score_gradients(big, p_big, span)

    mixed_swap.wait()
    acts[2, :, own_lanes] = mixed_mine[0].astype(bf16)
    acts[2, :, half_columns(other, tok)] = mixed_theirs[0].astype(bf16)
    for i in range(chips):
        if i < 2:
            v_parts[i, :, each:] = (mixed_mine[3 + i] + mixed_theirs[1 + i]).astype(bf16)
        else:
            v_parts[i, :, each:] = jnp.zeros((rank, HEAD_SIZE), bf16)
    project_down(v_parts, acts[2])
    start_scatter(v_set)

    act = jnp.zeros((rank, pair), f32)
    for h in range(2):
        more, up = query_adapter(h)
        act = act + more
        for i in range(chips // 2):
            q_parts[h * (chips // 2) + i, :, each:] = up[:, i * up_each : (i + 1) * up_each]
    act_mine[...] = act
    act_swap.start()
    act_swap.wait()
    project_down(q_parts, (act_mine[...] + act_theirs[...]).astype(bf16))
    start_scatter(q_set)

    key_part(big, p_big, span, ps + mid + 1)
    key_part(small, p_small, mid, ps + 1)

    start_spread(v_set)
    start_spread(q_set)
    collect(0, gk_ref)
    start_hand(v_set)
    start_hand(q_set)
    finish(v_set, vd_out, vu_out, HEAD_SIZE, 2)
    finish(q_set, qd_out, qu_out, width, chips)

    for h in range(2):
        dq_own(h).wait()
        dq_swap(h).wait_send()
        dq_wait(h).wait_recv()
        for i in range(2):
            swap_half(h, i).wait_send()
            part_swap(i, h).wait_send()
            gather_copy(i, h, 0, other, core).wait_send()
    swap_columns(core).wait_send()
    for which in range(2):
        for d in range(1, span):

            @pl.when(ps + d < span)
            def _():
                gather_sent(which, small, d)

            @pl.when(d <= ps + mid)
            def _():
                for to in range(2):
                    return_copy(which, big, d, to, core).wait_send()

        for d in range(1, mid):

            @pl.when(ps + d < mid)
            def _():
                gather_sent(which, big, d)

            @pl.when(d <= ps)
            def _():
                for to in range(2):
                    return_copy(which, small, d, to, core).wait_send()


def paired_backward(q, do, k, v, seg, x, q_down, v_down, q_up, v_up, span):
    tok, width = q.shape[1], q.shape[2] // 2
    pair = 2 * tok
    heads = width // HEAD_SIZE
    chips = lax.axis_size("ctx") // 2
    rank = q_down.shape[0]
    columns = x.shape[1] // 2
    bf16, f32 = jnp.bfloat16, jnp.float32
    vmem = pl.BlockSpec(memory_space=pltpu.VMEM)
    anywhere = pl.BlockSpec(memory_space=pl.ANY)
    q_piece = columns // chips + 2 * width // chips
    v_piece = columns // chips + HEAD_SIZE
    scratch = [
        pltpu.VMEM((2, pair, width), bf16),
        pltpu.VMEM((2, pair, width), bf16),
        pltpu.VMEM((2, span, pair, HEAD_SIZE), bf16),
        pltpu.VMEM((2, span, pair, HEAD_SIZE), bf16),
        pltpu.VMEM((pair, columns), bf16),
        pltpu.VMEM((2, pair, width), bf16),
        pltpu.VMEM((heads * pair, span // 2 * pair), bf16),
        pltpu.VMEM((heads * pair, span * pair), bf16),
        pltpu.VMEM((2, pair, span * pair), f32),
        pltpu.VMEM((2, 2, span, pair, HEAD_SIZE), bf16),
        pltpu.VMEM((2, 2, span, 2, tok, HEAD_SIZE), bf16),
        pltpu.VMEM((2, 2, 2, tok, HEAD_SIZE), f32),
        pltpu.VMEM((2, 2, tok, HEAD_SIZE), f32),
        pltpu.VMEM((2, rank, pair), f32),
        pltpu.VMEM((2, rank, pair), f32),
        pltpu.VMEM((rank, pair), f32),
        pltpu.VMEM((rank, pair), f32),
        pltpu.VMEM((5, rank, HEAD_SIZE), f32),
        pltpu.VMEM((5, rank, HEAD_SIZE), f32),
        pltpu.VMEM((3, rank, pair), bf16),
    ]
    for piece in (q_piece, v_piece):
        scratch += [pltpu.VMEM((chips, rank, piece), bf16) for _ in range(4)]
    scratch += [
        pltpu.SemaphoreType.DMA((7,)),
        pltpu.SemaphoreType.DMA((16,)),
        pltpu.SemaphoreType.DMA((16,)),
    ]
    scratch += [pltpu.SemaphoreType.DMA((2, 2, span, 2)) for _ in range(4)]
    scratch += [pltpu.SemaphoreType.DMA((4, chips)) for _ in range(2)]
    return pl.pallas_call(
        functools.partial(paired_kernel, chips, span),
        out_shape=tuple(
            [jax.ShapeDtypeStruct(a.shape, bf16) for a in (q, k, v)]
            + [jax.ShapeDtypeStruct(a.shape, f32) for a in (q_down, q_up, v_down, v_up)]
        ),
        in_specs=[anywhere, anywhere, vmem, vmem, vmem, anywhere, vmem, vmem, vmem, vmem],
        out_specs=(anywhere,) + (vmem,) * 6,
        scratch_shapes=scratch,
        compiler_params=pltpu.CompilerParams(
            collective_id=1, has_side_effects=True, vmem_limit_bytes=48 * 1024 * 1024
        ),
        name="paired_backward",
    )(q, do, k, v, seg, x, q_down, v_down, q_up, v_up)


def on_device(
    projected_queries,
    projected_keys,
    projected_values,
    output_gradient,
    normed_layer_input,
    segment,
    query_adapter_down,
    query_adapter_up,
    value_adapter_down,
    value_adapter_up,
):
    tok_rows = projected_queries.shape[0]
    query_width = projected_queries.shape[2]
    key_width = projected_keys.shape[2]
    key_value_heads = key_width // HEAD_SIZE
    group_devs = GROUP // tok_rows
    ctx = lax.axis_size("ctx")
    paired = (
        lax.axis_size("fsdp") == 1
        and group_devs % 4 == 0
        and key_value_heads == 2
        and tok_rows == HEAD_SIZE
        and query_width % (ctx * HEAD_SIZE // 2) == 0
        and normed_layer_input.shape[1] % (ctx * HEAD_SIZE) == 0
    )
    operands = (
        projected_queries.transpose(1, 0, 2),
        output_gradient.transpose(1, 0, 2),
        projected_keys.transpose(1, 0, 2),
        projected_values.transpose(1, 0, 2),
        segment.reshape(-1, tok_rows),
    )
    if paired:
        query_grad, key_grad, value_grad, *totals = paired_backward(
            *operands,
            normed_layer_input,
            query_adapter_down,
            value_adapter_down,
            query_adapter_up,
            value_adapter_up,
            group_devs // 2,
        )
    else:
        query_grad, key_grad, value_grad = attention_backward(*operands, group_devs)
    grad_query = query_grad.transpose(1, 0, 2)
    grad_key = key_grad.transpose(1, 0, 2)
    grad_value = value_grad.transpose(1, 0, 2)
    if paired:
        return (grad_query, grad_key, grad_value, *totals)
    adapter_input = lax.psum(
        (
            jnp.dot(normed_layer_input, query_adapter_down.T, preferred_element_type=jnp.float32),
            jnp.dot(normed_layer_input, value_adapter_down.T, preferred_element_type=jnp.float32),
        ),
        "fsdp",
    )
    query_down_part = adapter_input[0].astype(jnp.bfloat16)
    value_down_part = adapter_input[1].astype(jnp.bfloat16)
    query_flattened_rows = grad_query.reshape(tok_rows, -1)
    value_flattened_rows = grad_value.reshape(tok_rows, -1)
    adapter_rank_rows = query_adapter_up.shape[0]
    adapter_output = lax.psum(
        (
            jnp.dot(
                query_flattened_rows,
                query_adapter_up.reshape(adapter_rank_rows, -1).T,
                preferred_element_type=jnp.float32,
            ),
            jnp.dot(
                value_flattened_rows,
                value_adapter_up.reshape(adapter_rank_rows, -1).T,
                preferred_element_type=jnp.float32,
            ),
        ),
        "fsdp",
    )
    query_up_part = adapter_output[0].astype(jnp.bfloat16)
    value_up_part = adapter_output[1].astype(jnp.bfloat16)
    local_down_query = jnp.dot(
        query_up_part.T, normed_layer_input, preferred_element_type=jnp.float32
    )
    local_up_query = jnp.dot(
        query_down_part.T, query_flattened_rows, preferred_element_type=jnp.float32
    ).reshape(adapter_rank_rows, 2, -1)
    local_down_value = jnp.dot(
        value_up_part.T, normed_layer_input, preferred_element_type=jnp.float32
    )
    local_up_value = jnp.dot(
        value_down_part.T, value_flattened_rows, preferred_element_type=jnp.float32
    ).reshape(adapter_rank_rows, 2, -1)
    gradient_totals = lax.psum(
        (local_down_query, local_up_query, local_down_value, local_up_value), "ctx"
    )
    return (
        grad_query,
        grad_key,
        grad_value,
        adapter_scale * gradient_totals[0],
        adapter_scale * gradient_totals[1],
        adapter_scale * gradient_totals[2],
        adapter_scale * gradient_totals[3],
    )


def solution(mesh):
    in_specs = (
        P(("rep", "ctx"), None, "fsdp"),
        P(("rep", "ctx"), None, "fsdp"),
        P(("rep", "ctx"), None, "fsdp"),
        P(("rep", "ctx"), None, "fsdp"),
        P(("rep", "ctx"), "fsdp"),
        P("rep"),
        P(None, "fsdp"),
        P(None, None, "fsdp"),
        P(None, "fsdp"),
        P(None, None, "fsdp"),
    )
    out_specs = (
        P(("rep", "ctx"), None, "fsdp"),
        P(("rep", "ctx"), None, "fsdp"),
        P(("rep", "ctx"), None, "fsdp"),
        P("rep", "fsdp"),
        P("rep", None, "fsdp"),
        P("rep", "fsdp"),
        P("rep", None, "fsdp"),
    )
    return jax.shard_map(
        on_device, mesh=mesh, in_specs=in_specs, out_specs=out_specs, check_vma=False
    )
```

```python
import functools
import math

import jax
import jax.numpy as jnp
from jax import lax
from jax.experimental import pallas as pl
from jax.experimental.pallas import tpu as pltpu
from jax.sharding import PartitionSpec as P

MESH = pl.DeviceIdType.MESH
MASKED = -1e30
UNROLL = 4

QUERY_HEADS = 32
KEY_VALUE_HEADS = 4
HEAD_SIZE = 128
GROUP = 1024


adapter_scale = 2.0


def attention_kernel(
    ctx,
    devs,
    with_adapters,
    q_ref,
    do_ref,
    k_ref,
    v_ref,
    seg_ref,
    *refs,
):
    if with_adapters:
        x_ref, q_down_ref, v_down_ref, q_up_ref, v_up_ref = refs[:5]
        dq_ref, gk_ref, gv_ref, qd_out, qu_out, vd_out, vu_out = refs[5:12]
        refs = refs[12:]
    else:
        dq_ref, gk_ref, gv_ref = refs[:3]
        refs = refs[3:]
    kv_buf, part_send, part_recv, own_part, p_scr, w_scr, bias, g_send, g_recv, r_send, r_recv = (
        refs[:11]
    )
    if with_adapters:
        q_down, v_down, q_up, v_up, q_act = refs[11:16]
        q_bufs, v_bufs = refs[16:26], refs[26:]
    tok = k_ref.shape[1]
    kv_heads = k_ref.shape[2] // HEAD_SIZE
    repeat = q_ref.shape[2] // k_ref.shape[2]
    group_width = repeat * HEAD_SIZE
    mid = devs // 2
    scaling = HEAD_SIZE ** (-0.5)
    exponent = scaling * math.log2(math.e)
    me = lax.axis_index("ctx")
    p0 = lax.rem(me, devs)
    small = p0 // mid
    big = 1 - small
    ps = lax.rem(p0, mid)

    def ahead(d):
        return lax.rem(me + d, ctx)

    def behind(d):
        return lax.rem(me + ctx - d, ctx)

    for h in range(2):
        for g in range(kv_heads):
            lanes = slice(g * HEAD_SIZE, (g + 1) * HEAD_SIZE)
            kv_buf[h, 0, g, :, :HEAD_SIZE] = k_ref[h, :, lanes]
            kv_buf[h, 0, g, :, HEAD_SIZE:] = v_ref[h, :, lanes]

    barrier = pltpu.get_barrier_semaphore()
    for d in range(1, devs):
        pl.semaphore_signal(barrier, inc=1, device_id={"ctx": ahead(d)}, device_id_type=MESH)
        pl.semaphore_signal(barrier, inc=1, device_id={"ctx": behind(d)}, device_id_type=MESH)
    planes = ctx // devs
    plane = me // devs
    far = range(1, planes) if with_adapters else range(0)
    for j in far:
        pl.semaphore_signal(
            barrier,
            inc=1,
            device_id={"ctx": lax.rem(me + j * devs, ctx)},
            device_id_type=MESH,
        )
    pl.semaphore_wait(barrier, 2 * (devs - 1) + len(far))

    def gather_copy(h, d):
        return pltpu.make_async_remote_copy(
            src_ref=kv_buf.at[h, 0],
            dst_ref=kv_buf.at[h, d],
            send_sem=g_send.at[h, d],
            recv_sem=g_recv.at[h, d],
            device_id={"ctx": ahead(d)},
            device_id_type=MESH,
        )

    def return_copy(which, h, g, d):
        return pltpu.make_async_remote_copy(
            src_ref=part_send.at[which, h, g, d],
            dst_ref=part_recv.at[which, h, g, d],
            send_sem=r_send.at[which, h, g, d],
            recv_sem=r_recv.at[which, h, g, d],
            device_id={"ctx": behind(d)},
            device_id_type=MESH,
        )

    for d in range(1, mid):

        @pl.when(ps + d < mid)
        def _():
            gather_copy(small, d).start()

    for d in range(1, devs):

        @pl.when((ps + d >= mid) & (ps + d < devs))
        def _():
            gather_copy(small, d).start()

    for d in range(1, mid):

        @pl.when(ps + d < mid)
        def _():
            gather_copy(big, d).start()

    for d in range(1, mid):

        @pl.when(d > ps)
        def _():
            kv_buf[small, d] = jnp.zeros(kv_buf.shape[2:], kv_buf.dtype)

        @pl.when(d > ps)
        def _():
            kv_buf[big, mid + d] = jnp.zeros(kv_buf.shape[2:], kv_buf.dtype)

    own_ids = jnp.transpose(
        jnp.broadcast_to(seg_ref[pl.ds(me, 1), :].astype(jnp.float32), (tok, tok))
    )
    rows = lax.broadcasted_iota(jnp.int32, (tok, tok), 0)
    columns = lax.broadcasted_iota(jnp.int32, (tok, tok), 1)
    for d in range(devs):
        ids = seg_ref[pl.ds(behind(d), 1), :].astype(jnp.float32)
        block = jnp.where(own_ids == ids, 0.0, MASKED)
        if d == 0:
            block = jnp.where(columns <= rows, block, MASKED)
        bias[1, :, d * tok : (d + 1) * tok] = jnp.where(d <= ps + mid, block, MASKED)
        if d < mid:
            bias[0, :, d * tok : (d + 1) * tok] = jnp.where(d <= ps, block, MASKED)

    def within(j):
        return lax.rem(p0 + j, devs)

    def scatter_copy(bufs, j):
        part, landed, s_send, s_recv = bufs[0], bufs[1], bufs[4], bufs[5]
        return pltpu.make_async_remote_copy(
            src_ref=part.at[within(j)],
            dst_ref=landed.at[j],
            send_sem=s_send.at[j],
            recv_sem=s_recv.at[j],
            device_id={"ctx": plane * devs + within(j)},
            device_id_type=MESH,
        )

    def plane_copy(bufs, j):
        across, s_send, s_recv = bufs[2], bufs[6], bufs[7]
        return pltpu.make_async_remote_copy(
            src_ref=across.at[plane],
            dst_ref=across.at[plane],
            send_sem=s_send.at[j],
            recv_sem=s_recv.at[j],
            device_id={"ctx": lax.rem(me + j * devs, ctx)},
            device_id_type=MESH,
        )

    def spread_copy(bufs, j):
        whole, s_send, s_recv = bufs[3], bufs[8], bufs[9]
        return pltpu.make_async_remote_copy(
            src_ref=whole.at[p0],
            dst_ref=whole.at[p0],
            send_sem=s_send.at[j],
            recv_sem=s_recv.at[j],
            device_id={"ctx": plane * devs + within(j)},
            device_id_type=MESH,
        )

    def start_scatter(bufs):
        for j in range(1, devs):
            scatter_copy(bufs, j).start()

    def start_planes(bufs):
        total = bufs[0][p0].astype(jnp.float32)
        for j in range(1, devs):
            scatter_copy(bufs, j).wait_recv()
            total = total + bufs[1][j].astype(jnp.float32)
        bufs[2][plane] = total.astype(jnp.bfloat16)
        for j in range(1, planes):
            plane_copy(bufs, j).start()

    def start_spread(bufs):
        for j in range(1, planes):
            plane_copy(bufs, j).wait_recv()
        total = bufs[2][0].astype(jnp.float32)
        for j in range(1, planes):
            total = total + bufs[2][j].astype(jnp.float32)
        bufs[3][p0] = total.astype(jnp.bfloat16)
        for j in range(1, devs):
            spread_copy(bufs, j).start()

    def finish(bufs, down_out, up_out, up_pieces):
        for j in range(1, devs):
            spread_copy(bufs, j).wait_recv()
        width = down_out.shape[1] // devs
        up_width = 2 * up_out.shape[2] // up_pieces
        for p in range(devs):
            down_out[:, p * width : (p + 1) * width] = adapter_scale * bufs[3][
                p, :, :width
            ].astype(jnp.float32)
            if p < up_pieces:
                h, at = p // (up_pieces // 2), p % (up_pieces // 2)
                up_out[:, h, at * up_width : (at + 1) * up_width] = adapter_scale * bufs[3][
                    p, :, width:
                ].astype(jnp.float32)
        for j in range(1, devs):
            scatter_copy(bufs, j).wait_send()
            spread_copy(bufs, j).wait_send()
        for j in range(1, planes):
            plane_copy(bufs, j).wait_send()

    def project_down(bufs, act):
        width = x_ref.shape[1] // devs
        for p in range(devs):
            bufs[0][p, :, :width] = jnp.dot(
                act, x_ref[:, p * width : (p + 1) * width], preferred_element_type=jnp.float32
            ).astype(jnp.bfloat16)

    if with_adapters:
        for source, act in ((q_down_ref, q_down), (v_down_ref, v_down)):
            act[...] = lax.dot_general(
                source[...],
                x_ref[...],
                (((1,), (1,)), ((), ())),
                preferred_element_type=jnp.float32,
            ).astype(jnp.bfloat16)
        for h in range(2):
            q_up[h] = q_up_ref[:, h, :]
            v_up[h] = v_up_ref[:, h, :]
        q_act[...] = jnp.zeros_like(q_act)
        rank = q_act.shape[0]
        for p in range(2 * kv_heads, devs):
            v_bufs[0][p, :, x_ref.shape[1] // devs :] = jnp.zeros((rank, HEAD_SIZE), jnp.bfloat16)

    def stacked(ref, h, g):
        return jnp.concatenate(
            [
                ref[h, :, g * group_width + r * HEAD_SIZE : g * group_width + (r + 1) * HEAD_SIZE]
                for r in range(repeat)
            ],
            axis=0,
        )

    def send_parts(which, total, h, g, slots, limit):
        for d in range(slots):
            block = jnp.transpose(total[:, d * tok : (d + 1) * tok])
            if d == 0:
                own_part[which, h, g] = block
            else:
                part_send[which, h, g, d] = block.astype(jnp.bfloat16)
        for d in range(1, slots):

            @pl.when(d < limit)
            def _():
                return_copy(which, h, g, d).start()

    def probabilities(h, g, slots, limit):
        keys = slots * tok
        k = kv_buf[h, :slots, g, :, :HEAD_SIZE].reshape(keys, HEAD_SIZE)

        def one_head(r, inner):
            lanes = pl.ds(pl.multiple_of(g * group_width + r * HEAD_SIZE, HEAD_SIZE), HEAD_SIZE)
            at = pl.ds(pl.multiple_of(r * tok, tok), tok)
            s = lax.dot_general(
                q_ref[h, :, lanes],
                k,
                (((1,), (1,)), ((), ())),
                preferred_element_type=jnp.float32,
            )
            t = s * exponent + bias[int(slots == devs), :, :keys]
            e = jnp.exp2(t - jnp.max(t, axis=1, keepdims=True))
            w = e * (1.0 / jnp.sum(e, axis=1, keepdims=True))
            w_scr[g, at, :keys] = w
            p_scr[at, :keys] = w.astype(jnp.bfloat16)
            return inner

        lax.fori_loop(0, repeat, one_head, 0, unroll=8)
        dv = lax.dot_general(
            stacked(do_ref, h, g),
            p_scr[:, :keys],
            (((0,), (0,)), ((), ())),
            preferred_element_type=jnp.float32,
        )
        send_parts(1, dv, h, g, slots, limit)

    def score_gradients(h, g, slots, limit):
        keys = slots * tok
        k = kv_buf[h, :slots, g, :, :HEAD_SIZE].reshape(keys, HEAD_SIZE)
        v = kv_buf[h, :slots, g, :, HEAD_SIZE:].reshape(keys, HEAD_SIZE)

        def one_head(r, inner):
            lanes = pl.ds(pl.multiple_of(g * group_width + r * HEAD_SIZE, HEAD_SIZE), HEAD_SIZE)
            at = pl.ds(pl.multiple_of(r * tok, tok), tok)
            dp = lax.dot_general(
                do_ref[h, :, lanes],
                v,
                (((1,), (1,)), ((), ())),
                preferred_element_type=jnp.float32,
            )
            w = w_scr[g, at, :keys]
            low = w.astype(jnp.bfloat16).astype(jnp.float32)
            dot = jnp.sum(low * dp, axis=1, keepdims=True)
            ds = (w * (dp - dot)).astype(jnp.bfloat16)
            p_scr[at, :keys] = ds
            dq = jnp.dot(ds, k, preferred_element_type=jnp.float32) * scaling
            dq_ref[h, :, lanes] = dq.astype(jnp.bfloat16)
            return inner

        lax.fori_loop(0, repeat, one_head, 0, unroll=8)
        if with_adapters:
            lanes = slice(g * group_width, (g + 1) * group_width)
            dq_all = dq_ref[h, :, lanes]
            q_act[...] += lax.dot_general(
                q_up[h, :, lanes],
                dq_all,
                (((1,), (1,)), ((), ())),
                preferred_element_type=jnp.float32,
            )
            up = jnp.dot(q_down[...], dq_all, preferred_element_type=jnp.float32)
            up = up.astype(jnp.bfloat16)
            width = x_ref.shape[1] // devs
            each = group_width * 2 * kv_heads // devs
            pieces = group_width // each
            for i in range(pieces):
                q_bufs[0][(h * kv_heads + g) * pieces + i, :, width:] = up[
                    :, i * each : (i + 1) * each
                ]
        dk = lax.dot_general(
            stacked(q_ref, h, g),
            p_scr[:, :keys],
            (((0,), (0,)), ((), ())),
            preferred_element_type=jnp.float32,
        )
        send_parts(0, dk * scaling, h, g, slots, limit)

    def collect(which, out_ref):
        for d in range(1, devs):
            for g in range(kv_heads):

                @pl.when(ps + d < devs)
                def _():
                    return_copy(which, small, g, d).wait_recv()
                    own_part[which, small, g] += part_recv[which, small, g, d].astype(jnp.float32)

        for d in range(1, mid):
            for g in range(kv_heads):

                @pl.when(ps + d < mid)
                def _():
                    return_copy(which, big, g, d).wait_recv()
                    own_part[which, big, g] += part_recv[which, big, g, d].astype(jnp.float32)

        for h in range(2):
            for g in range(kv_heads):
                out_ref[h, :, g * HEAD_SIZE : (g + 1) * HEAD_SIZE] = own_part[which, h, g].astype(
                    jnp.bfloat16
                )

    def value_adapter():
        v_act = jnp.zeros(q_act.shape, jnp.float32)
        for h in range(2):
            v_act = v_act + lax.dot_general(
                v_up[h], gv_ref[h], (((1,), (1,)), ((), ())), preferred_element_type=jnp.float32
            )
            up = jnp.dot(v_down[...], gv_ref[h], preferred_element_type=jnp.float32)
            for g in range(kv_heads):
                v_bufs[0][h * kv_heads + g, :, x_ref.shape[1] // devs :] = up[
                    :, g * HEAD_SIZE : (g + 1) * HEAD_SIZE
                ].astype(jnp.bfloat16)
        project_down(v_bufs, v_act.astype(jnp.bfloat16))
        start_scatter(v_bufs)

    for d in range(1, mid):

        @pl.when(d <= ps)
        def _():
            gather_copy(small, d).wait_recv()

    for g in range(kv_heads):
        probabilities(small, g, mid, ps + 1)
    for g in range(kv_heads):
        score_gradients(small, g, mid, ps + 1)

    for d in range(1, devs):

        @pl.when(d <= ps + mid)
        def _():
            gather_copy(big, d).wait_recv()

    for g in range(kv_heads):
        probabilities(big, g, devs, ps + mid + 1)
    for g in range(kv_heads):
        score_gradients(big, g, devs, ps + mid + 1)
        if g == 0:
            collect(1, gv_ref)
            if with_adapters:
                value_adapter()

    if with_adapters:
        project_down(q_bufs, q_act[...].astype(jnp.bfloat16))
        start_scatter(q_bufs)
        start_planes(v_bufs)
        start_planes(q_bufs)
        start_spread(v_bufs)
        start_spread(q_bufs)
    collect(0, gk_ref)
    if with_adapters:
        finish(v_bufs, vd_out, vu_out, 2 * kv_heads)
        finish(q_bufs, qd_out, qu_out, devs)

    for d in range(1, devs):

        @pl.when(ps + d < devs)
        def _():
            gather_copy(small, d).wait_send()

        @pl.when(d <= ps + mid)
        def _():
            for which in range(2):
                for g in range(kv_heads):
                    return_copy(which, big, g, d).wait_send()

    for d in range(1, mid):

        @pl.when(ps + d < mid)
        def _():
            gather_copy(big, d).wait_send()

        @pl.when(d <= ps)
        def _():
            for which in range(2):
                for g in range(kv_heads):
                    return_copy(which, small, g, d).wait_send()


def attention_backward(q, do, k, v, seg, devs, adapters=None):
    tok, width = q.shape[1], q.shape[2]
    kv_heads = k.shape[2] // HEAD_SIZE
    repeat = width // k.shape[2]
    ctx = lax.axis_size("ctx")
    planes = ctx // devs
    bf16, f32 = jnp.bfloat16, jnp.float32
    vmem = pl.BlockSpec(memory_space=pltpu.VMEM)
    operands = (q, do, k, v, seg)
    results = [jax.ShapeDtypeStruct(a.shape, bf16) for a in (q, k, v)]
    scratch = [
        pltpu.VMEM((2, devs, kv_heads, tok, 2 * HEAD_SIZE), bf16),
        pltpu.VMEM((2, 2, kv_heads, devs, tok, HEAD_SIZE), bf16),
        pltpu.VMEM((2, 2, kv_heads, devs, tok, HEAD_SIZE), bf16),
        pltpu.VMEM((2, 2, kv_heads, tok, HEAD_SIZE), f32),
        pltpu.VMEM((repeat * tok, devs * tok), bf16),
        pltpu.VMEM((kv_heads, repeat * tok, devs * tok), f32),
        pltpu.VMEM((2, tok, devs * tok), f32),
        pltpu.SemaphoreType.DMA((2, devs)),
        pltpu.SemaphoreType.DMA((2, devs)),
        pltpu.SemaphoreType.DMA((2, 2, kv_heads, devs)),
        pltpu.SemaphoreType.DMA((2, 2, kv_heads, devs)),
    ]
    if adapters is not None:
        operands = operands + adapters
        x, q_down, v_down, q_up, v_up = adapters
        rank = q_down.shape[0]
        results += [jax.ShapeDtypeStruct(a.shape, f32) for a in (q_down, q_up, v_down, v_up)]
        scratch += [
            pltpu.VMEM((rank, tok), bf16),
            pltpu.VMEM((rank, tok), bf16),
            pltpu.VMEM((2, rank, q.shape[2]), bf16),
            pltpu.VMEM((2, rank, k.shape[2]), bf16),
            pltpu.VMEM((rank, tok), f32),
        ]
        for columns in ((x.shape[1] + 2 * width) // devs, x.shape[1] // devs + HEAD_SIZE):
            scratch += [
                pltpu.VMEM((n, rank, columns), bf16) for n in (devs, devs, planes, devs)
            ]
            scratch += [
                pltpu.SemaphoreType.DMA((n,)) for n in (devs, devs, planes, planes, devs, devs)
            ]
    return pl.pallas_call(
        functools.partial(attention_kernel, ctx, devs, adapters is not None),
        out_shape=tuple(results),
        in_specs=[vmem] * len(operands),
        out_specs=(vmem,) * len(results),
        scratch_shapes=scratch,
        compiler_params=pltpu.CompilerParams(
            collective_id=0, has_side_effects=True, vmem_limit_bytes=52 * 1024 * 1024
        ),
        name="attention_backward",
    )(*operands)


def paired_kernel(
    chips,
    span,
    q_hbm,
    do_hbm,
    k_hbm,
    v_hbm,
    seg_hbm,
    x_ref,
    q_down_hbm,
    v_down_hbm,
    q_up_hbm,
    v_up_hbm,
    dq_out,
    gk_out,
    gv_out,
    qd_out,
    qu_out,
    vd_out,
    vu_out,
    q_raw,
    do_raw,
    k_raw,
    v_raw,
    seg_ref,
    q_down_ref,
    v_down_ref,
    q_up_ref,
    v_up_ref,
    q_away,
    do_away,
    k_ref,
    v_ref,
    dq_land,
    qb,
    dob,
    kb,
    vb,
    xb,
    dqb,
    p_small,
    p_big,
    bias,
    part_send,
    part_recv,
    acc,
    sib_part,
    down_mine,
    down_theirs,
    act_mine,
    act_theirs,
    mixed_mine,
    mixed_theirs,
    acts,
    q_parts,
    q_land,
    q_sums,
    q_other,
    v_parts,
    v_land,
    v_sums,
    v_other,
    local_sem,
    swap_send,
    swap_recv,
    g_send,
    g_recv,
    r_send,
    r_recv,
    a_send,
    a_recv,
):
    bf16, f32 = jnp.bfloat16, jnp.float32
    tok = q_raw.shape[0]
    pair = 2 * tok
    width = qb.shape[2]
    heads = width // HEAD_SIZE
    columns = xb.shape[1]
    each = columns // chips
    up_each = 2 * width // chips
    rank = acts.shape[1]
    mid = span // 2
    scaling = HEAD_SIZE ** (-0.5)
    exponent = scaling * math.log2(math.e)
    me = lax.axis_index("ctx")
    chip = me // 2
    core = lax.rem(me, 2)
    other = 1 - core
    place = lax.rem(chip, span)
    small = place // mid
    big = 1 - small
    ps = lax.rem(place, mid)

    def ahead(d):
        return lax.rem(chip + d, chips)

    def behind(d):
        return lax.rem(chip + chips - d, chips)

    def device(chip_at, core_at):
        return {"ctx": 2 * chip_at + core_at}

    sibling = device(chip, other)

    def rows(at):
        return pl.ds(pl.multiple_of(at * tok, tok), tok)

    def half_columns(at, size):
        return pl.ds(pl.multiple_of(at * size, size), size)

    barrier = pltpu.get_barrier_semaphore()
    pl.semaphore_signal(barrier, inc=1, device_id=sibling, device_id_type=MESH)
    for d in range(1, chips):
        pl.semaphore_signal(
            barrier, inc=1, device_id=device(ahead(d), core), device_id_type=MESH
        )
    for d in range(1, span):
        pl.semaphore_signal(
            barrier, inc=1, device_id=device(ahead(d), other), device_id_type=MESH
        )
        pl.semaphore_signal(
            barrier, inc=1, device_id=device(behind(d), other), device_id_type=MESH
        )

    staged = [
        pltpu.make_async_copy(src, dst, local_sem.at[i])
        for i, (src, dst) in enumerate(
            (
                (k_hbm, k_raw),
                (v_hbm, v_raw),
                (q_hbm, q_raw),
                (do_hbm, do_raw),
                (seg_hbm, seg_ref),
                (x_ref.at[:, half_columns(core, columns)], xb.at[rows(core)]),
                (q_down_hbm, q_down_ref),
                (v_down_hbm, v_down_ref),
                (q_up_hbm, q_up_ref),
                (v_up_hbm, v_up_ref),
            )
        )
    ]
    for copy in staged:
        copy.start()

    def swap_columns(row):
        return pltpu.make_async_remote_copy(
            src_ref=x_ref.at[:, half_columns(other, columns)],
            dst_ref=xb.at[rows(row)],
            send_sem=swap_send.at[4],
            recv_sem=swap_recv.at[4],
            device_id=sibling,
            device_id_type=MESH,
        )

    def swap_half(h, i, row):
        return pltpu.make_async_remote_copy(
            src_ref=(q_away, do_away)[i].at[h],
            dst_ref=(qb, dob)[i].at[h, rows(row)],
            send_sem=swap_send.at[2 * h + i],
            recv_sem=swap_recv.at[2 * h + i],
            device_id=sibling,
            device_id_type=MESH,
        )

    def gather_copy(which, h, d, to, row):
        src = (k_ref, v_ref)[which].at[h, :, half_columns(to, HEAD_SIZE)]
        return pltpu.make_async_remote_copy(
            src_ref=src,
            dst_ref=(kb, vb)[which].at[h, d, rows(row)],
            send_sem=g_send.at[which, h, d, to],
            recv_sem=g_recv.at[which, h, d, row],
            device_id=device(ahead(d), to),
            device_id_type=MESH,
        )

    def gather_start(which, h, d):
        for to in range(2):
            gather_copy(which, h, d, to, core).start()

    def gather_wait(which, h, d):
        for row in range(2):
            gather_copy(which, h, d, row, row).wait_recv()

    def gather_sent(which, h, d):
        for to in range(2):
            gather_copy(which, h, d, to, core).wait_send()

    @pl.when(ps == 0)
    def _():
        for buf in (kb, vb):
            buf[small, 1] = jnp.zeros(buf.shape[2:], bf16)
            buf[big, span - 1] = jnp.zeros(buf.shape[2:], bf16)

    to_row = lax.broadcasted_iota(jnp.int32, (pair, pair), 0)
    from_row = lax.broadcasted_iota(jnp.int32, (pair, pair), 1)
    parting = jnp.where(from_row == 2 * lax.rem(to_row, tok) + to_row // tok, 1.0, 0.0).astype(bf16)

    def parted(raw, lanes):
        return jnp.dot(
            parting, raw[:, :, lanes].reshape(pair, HEAD_SIZE), preferred_element_type=f32
        ).astype(bf16)

    for i, (raw, ref, buf) in enumerate(((k_raw, k_ref, kb), (v_raw, v_ref, vb))):
        staged[i].wait()
        for head in range(2):
            lanes = slice(head * HEAD_SIZE, (head + 1) * HEAD_SIZE)
            both = parted(raw, lanes)
            for h in range(2):
                ref[h, :, lanes] = both[h * tok : (h + 1) * tok]
        for h in range(2):
            buf[h, 0, rows(core)] = ref[h, :, half_columns(core, HEAD_SIZE)]
    for i, (raw, buf, away) in enumerate(((q_raw, qb, q_away), (do_raw, dob, do_away))):
        staged[2 + i].wait()
        for j in range(heads):
            lanes = slice(j * HEAD_SIZE, (j + 1) * HEAD_SIZE)
            for at, dst in ((core, buf), (other, away)):
                both = parted(raw, pl.ds(pl.multiple_of(at * width + j * HEAD_SIZE, HEAD_SIZE), HEAD_SIZE))
                for h in range(2):
                    block = both[h * tok : (h + 1) * tok]
                    if dst is buf:
                        dst[h, rows(core), lanes] = block
                    else:
                        dst[h, :, lanes] = block

    staged[4].wait()

    def chip_ids(at):
        first = seg_ref[pl.ds(2 * at, 1), :]
        second = seg_ref[pl.ds(2 * at + 1, 1), :]
        return jnp.concatenate([first, second], axis=1).astype(f32)

    own_ids = jnp.transpose(jnp.broadcast_to(chip_ids(chip), (pair, pair)))
    row = lax.broadcasted_iota(jnp.int32, (pair, pair), 0)
    column = lax.broadcasted_iota(jnp.int32, (pair, pair), 1)
    for d in range(span):
        block = jnp.where(own_ids == chip_ids(behind(d)), 0.0, MASKED)
        if d == 0:
            block = jnp.where(column <= row, block, MASKED)
        bias[1, :, d * pair : (d + 1) * pair] = jnp.where(d <= ps + mid, block, MASKED)
        if d < mid:
            bias[0, :, d * pair : (d + 1) * pair] = jnp.where(d <= ps, block, MASKED)

    pl.semaphore_wait(barrier, chips + 2 * (span - 1))

    for which in range(2):
        if which == 0:
            gather_copy(0, small, 0, other, core).start()
        for d in range(1, mid):

            @pl.when(ps + d < mid)
            def _():
                gather_start(which, small, d)

        if which == 0:
            swap_half(small, 0, core).start()
        for d in range(1, span):

            @pl.when((ps + d >= mid) & (ps + d < span))
            def _():
                gather_start(which, small, d)

        for d in range(1, mid):

            @pl.when(ps + d < mid)
            def _():
                gather_start(which, big, d)

        if which == 0:
            swap_half(small, 1, core).start()
            gather_copy(0, big, 0, other, core).start()
            for i in range(2):
                swap_half(big, i, core).start()
            for h in range(2):
                gather_copy(1, h, 0, other, core).start()
            swap_columns(core).start()

    def exchange(src, dst, i):
        return pltpu.make_async_remote_copy(
            src_ref=src,
            dst_ref=dst,
            send_sem=swap_send.at[i],
            recv_sem=swap_recv.at[i],
            device_id=sibling,
            device_id_type=MESH,
        )

    down_swap = exchange(down_mine, down_theirs, 5)
    act_swap = exchange(act_mine, act_theirs, 6)
    mixed_swap = exchange(mixed_mine, mixed_theirs, 7)

    def part_swap(which, h):
        return pltpu.make_async_remote_copy(
            src_ref=sib_part.at[which, h],
            dst_ref=acc.at[which, h, core],
            send_sem=swap_send.at[8 + 2 * which + h],
            recv_sem=swap_recv.at[8 + 2 * which + h],
            device_id=sibling,
            device_id_type=MESH,
        )

    def part_wait(which, h):
        return pltpu.make_async_remote_copy(
            src_ref=sib_part.at[which, h],
            dst_ref=acc.at[which, h, other],
            send_sem=swap_send.at[8 + 2 * which + h],
            recv_sem=swap_recv.at[8 + 2 * which + h],
            device_id=sibling,
            device_id_type=MESH,
        )

    def dq_swap(h):
        return exchange(dqb.at[h, rows(other)], dq_land.at[h], 12 + h)

    def scatter_copy(s, parts, land, j):
        return pltpu.make_async_remote_copy(
            src_ref=parts.at[ahead(j)],
            dst_ref=land.at[j],
            send_sem=a_send.at[s, j],
            recv_sem=a_recv.at[s, j],
            device_id=device(ahead(j), core),
            device_id_type=MESH,
        )

    def spread_copy(s, sums, j, source):
        return pltpu.make_async_remote_copy(
            src_ref=sums.at[source],
            dst_ref=sums.at[source],
            send_sem=a_send.at[2 + s, j],
            recv_sem=a_recv.at[2 + s, j],
            device_id=device(ahead(j), core),
            device_id_type=MESH,
        )

    q_set = (0, q_parts, q_land, q_sums, q_other)
    v_set = (1, v_parts, v_land, v_sums, v_other)

    def start_scatter(bufs):
        for j in range(1, chips):
            scatter_copy(bufs[0], bufs[1], bufs[2], j).start()

    def start_spread(bufs):
        total = bufs[1][chip].astype(f32)
        for j in range(1, chips):
            scatter_copy(bufs[0], bufs[1], bufs[2], j).wait_recv()
            total = total + bufs[2][j].astype(f32)
        bufs[3][chip] = total.astype(bf16)
        for j in range(1, chips):
            spread_copy(bufs[0], bufs[3], j, chip).start()

    def hand_copy(bufs):
        return exchange(bufs[3], bufs[4], 14 + bufs[0])

    def start_hand(bufs):
        for j in range(1, chips):
            spread_copy(bufs[0], bufs[3], j, behind(j)).wait_recv()
        hand_copy(bufs).start()

    def finish(bufs, down_out, up_out, up_width, up_pieces):
        def write(source, at):
            for i in range(chips):
                lanes = pl.ds(pl.multiple_of(at * columns + i * each, each), each)
                down_out[:, lanes] = adapter_scale * source[i, :, :each].astype(f32)
                if i < up_pieces:
                    h, step = i // (up_pieces // 2), i % (up_pieces // 2)
                    size = up_width // (up_pieces // 2)
                    lanes = pl.ds(pl.multiple_of(at * up_width + step * size, size), size)
                    up_out[:, h, lanes] = adapter_scale * source[i, :, each:].astype(f32)

        write(bufs[3], core)
        hand_copy(bufs).wait_recv()
        write(bufs[4], other)
        for j in range(1, chips):
            scatter_copy(bufs[0], bufs[1], bufs[2], j).wait_send()
            spread_copy(bufs[0], bufs[3], j, chip).wait_send()
        hand_copy(bufs).wait_send()

    def project_down(parts, act):
        for i in range(chips):
            parts[i, :, :each] = jnp.dot(
                act, xb[:, i * each : (i + 1) * each], preferred_element_type=f32
            ).astype(bf16)

    def return_copy(which, h, d, to, head):
        return pltpu.make_async_remote_copy(
            src_ref=part_send.at[which, h, d, rows(to)],
            dst_ref=part_recv.at[which, h, d, head],
            send_sem=r_send.at[which, h, d, to],
            recv_sem=r_recv.at[which, h, d, head],
            device_id=device(behind(d), to),
            device_id_type=MESH,
        )

    def send_parts(which, total, h, slots, limit):
        for d in reversed(range(slots)):
            block = jnp.transpose(total[:, d * pair : (d + 1) * pair])
            if d == 0:
                acc[which, h, core] = jnp.where(core == 0, block[:tok], block[tok:])
                sib_part[which, h] = jnp.where(core == 0, block[tok:], block[:tok])
                part_swap(which, h).start()
            else:
                part_send[which, h, d] = block.astype(bf16)

                @pl.when(d < limit)
                def _():
                    for to in range(2):
                        return_copy(which, h, d, to, core).start()

    def stacked(ref, h):
        return jnp.concatenate(
            [ref[h, :, j * HEAD_SIZE : (j + 1) * HEAD_SIZE] for j in range(heads)], axis=0
        )

    def head_lanes(j):
        return pl.ds(pl.multiple_of(j * HEAD_SIZE, HEAD_SIZE), HEAD_SIZE)

    def head_rows(j):
        return pl.ds(pl.multiple_of(j * pair, pair), pair)

    def probabilities(h, p_ref, slots, limit):
        keys = slots * pair
        k = kb[h, :slots].reshape(keys, HEAD_SIZE)

        def one_head(j, inner):
            s = lax.dot_general(
                qb[h, :, head_lanes(j)], k, (((1,), (1,)), ((), ())), preferred_element_type=f32
            )
            t = s * exponent + bias[int(slots == span), :, :keys]
            e = jnp.exp2(t - jnp.max(t, axis=1, keepdims=True))
            w = e * (1.0 / jnp.sum(e, axis=1, keepdims=True))
            p_ref[head_rows(j)] = w.astype(bf16)
            return inner

        lax.fori_loop(0, heads, one_head, 0, unroll=UNROLL)

    def value_part(h, p_ref, slots, limit):
        dv = lax.dot_general(
            stacked(dob, h), p_ref[...], (((0,), (0,)), ((), ())), preferred_element_type=f32
        )
        send_parts(1, dv, h, slots, limit)

    def score_gradients(h, p_ref, slots, first, last):
        keys = slots * pair
        k = kb[h, :slots].reshape(keys, HEAD_SIZE)
        v = vb[h, :slots].reshape(keys, HEAD_SIZE)

        def one_head(j, inner):
            dp = lax.dot_general(
                dob[h, :, head_lanes(j)], v, (((1,), (1,)), ((), ())), preferred_element_type=f32
            )
            w = p_ref[head_rows(j)].astype(f32)
            dot = jnp.sum(w * dp, axis=1, keepdims=True)
            ds = (w * (dp - dot)).astype(bf16)
            p_ref[head_rows(j)] = ds
            dq = jnp.dot(ds, k, preferred_element_type=f32) * scaling
            dqb[h, :, head_lanes(j)] = dq.astype(bf16)
            return inner

        lax.fori_loop(first, last, one_head, 0, unroll=UNROLL)
        if last == heads:
            dq_swap(h).start()

    def query_adapter(h):
        dq = dqb[h]
        up_rows = q_up_ref[:, h, half_columns(core, width)]
        up = jnp.dot(acts[0], dq, preferred_element_type=f32).astype(bf16)
        return lax.dot_general(
            up_rows, dq, (((1,), (1,)), ((), ())), preferred_element_type=f32
        ), up

    def key_part(h, p_ref, slots, limit):
        dk = lax.dot_general(
            stacked(qb, h), p_ref[...], (((0,), (0,)), ((), ())), preferred_element_type=f32
        )
        send_parts(0, dk * scaling, h, slots, limit)

    def collect(which):
        for h in range(2):
            part_wait(which, h).wait_recv()
        for d in range(1, span):

            @pl.when(ps + d < span)
            def _():
                for head in range(2):
                    return_copy(which, small, d, head, head).wait_recv()
                    acc[which, small, head] += part_recv[which, small, d, head].astype(f32)

        for d in range(1, mid):

            @pl.when(ps + d < mid)
            def _():
                for head in range(2):
                    return_copy(which, big, d, head, head).wait_recv()
                    acc[which, big, head] += part_recv[which, big, d, head].astype(f32)

        return [
            jnp.concatenate([acc[which, h, 0], acc[which, h, 1]], axis=1).astype(bf16)
            for h in range(2)
        ]

    def wait_swap(h, i):
        swap_half(h, i, other).wait_recv()

    wait_swap(small, 0)
    gather_copy(0, small, 0, other, other).wait_recv()
    for d in range(1, mid):

        @pl.when(d <= ps)
        def _():
            gather_wait(0, small, d)

    probabilities(small, p_small, mid, ps + 1)
    wait_swap(small, 1)
    value_part(small, p_small, mid, ps + 1)

    for i in range(5, 10):
        staged[i].wait()
    swap_columns(other).wait_recv()
    for i, source in enumerate((q_down_ref, v_down_ref)):
        down_mine[i] = lax.dot_general(
            source[:, half_columns(core, columns)],
            xb[...],
            (((1,), (1,)), ((), ())),
            preferred_element_type=f32,
        )
    down_swap.start()

    wait_swap(big, 0)
    gather_copy(0, big, 0, other, other).wait_recv()
    for d in range(1, span):

        @pl.when(d <= ps + mid)
        def _():
            gather_wait(0, big, d)

    probabilities(big, p_big, span, ps + mid + 1)
    wait_swap(big, 1)
    value_part(big, p_big, span, ps + mid + 1)

    down_swap.wait()
    for i in range(2):
        acts[i] = (down_mine[i] + down_theirs[i]).astype(bf16)

    for h in (small, big):
        gather_copy(1, h, 0, other, other).wait_recv()
    for d in range(1, mid):

        @pl.when(d <= ps)
        def _():
            gather_wait(1, small, d)

    for d in range(1, span):

        @pl.when(d <= ps + mid)
        def _():
            gather_wait(1, big, d)

    score_gradients(small, p_small, mid, 0, heads)
    score_gradients(big, p_big, span, 0, heads // 2)

    gv = collect(1)
    v_act = jnp.zeros((rank, tok), f32)
    own_lanes = half_columns(core, tok)
    for h in range(2):
        v_act = v_act + lax.dot_general(
            v_up_ref[:, h, :], gv[h], (((1,), (1,)), ((), ())), preferred_element_type=f32
        )
        up = jnp.dot(acts[1, :, own_lanes], gv[h], preferred_element_type=f32)
        first, second = up[:, :HEAD_SIZE], up[:, HEAD_SIZE:]
        mixed_mine[1 + h] = jnp.where(core == 0, second, first)
        mixed_mine[3 + h] = jnp.where(core == 0, first, second)
    mixed_mine[0] = v_act
    mixed_swap.start()
    for h in range(2):
        gv_out[:, h, :] = gv[h]

    score_gradients(big, p_big, span, heads // 2, 3 * heads // 4)

    mixed_swap.wait()
    acts[2, :, own_lanes] = mixed_mine[0].astype(bf16)
    acts[2, :, half_columns(other, tok)] = mixed_theirs[0].astype(bf16)
    for i in range(chips):
        if i < 2:
            v_parts[i, :, each:] = (mixed_mine[3 + i] + mixed_theirs[1 + i]).astype(bf16)
        else:
            v_parts[i, :, each:] = jnp.zeros((rank, HEAD_SIZE), bf16)
    project_down(v_parts, acts[2])
    start_scatter(v_set)

    score_gradients(big, p_big, span, 3 * heads // 4, heads)

    act = jnp.zeros((rank, pair), f32)
    for h in range(2):
        more, up = query_adapter(h)
        act = act + more
        for i in range(chips // 2):
            q_parts[h * (chips // 2) + i, :, each:] = up[:, i * up_each : (i + 1) * up_each]
    act_mine[...] = act
    act_swap.start()
    act_swap.wait()
    project_down(q_parts, (act_mine[...] + act_theirs[...]).astype(bf16))
    start_scatter(q_set)

    key_part(big, p_big, span, ps + mid + 1)
    key_part(small, p_small, mid, ps + 1)

    start_spread(v_set)
    start_spread(q_set)
    gk = collect(0)
    for h in range(2):
        gk_out[:, h, :] = gk[h]
    for h in range(2):
        dq_out[:, h, half_columns(core, width)] = dqb[h, rows(core)]
        dq_swap(h).wait_recv()
        dq_out[:, h, half_columns(other, width)] = dq_land[h]
    start_hand(v_set)
    start_hand(q_set)
    finish(v_set, vd_out, vu_out, HEAD_SIZE, 2)
    finish(q_set, qd_out, qu_out, width, chips)

    for h in range(2):
        dq_swap(h).wait_send()
        for i in range(2):
            swap_half(h, i, core).wait_send()
            part_swap(i, h).wait_send()
            gather_copy(i, h, 0, other, core).wait_send()
    swap_columns(core).wait_send()
    for which in range(2):
        for d in range(1, span):

            @pl.when(ps + d < span)
            def _():
                gather_sent(which, small, d)

            @pl.when(d <= ps + mid)
            def _():
                for to in range(2):
                    return_copy(which, big, d, to, core).wait_send()

        for d in range(1, mid):

            @pl.when(ps + d < mid)
            def _():
                gather_sent(which, big, d)

            @pl.when(d <= ps)
            def _():
                for to in range(2):
                    return_copy(which, small, d, to, core).wait_send()


def deliver_kernel(*refs):
    count = (len(refs) - 1) // 2
    copies = [
        pltpu.make_async_copy(refs[i], refs[count + i], refs[-1].at[i]) for i in range(count)
    ]
    for copy in copies:
        copy.start()
    for copy in copies:
        copy.wait()


def deliver(arrays):
    vmem = pl.BlockSpec(memory_space=pltpu.VMEM)
    hbm = pl.BlockSpec(memory_space=pltpu.MemorySpace.HBM)
    return pl.pallas_call(
        deliver_kernel,
        out_shape=tuple(jax.ShapeDtypeStruct(a.shape, a.dtype) for a in arrays),
        in_specs=[vmem] * len(arrays),
        out_specs=(hbm,) * len(arrays),
        scratch_shapes=[pltpu.SemaphoreType.DMA((len(arrays),))],
        name="deliver",
    )(*arrays)


def paired_backward(q, do, k, v, seg, x, q_down, v_down, q_up, v_up, span):
    tok, width = q.shape[0], q.shape[2] // 2
    pair = 2 * tok
    heads = width // HEAD_SIZE
    chips = lax.axis_size("ctx") // 2
    rank = q_down.shape[0]
    columns = x.shape[1] // 2
    bf16, f32 = jnp.bfloat16, jnp.float32
    vmem = pl.BlockSpec(memory_space=pltpu.VMEM)
    hbm = pl.BlockSpec(memory_space=pltpu.MemorySpace.HBM)
    q_piece = columns // chips + 2 * width // chips
    v_piece = columns // chips + HEAD_SIZE
    scratch = [pltpu.VMEM(a.shape, a.dtype) for a in (q, do, k, v, seg, q_down, v_down, q_up, v_up)]
    scratch += [
        pltpu.VMEM((2, tok, width), bf16),
        pltpu.VMEM((2, tok, width), bf16),
        pltpu.VMEM((2, tok, 2 * HEAD_SIZE), bf16),
        pltpu.VMEM((2, tok, 2 * HEAD_SIZE), bf16),
        pltpu.VMEM((2, tok, width), bf16),
        pltpu.VMEM((2, pair, width), bf16),
        pltpu.VMEM((2, pair, width), bf16),
        pltpu.VMEM((2, span, pair, HEAD_SIZE), bf16),
        pltpu.VMEM((2, span, pair, HEAD_SIZE), bf16),
        pltpu.VMEM((pair, columns), bf16),
        pltpu.VMEM((2, pair, width), bf16),
        pltpu.VMEM((heads * pair, span // 2 * pair), bf16),
        pltpu.VMEM((heads * pair, span * pair), bf16),
        pltpu.VMEM((2, pair, span * pair), f32),
        pltpu.VMEM((2, 2, span, pair, HEAD_SIZE), bf16),
        pltpu.VMEM((2, 2, span, 2, tok, HEAD_SIZE), bf16),
        pltpu.VMEM((2, 2, 2, tok, HEAD_SIZE), f32),
        pltpu.VMEM((2, 2, tok, HEAD_SIZE), f32),
        pltpu.VMEM((2, rank, pair), f32),
        pltpu.VMEM((2, rank, pair), f32),
        pltpu.VMEM((rank, pair), f32),
        pltpu.VMEM((rank, pair), f32),
        pltpu.VMEM((5, rank, HEAD_SIZE), f32),
        pltpu.VMEM((5, rank, HEAD_SIZE), f32),
        pltpu.VMEM((3, rank, pair), bf16),
    ]
    for piece in (q_piece, v_piece):
        scratch += [pltpu.VMEM((chips, rank, piece), bf16) for _ in range(4)]
    scratch += [
        pltpu.SemaphoreType.DMA((10,)),
        pltpu.SemaphoreType.DMA((16,)),
        pltpu.SemaphoreType.DMA((16,)),
    ]
    scratch += [pltpu.SemaphoreType.DMA((2, 2, span, 2)) for _ in range(4)]
    scratch += [pltpu.SemaphoreType.DMA((4, chips)) for _ in range(2)]
    return pl.pallas_call(
        functools.partial(paired_kernel, chips, span),
        out_shape=tuple(
            [jax.ShapeDtypeStruct(a.shape, bf16) for a in (q, k, v)]
            + [jax.ShapeDtypeStruct(a.shape, f32) for a in (q_down, q_up, v_down, v_up)]
        ),
        in_specs=[hbm] * 10,
        out_specs=(vmem,) * 7,
        scratch_shapes=scratch,
        compiler_params=pltpu.CompilerParams(
            collective_id=1, has_side_effects=True, vmem_limit_bytes=60 * 1024 * 1024
        ),
        name="paired_backward",
    )(q, do, k, v, seg, x, q_down, v_down, q_up, v_up)


def on_device(
    projected_queries,
    projected_keys,
    projected_values,
    output_gradient,
    normed_layer_input,
    segment,
    query_adapter_down,
    query_adapter_up,
    value_adapter_down,
    value_adapter_up,
):
    tok_rows = projected_queries.shape[0]
    query_width = projected_queries.shape[2]
    key_width = projected_keys.shape[2]
    key_value_heads = key_width // HEAD_SIZE
    group_devs = GROUP // tok_rows
    ctx = lax.axis_size("ctx")
    paired = (
        lax.axis_size("fsdp") == 1
        and group_devs % 4 == 0
        and key_value_heads == 2
        and tok_rows == HEAD_SIZE
        and query_width % (ctx * HEAD_SIZE // 2) == 0
        and normed_layer_input.shape[1] % (ctx * HEAD_SIZE) == 0
    )
    if paired:
        return deliver(
            paired_backward(
                projected_queries,
                output_gradient,
                projected_keys,
                projected_values,
                segment.reshape(-1, tok_rows),
                normed_layer_input,
                query_adapter_down,
                value_adapter_down,
                query_adapter_up,
                value_adapter_up,
                group_devs // 2,
            )
        )
    query_grad, key_grad, value_grad = attention_backward(
        projected_queries.transpose(1, 0, 2),
        output_gradient.transpose(1, 0, 2),
        projected_keys.transpose(1, 0, 2),
        projected_values.transpose(1, 0, 2),
        segment.reshape(-1, tok_rows),
        group_devs,
    )
    grad_query = query_grad.transpose(1, 0, 2)
    grad_key = key_grad.transpose(1, 0, 2)
    grad_value = value_grad.transpose(1, 0, 2)
    adapter_input = lax.psum(
        (
            jnp.dot(normed_layer_input, query_adapter_down.T, preferred_element_type=jnp.float32),
            jnp.dot(normed_layer_input, value_adapter_down.T, preferred_element_type=jnp.float32),
        ),
        "fsdp",
    )
    query_down_part = adapter_input[0].astype(jnp.bfloat16)
    value_down_part = adapter_input[1].astype(jnp.bfloat16)
    query_flattened_rows = grad_query.reshape(tok_rows, -1)
    value_flattened_rows = grad_value.reshape(tok_rows, -1)
    adapter_rank_rows = query_adapter_up.shape[0]
    adapter_output = lax.psum(
        (
            jnp.dot(
                query_flattened_rows,
                query_adapter_up.reshape(adapter_rank_rows, -1).T,
                preferred_element_type=jnp.float32,
            ),
            jnp.dot(
                value_flattened_rows,
                value_adapter_up.reshape(adapter_rank_rows, -1).T,
                preferred_element_type=jnp.float32,
            ),
        ),
        "fsdp",
    )
    query_up_part = adapter_output[0].astype(jnp.bfloat16)
    value_up_part = adapter_output[1].astype(jnp.bfloat16)
    local_down_query = jnp.dot(
        query_up_part.T, normed_layer_input, preferred_element_type=jnp.float32
    )
    local_up_query = jnp.dot(
        query_down_part.T, query_flattened_rows, preferred_element_type=jnp.float32
    ).reshape(adapter_rank_rows, 2, -1)
    local_down_value = jnp.dot(
        value_up_part.T, normed_layer_input, preferred_element_type=jnp.float32
    )
    local_up_value = jnp.dot(
        value_down_part.T, value_flattened_rows, preferred_element_type=jnp.float32
    ).reshape(adapter_rank_rows, 2, -1)
    gradient_totals = lax.psum(
        (local_down_query, local_up_query, local_down_value, local_up_value), "ctx"
    )
    return (
        grad_query,
        grad_key,
        grad_value,
        adapter_scale * gradient_totals[0],
        adapter_scale * gradient_totals[1],
        adapter_scale * gradient_totals[2],
        adapter_scale * gradient_totals[3],
    )


def solution(mesh):
    in_specs = (
        P(("rep", "ctx"), None, "fsdp"),
        P(("rep", "ctx"), None, "fsdp"),
        P(("rep", "ctx"), None, "fsdp"),
        P(("rep", "ctx"), None, "fsdp"),
        P(("rep", "ctx"), "fsdp"),
        P("rep"),
        P(None, "fsdp"),
        P(None, None, "fsdp"),
        P(None, "fsdp"),
        P(None, None, "fsdp"),
    )
    out_specs = (
        P(("rep", "ctx"), None, "fsdp"),
        P(("rep", "ctx"), None, "fsdp"),
        P(("rep", "ctx"), None, "fsdp"),
        P("rep", "fsdp"),
        P("rep", None, "fsdp"),
        P("rep", "fsdp"),
        P("rep", None, "fsdp"),
    )
    return jax.shard_map(
        on_device, mesh=mesh, in_specs=in_specs, out_specs=out_specs, check_vma=False
    )
```

```python
import functools
import math

import jax
import jax.numpy as jnp
from jax import lax
from jax.experimental import pallas as pl
from jax.experimental.pallas import tpu as pltpu
from jax.sharding import PartitionSpec as P

MESH = pl.DeviceIdType.MESH
MASKED = -1e30

QUERY_HEADS = 32
KEY_VALUE_HEADS = 4
HEAD_SIZE = 128
GROUP = 1024


adapter_scale = 2.0


def attention_kernel(
    ctx,
    devs,
    with_adapters,
    q_ref,
    do_ref,
    k_ref,
    v_ref,
    seg_ref,
    *refs,
):
    if with_adapters:
        x_ref, q_down_ref, v_down_ref, q_up_ref, v_up_ref = refs[:5]
        dq_ref, gk_ref, gv_ref, qd_out, qu_out, vd_out, vu_out = refs[5:12]
        refs = refs[12:]
    else:
        dq_ref, gk_ref, gv_ref = refs[:3]
        refs = refs[3:]
    kv_buf, part_send, part_recv, own_part, p_scr, w_scr, bias, g_send, g_recv, r_send, r_recv = (
        refs[:11]
    )
    if with_adapters:
        q_down, v_down, q_up, v_up, q_act = refs[11:16]
        q_bufs, v_bufs = refs[16:26], refs[26:]
    tok = k_ref.shape[1]
    kv_heads = k_ref.shape[2] // HEAD_SIZE
    repeat = q_ref.shape[2] // k_ref.shape[2]
    group_width = repeat * HEAD_SIZE
    mid = devs // 2
    scaling = HEAD_SIZE ** (-0.5)
    exponent = scaling * math.log2(math.e)
    me = lax.axis_index("ctx")
    p0 = lax.rem(me, devs)
    small = p0 // mid
    big = 1 - small
    ps = lax.rem(p0, mid)

    def ahead(d):
        return lax.rem(me + d, ctx)

    def behind(d):
        return lax.rem(me + ctx - d, ctx)

    for h in range(2):
        for g in range(kv_heads):
            lanes = slice(g * HEAD_SIZE, (g + 1) * HEAD_SIZE)
            kv_buf[h, 0, g, :, :HEAD_SIZE] = k_ref[h, :, lanes]
            kv_buf[h, 0, g, :, HEAD_SIZE:] = v_ref[h, :, lanes]

    barrier = pltpu.get_barrier_semaphore()
    for d in range(1, devs):
        pl.semaphore_signal(barrier, inc=1, device_id={"ctx": ahead(d)}, device_id_type=MESH)
        pl.semaphore_signal(barrier, inc=1, device_id={"ctx": behind(d)}, device_id_type=MESH)
    planes = ctx // devs
    plane = me // devs
    far = range(1, planes) if with_adapters else range(0)
    for j in far:
        pl.semaphore_signal(
            barrier,
            inc=1,
            device_id={"ctx": lax.rem(me + j * devs, ctx)},
            device_id_type=MESH,
        )
    pl.semaphore_wait(barrier, 2 * (devs - 1) + len(far))

    def gather_copy(h, d):
        return pltpu.make_async_remote_copy(
            src_ref=kv_buf.at[h, 0],
            dst_ref=kv_buf.at[h, d],
            send_sem=g_send.at[h, d],
            recv_sem=g_recv.at[h, d],
            device_id={"ctx": ahead(d)},
            device_id_type=MESH,
        )

    def return_copy(which, h, g, d):
        return pltpu.make_async_remote_copy(
            src_ref=part_send.at[which, h, g, d],
            dst_ref=part_recv.at[which, h, g, d],
            send_sem=r_send.at[which, h, g, d],
            recv_sem=r_recv.at[which, h, g, d],
            device_id={"ctx": behind(d)},
            device_id_type=MESH,
        )

    for d in range(1, mid):

        @pl.when(ps + d < mid)
        def _():
            gather_copy(small, d).start()

    for d in range(1, devs):

        @pl.when((ps + d >= mid) & (ps + d < devs))
        def _():
            gather_copy(small, d).start()

    for d in range(1, mid):

        @pl.when(ps + d < mid)
        def _():
            gather_copy(big, d).start()

    for d in range(1, mid):

        @pl.when(d > ps)
        def _():
            kv_buf[small, d] = jnp.zeros(kv_buf.shape[2:], kv_buf.dtype)

        @pl.when(d > ps)
        def _():
            kv_buf[big, mid + d] = jnp.zeros(kv_buf.shape[2:], kv_buf.dtype)

    own_ids = jnp.transpose(
        jnp.broadcast_to(seg_ref[pl.ds(me, 1), :].astype(jnp.float32), (tok, tok))
    )
    rows = lax.broadcasted_iota(jnp.int32, (tok, tok), 0)
    columns = lax.broadcasted_iota(jnp.int32, (tok, tok), 1)
    for d in range(devs):
        ids = seg_ref[pl.ds(behind(d), 1), :].astype(jnp.float32)
        block = jnp.where(own_ids == ids, 0.0, MASKED)
        if d == 0:
            block = jnp.where(columns <= rows, block, MASKED)
        bias[1, :, d * tok : (d + 1) * tok] = jnp.where(d <= ps + mid, block, MASKED)
        if d < mid:
            bias[0, :, d * tok : (d + 1) * tok] = jnp.where(d <= ps, block, MASKED)

    def within(j):
        return lax.rem(p0 + j, devs)

    def scatter_copy(bufs, j):
        part, landed, s_send, s_recv = bufs[0], bufs[1], bufs[4], bufs[5]
        return pltpu.make_async_remote_copy(
            src_ref=part.at[within(j)],
            dst_ref=landed.at[j],
            send_sem=s_send.at[j],
            recv_sem=s_recv.at[j],
            device_id={"ctx": plane * devs + within(j)},
            device_id_type=MESH,
        )

    def plane_copy(bufs, j):
        across, s_send, s_recv = bufs[2], bufs[6], bufs[7]
        return pltpu.make_async_remote_copy(
            src_ref=across.at[plane],
            dst_ref=across.at[plane],
            send_sem=s_send.at[j],
            recv_sem=s_recv.at[j],
            device_id={"ctx": lax.rem(me + j * devs, ctx)},
            device_id_type=MESH,
        )

    def spread_copy(bufs, j):
        whole, s_send, s_recv = bufs[3], bufs[8], bufs[9]
        return pltpu.make_async_remote_copy(
            src_ref=whole.at[p0],
            dst_ref=whole.at[p0],
            send_sem=s_send.at[j],
            recv_sem=s_recv.at[j],
            device_id={"ctx": plane * devs + within(j)},
            device_id_type=MESH,
        )

    def start_scatter(bufs):
        for j in range(1, devs):
            scatter_copy(bufs, j).start()

    def start_planes(bufs):
        total = bufs[0][p0].astype(jnp.float32)
        for j in range(1, devs):
            scatter_copy(bufs, j).wait_recv()
            total = total + bufs[1][j].astype(jnp.float32)
        bufs[2][plane] = total.astype(jnp.bfloat16)
        for j in range(1, planes):
            plane_copy(bufs, j).start()

    def start_spread(bufs):
        for j in range(1, planes):
            plane_copy(bufs, j).wait_recv()
        total = bufs[2][0].astype(jnp.float32)
        for j in range(1, planes):
            total = total + bufs[2][j].astype(jnp.float32)
        bufs[3][p0] = total.astype(jnp.bfloat16)
        for j in range(1, devs):
            spread_copy(bufs, j).start()

    def finish(bufs, down_out, up_out, up_pieces):
        for j in range(1, devs):
            spread_copy(bufs, j).wait_recv()
        width = down_out.shape[1] // devs
        up_width = 2 * up_out.shape[2] // up_pieces
        for p in range(devs):
            down_out[:, p * width : (p + 1) * width] = adapter_scale * bufs[3][
                p, :, :width
            ].astype(jnp.float32)
            if p < up_pieces:
                h, at = p // (up_pieces // 2), p % (up_pieces // 2)
                up_out[:, h, at * up_width : (at + 1) * up_width] = adapter_scale * bufs[3][
                    p, :, width:
                ].astype(jnp.float32)
        for j in range(1, devs):
            scatter_copy(bufs, j).wait_send()
            spread_copy(bufs, j).wait_send()
        for j in range(1, planes):
            plane_copy(bufs, j).wait_send()

    def project_down(bufs, act):
        width = x_ref.shape[1] // devs
        for p in range(devs):
            bufs[0][p, :, :width] = jnp.dot(
                act, x_ref[:, p * width : (p + 1) * width], preferred_element_type=jnp.float32
            ).astype(jnp.bfloat16)

    if with_adapters:
        for source, act in ((q_down_ref, q_down), (v_down_ref, v_down)):
            act[...] = lax.dot_general(
                source[...],
                x_ref[...],
                (((1,), (1,)), ((), ())),
                preferred_element_type=jnp.float32,
            ).astype(jnp.bfloat16)
        for h in range(2):
            q_up[h] = q_up_ref[:, h, :]
            v_up[h] = v_up_ref[:, h, :]
        q_act[...] = jnp.zeros_like(q_act)
        rank = q_act.shape[0]
        for p in range(2 * kv_heads, devs):
            v_bufs[0][p, :, x_ref.shape[1] // devs :] = jnp.zeros((rank, HEAD_SIZE), jnp.bfloat16)

    def stacked(ref, h, g):
        return jnp.concatenate(
            [
                ref[h, :, g * group_width + r * HEAD_SIZE : g * group_width + (r + 1) * HEAD_SIZE]
                for r in range(repeat)
            ],
            axis=0,
        )

    def send_parts(which, total, h, g, slots, limit):
        for d in range(slots):
            block = jnp.transpose(total[:, d * tok : (d + 1) * tok])
            if d == 0:
                own_part[which, h, g] = block
            else:
                part_send[which, h, g, d] = block.astype(jnp.bfloat16)
        for d in range(1, slots):

            @pl.when(d < limit)
            def _():
                return_copy(which, h, g, d).start()

    def probabilities(h, g, slots, limit):
        keys = slots * tok
        k = kv_buf[h, :slots, g, :, :HEAD_SIZE].reshape(keys, HEAD_SIZE)

        def one_head(r, inner):
            lanes = pl.ds(pl.multiple_of(g * group_width + r * HEAD_SIZE, HEAD_SIZE), HEAD_SIZE)
            at = pl.ds(pl.multiple_of(r * tok, tok), tok)
            s = lax.dot_general(
                q_ref[h, :, lanes],
                k,
                (((1,), (1,)), ((), ())),
                preferred_element_type=jnp.float32,
            )
            t = s * exponent + bias[int(slots == devs), :, :keys]
            e = jnp.exp2(t - jnp.max(t, axis=1, keepdims=True))
            w = e * (1.0 / jnp.sum(e, axis=1, keepdims=True))
            w_scr[g, at, :keys] = w
            p_scr[at, :keys] = w.astype(jnp.bfloat16)
            return inner

        lax.fori_loop(0, repeat, one_head, 0, unroll=8)
        dv = lax.dot_general(
            stacked(do_ref, h, g),
            p_scr[:, :keys],
            (((0,), (0,)), ((), ())),
            preferred_element_type=jnp.float32,
        )
        send_parts(1, dv, h, g, slots, limit)

    def score_gradients(h, g, slots, limit):
        keys = slots * tok
        k = kv_buf[h, :slots, g, :, :HEAD_SIZE].reshape(keys, HEAD_SIZE)
        v = kv_buf[h, :slots, g, :, HEAD_SIZE:].reshape(keys, HEAD_SIZE)

        def one_head(r, inner):
            lanes = pl.ds(pl.multiple_of(g * group_width + r * HEAD_SIZE, HEAD_SIZE), HEAD_SIZE)
            at = pl.ds(pl.multiple_of(r * tok, tok), tok)
            dp = lax.dot_general(
                do_ref[h, :, lanes],
                v,
                (((1,), (1,)), ((), ())),
                preferred_element_type=jnp.float32,
            )
            w = w_scr[g, at, :keys]
            low = w.astype(jnp.bfloat16).astype(jnp.float32)
            dot = jnp.sum(low * dp, axis=1, keepdims=True)
            ds = (w * (dp - dot)).astype(jnp.bfloat16)
            p_scr[at, :keys] = ds
            dq = jnp.dot(ds, k, preferred_element_type=jnp.float32) * scaling
            dq_ref[h, :, lanes] = dq.astype(jnp.bfloat16)
            return inner

        lax.fori_loop(0, repeat, one_head, 0, unroll=8)
        if with_adapters:
            lanes = slice(g * group_width, (g + 1) * group_width)
            dq_all = dq_ref[h, :, lanes]
            q_act[...] += lax.dot_general(
                q_up[h, :, lanes],
                dq_all,
                (((1,), (1,)), ((), ())),
                preferred_element_type=jnp.float32,
            )
            up = jnp.dot(q_down[...], dq_all, preferred_element_type=jnp.float32)
            up = up.astype(jnp.bfloat16)
            width = x_ref.shape[1] // devs
            each = group_width * 2 * kv_heads // devs
            pieces = group_width // each
            for i in range(pieces):
                q_bufs[0][(h * kv_heads + g) * pieces + i, :, width:] = up[
                    :, i * each : (i + 1) * each
                ]
        dk = lax.dot_general(
            stacked(q_ref, h, g),
            p_scr[:, :keys],
            (((0,), (0,)), ((), ())),
            preferred_element_type=jnp.float32,
        )
        send_parts(0, dk * scaling, h, g, slots, limit)

    def collect(which, out_ref):
        for d in range(1, devs):
            for g in range(kv_heads):

                @pl.when(ps + d < devs)
                def _():
                    return_copy(which, small, g, d).wait_recv()
                    own_part[which, small, g] += part_recv[which, small, g, d].astype(jnp.float32)

        for d in range(1, mid):
            for g in range(kv_heads):

                @pl.when(ps + d < mid)
                def _():
                    return_copy(which, big, g, d).wait_recv()
                    own_part[which, big, g] += part_recv[which, big, g, d].astype(jnp.float32)

        for h in range(2):
            for g in range(kv_heads):
                out_ref[h, :, g * HEAD_SIZE : (g + 1) * HEAD_SIZE] = own_part[which, h, g].astype(
                    jnp.bfloat16
                )

    def value_adapter():
        v_act = jnp.zeros(q_act.shape, jnp.float32)
        for h in range(2):
            v_act = v_act + lax.dot_general(
                v_up[h], gv_ref[h], (((1,), (1,)), ((), ())), preferred_element_type=jnp.float32
            )
            up = jnp.dot(v_down[...], gv_ref[h], preferred_element_type=jnp.float32)
            for g in range(kv_heads):
                v_bufs[0][h * kv_heads + g, :, x_ref.shape[1] // devs :] = up[
                    :, g * HEAD_SIZE : (g + 1) * HEAD_SIZE
                ].astype(jnp.bfloat16)
        project_down(v_bufs, v_act.astype(jnp.bfloat16))
        start_scatter(v_bufs)

    for d in range(1, mid):

        @pl.when(d <= ps)
        def _():
            gather_copy(small, d).wait_recv()

    for g in range(kv_heads):
        probabilities(small, g, mid, ps + 1)
    for g in range(kv_heads):
        score_gradients(small, g, mid, ps + 1)

    for d in range(1, devs):

        @pl.when(d <= ps + mid)
        def _():
            gather_copy(big, d).wait_recv()

    for g in range(kv_heads):
        probabilities(big, g, devs, ps + mid + 1)
    for g in range(kv_heads):
        score_gradients(big, g, devs, ps + mid + 1)
        if g == 0:
            collect(1, gv_ref)
            if with_adapters:
                value_adapter()

    if with_adapters:
        project_down(q_bufs, q_act[...].astype(jnp.bfloat16))
        start_scatter(q_bufs)
        start_planes(v_bufs)
        start_planes(q_bufs)
        start_spread(v_bufs)
        start_spread(q_bufs)
    collect(0, gk_ref)
    if with_adapters:
        finish(v_bufs, vd_out, vu_out, 2 * kv_heads)
        finish(q_bufs, qd_out, qu_out, devs)

    for d in range(1, devs):

        @pl.when(ps + d < devs)
        def _():
            gather_copy(small, d).wait_send()

        @pl.when(d <= ps + mid)
        def _():
            for which in range(2):
                for g in range(kv_heads):
                    return_copy(which, big, g, d).wait_send()

    for d in range(1, mid):

        @pl.when(ps + d < mid)
        def _():
            gather_copy(big, d).wait_send()

        @pl.when(d <= ps)
        def _():
            for which in range(2):
                for g in range(kv_heads):
                    return_copy(which, small, g, d).wait_send()


def attention_backward(q, do, k, v, seg, devs, adapters=None):
    tok, width = q.shape[1], q.shape[2]
    kv_heads = k.shape[2] // HEAD_SIZE
    repeat = width // k.shape[2]
    ctx = lax.axis_size("ctx")
    planes = ctx // devs
    bf16, f32 = jnp.bfloat16, jnp.float32
    vmem = pl.BlockSpec(memory_space=pltpu.VMEM)
    operands = (q, do, k, v, seg)
    results = [jax.ShapeDtypeStruct(a.shape, bf16) for a in (q, k, v)]
    scratch = [
        pltpu.VMEM((2, devs, kv_heads, tok, 2 * HEAD_SIZE), bf16),
        pltpu.VMEM((2, 2, kv_heads, devs, tok, HEAD_SIZE), bf16),
        pltpu.VMEM((2, 2, kv_heads, devs, tok, HEAD_SIZE), bf16),
        pltpu.VMEM((2, 2, kv_heads, tok, HEAD_SIZE), f32),
        pltpu.VMEM((repeat * tok, devs * tok), bf16),
        pltpu.VMEM((kv_heads, repeat * tok, devs * tok), f32),
        pltpu.VMEM((2, tok, devs * tok), f32),
        pltpu.SemaphoreType.DMA((2, devs)),
        pltpu.SemaphoreType.DMA((2, devs)),
        pltpu.SemaphoreType.DMA((2, 2, kv_heads, devs)),
        pltpu.SemaphoreType.DMA((2, 2, kv_heads, devs)),
    ]
    if adapters is not None:
        operands = operands + adapters
        x, q_down, v_down, q_up, v_up = adapters
        rank = q_down.shape[0]
        results += [jax.ShapeDtypeStruct(a.shape, f32) for a in (q_down, q_up, v_down, v_up)]
        scratch += [
            pltpu.VMEM((rank, tok), bf16),
            pltpu.VMEM((rank, tok), bf16),
            pltpu.VMEM((2, rank, q.shape[2]), bf16),
            pltpu.VMEM((2, rank, k.shape[2]), bf16),
            pltpu.VMEM((rank, tok), f32),
        ]
        for columns in ((x.shape[1] + 2 * width) // devs, x.shape[1] // devs + HEAD_SIZE):
            scratch += [
                pltpu.VMEM((n, rank, columns), bf16) for n in (devs, devs, planes, devs)
            ]
            scratch += [
                pltpu.SemaphoreType.DMA((n,)) for n in (devs, devs, planes, planes, devs, devs)
            ]
    return pl.pallas_call(
        functools.partial(attention_kernel, ctx, devs, adapters is not None),
        out_shape=tuple(results),
        in_specs=[vmem] * len(operands),
        out_specs=(vmem,) * len(results),
        scratch_shapes=scratch,
        compiler_params=pltpu.CompilerParams(
            collective_id=0, has_side_effects=True, vmem_limit_bytes=52 * 1024 * 1024
        ),
        name="attention_backward",
    )(*operands)


def paired_kernel(
    chips,
    span,
    q_hbm,
    do_hbm,
    k_hbm,
    v_hbm,
    seg_hbm,
    x_ref,
    q_down_hbm,
    v_down_hbm,
    q_up_hbm,
    v_up_hbm,
    dq_out,
    gk_out,
    gv_out,
    qd_out,
    qu_out,
    vd_out,
    vu_out,
    q_raw,
    do_raw,
    k_raw,
    v_raw,
    seg_ref,
    q_down_ref,
    v_down_ref,
    q_up_ref,
    v_up_ref,
    q_away,
    do_away,
    k_ref,
    v_ref,
    dq_land,
    qb,
    dob,
    kb,
    vb,
    xb,
    dqb,
    p_small,
    p_big,
    bias,
    part_send,
    part_recv,
    acc,
    sib_part,
    down_mine,
    down_theirs,
    act_mine,
    act_theirs,
    mixed_mine,
    mixed_theirs,
    acts,
    q_parts,
    q_land,
    q_across,
    q_sums,
    q_other,
    v_parts,
    v_land,
    v_across,
    v_sums,
    v_other,
    local_sem,
    swap_send,
    swap_recv,
    g_send,
    g_recv,
    r_send,
    r_recv,
    a_send,
    a_recv,
):
    bf16, f32 = jnp.bfloat16, jnp.float32
    tok = q_raw.shape[0]
    pair = 2 * tok
    width = qb.shape[2]
    heads = width // HEAD_SIZE
    columns = xb.shape[1]
    cube = q_parts.shape[0]
    cubes = chips // cube
    each = columns // cube
    up_each = 2 * width // cube
    rank = acts.shape[1]
    mid = span // 2
    scaling = HEAD_SIZE ** (-0.5)
    exponent = scaling * math.log2(math.e)
    me = lax.axis_index("ctx")
    chip = me // 2
    core = lax.rem(me, 2)
    spot = lax.rem(chip, cube)
    mine = chip // cube
    other = 1 - core
    place = lax.rem(chip, span)
    small = place // mid
    big = 1 - small
    ps = lax.rem(place, mid)

    def ahead(d):
        return lax.rem(chip + d, chips)

    def behind(d):
        return lax.rem(chip + chips - d, chips)

    def within(j):
        return lax.rem(spot + j, cube)

    def device(chip_at, core_at):
        return {"ctx": 2 * chip_at + core_at}

    sibling = device(chip, other)

    def rows(at):
        return pl.ds(pl.multiple_of(at * tok, tok), tok)

    def half_columns(at, size):
        return pl.ds(pl.multiple_of(at * size, size), size)

    barrier = pltpu.get_barrier_semaphore()
    pl.semaphore_signal(barrier, inc=1, device_id=sibling, device_id_type=MESH)
    for j in range(1, cube):
        pl.semaphore_signal(
            barrier, inc=1, device_id=device(mine * cube + within(j), core), device_id_type=MESH
        )
    for j in range(1, cubes):
        pl.semaphore_signal(
            barrier, inc=1, device_id=device(ahead(j * cube), core), device_id_type=MESH
        )
    for d in range(1, span):
        for to in range(2):
            pl.semaphore_signal(
                barrier, inc=1, device_id=device(ahead(d), to), device_id_type=MESH
            )
            pl.semaphore_signal(
                barrier, inc=1, device_id=device(behind(d), to), device_id_type=MESH
            )

    staged = [
        pltpu.make_async_copy(src, dst, local_sem.at[i])
        for i, (src, dst) in enumerate(
            (
                (k_hbm, k_raw),
                (v_hbm, v_raw),
                (q_hbm, q_raw),
                (do_hbm, do_raw),
                (seg_hbm, seg_ref),
                (x_ref.at[:, half_columns(core, columns)], xb.at[rows(core)]),
                (q_down_hbm, q_down_ref),
                (v_down_hbm, v_down_ref),
                (q_up_hbm, q_up_ref),
                (v_up_hbm, v_up_ref),
            )
        )
    ]
    for copy in staged:
        copy.start()

    def swap_columns(row):
        return pltpu.make_async_remote_copy(
            src_ref=x_ref.at[:, half_columns(other, columns)],
            dst_ref=xb.at[rows(row)],
            send_sem=swap_send.at[4],
            recv_sem=swap_recv.at[4],
            device_id=sibling,
            device_id_type=MESH,
        )

    def swap_half(h, i, row):
        return pltpu.make_async_remote_copy(
            src_ref=(q_away, do_away)[i].at[h],
            dst_ref=(qb, dob)[i].at[h, rows(row)],
            send_sem=swap_send.at[2 * h + i],
            recv_sem=swap_recv.at[2 * h + i],
            device_id=sibling,
            device_id_type=MESH,
        )

    def gather_copy(which, h, d, to, row):
        src = (k_ref, v_ref)[which].at[h, :, half_columns(to, HEAD_SIZE)]
        return pltpu.make_async_remote_copy(
            src_ref=src,
            dst_ref=(kb, vb)[which].at[h, d, rows(row)],
            send_sem=g_send.at[which, h, d, to],
            recv_sem=g_recv.at[which, h, d, row],
            device_id=device(ahead(d), to),
            device_id_type=MESH,
        )

    def gather_start(which, h, d):
        for to in range(2):
            gather_copy(which, h, d, to, core).start()

    def gather_wait(which, h, d):
        for row in range(2):
            gather_copy(which, h, d, row, row).wait_recv()

    def gather_sent(which, h, d):
        for to in range(2):
            gather_copy(which, h, d, to, core).wait_send()

    @pl.when(ps == 0)
    def _():
        for buf in (kb, vb):
            buf[small, 1] = jnp.zeros(buf.shape[2:], bf16)
            buf[big, span - 1] = jnp.zeros(buf.shape[2:], bf16)

    to_row = lax.broadcasted_iota(jnp.int32, (pair, pair), 0)
    from_row = lax.broadcasted_iota(jnp.int32, (pair, pair), 1)
    parting = jnp.where(from_row == 2 * lax.rem(to_row, tok) + to_row // tok, 1.0, 0.0).astype(bf16)

    def parted(raw, lanes):
        return jnp.dot(
            parting, raw[:, :, lanes].reshape(pair, HEAD_SIZE), preferred_element_type=f32
        ).astype(bf16)

    for i, (raw, ref, buf) in enumerate(((k_raw, k_ref, kb), (v_raw, v_ref, vb))):
        staged[i].wait()
        for head in range(2):
            lanes = slice(head * HEAD_SIZE, (head + 1) * HEAD_SIZE)
            both = parted(raw, lanes)
            for h in range(2):
                ref[h, :, lanes] = both[h * tok : (h + 1) * tok]
        for h in range(2):
            buf[h, 0, rows(core)] = ref[h, :, half_columns(core, HEAD_SIZE)]
    def part_rows(i):
        raw, buf, away = ((q_raw, qb, q_away), (do_raw, dob, do_away))[i]
        staged[2 + i].wait()
        for j in range(heads):
            lanes = slice(j * HEAD_SIZE, (j + 1) * HEAD_SIZE)
            for at in (other, core):
                start = pl.multiple_of(at * width + j * HEAD_SIZE, HEAD_SIZE)
                both = parted(raw, pl.ds(start, HEAD_SIZE))
                for h in range(2):
                    block = both[h * tok : (h + 1) * tok]
                    if at is core:
                        buf[h, rows(core), lanes] = block
                    else:
                        away[h, :, lanes] = block

    part_rows(0)

    pl.semaphore_wait(barrier, cube + cubes - 1 + 4 * (span - 1))

    def gather_all(which):
        for d in range(1, mid):

            @pl.when(ps + d < mid)
            def _():
                gather_start(which, small, d)

        for d in range(1, span):

            @pl.when((ps + d >= mid) & (ps + d < span))
            def _():
                gather_start(which, small, d)

        for d in range(1, mid):

            @pl.when(ps + d < mid)
            def _():
                gather_start(which, big, d)

    gather_all(0)
    gather_copy(0, small, 0, other, core).start()
    swap_half(small, 0, core).start()
    gather_copy(0, big, 0, other, core).start()
    swap_half(big, 0, core).start()
    gather_all(1)
    part_rows(1)
    for h in (small, big):
        swap_half(h, 1, core).start()
        gather_copy(1, h, 0, other, core).start()
    swap_columns(core).start()

    staged[4].wait()

    def chip_ids(at):
        first = seg_ref[pl.ds(2 * at, 1), :]
        second = seg_ref[pl.ds(2 * at + 1, 1), :]
        return jnp.concatenate([first, second], axis=1).astype(f32)

    own_ids = jnp.transpose(jnp.broadcast_to(chip_ids(chip), (pair, pair)))
    row = lax.broadcasted_iota(jnp.int32, (pair, pair), 0)
    column = lax.broadcasted_iota(jnp.int32, (pair, pair), 1)
    for d in range(span):
        block = jnp.where(own_ids == chip_ids(behind(d)), 0.0, MASKED)
        if d == 0:
            block = jnp.where(column <= row, block, MASKED)
        bias[1, :, d * pair : (d + 1) * pair] = jnp.where(d <= ps + mid, block, MASKED)
        if d < mid:
            bias[0, :, d * pair : (d + 1) * pair] = jnp.where(d <= ps, block, MASKED)

    def exchange(src, dst, i):
        return pltpu.make_async_remote_copy(
            src_ref=src,
            dst_ref=dst,
            send_sem=swap_send.at[i],
            recv_sem=swap_recv.at[i],
            device_id=sibling,
            device_id_type=MESH,
        )

    down_swap = exchange(down_mine, down_theirs, 5)
    act_swap = exchange(act_mine, act_theirs, 6)
    mixed_swap = exchange(mixed_mine, mixed_theirs, 7)

    def part_swap(which, h):
        return pltpu.make_async_remote_copy(
            src_ref=sib_part.at[which, h],
            dst_ref=acc.at[which, h, core],
            send_sem=swap_send.at[8 + 2 * which + h],
            recv_sem=swap_recv.at[8 + 2 * which + h],
            device_id=sibling,
            device_id_type=MESH,
        )

    def part_wait(which, h):
        return pltpu.make_async_remote_copy(
            src_ref=sib_part.at[which, h],
            dst_ref=acc.at[which, h, other],
            send_sem=swap_send.at[8 + 2 * which + h],
            recv_sem=swap_recv.at[8 + 2 * which + h],
            device_id=sibling,
            device_id_type=MESH,
        )

    def dq_swap(h):
        return exchange(dqb.at[h, rows(other)], dq_land.at[h], 12 + h)

    def scatter_copy(bufs, j):
        s, parts, land = bufs[:3]
        return pltpu.make_async_remote_copy(
            src_ref=parts.at[within(j)],
            dst_ref=land.at[j],
            send_sem=a_send.at[3 * s, j],
            recv_sem=a_recv.at[3 * s, j],
            device_id=device(mine * cube + within(j), core),
            device_id_type=MESH,
        )

    def across_copy(bufs, j, source):
        s, across = bufs[0], bufs[3]
        return pltpu.make_async_remote_copy(
            src_ref=across.at[source],
            dst_ref=across.at[source],
            send_sem=a_send.at[3 * s + 1, j],
            recv_sem=a_recv.at[3 * s + 1, j],
            device_id=device(ahead(j * cube), core),
            device_id_type=MESH,
        )

    def spread_copy(bufs, j, source):
        s, sums = bufs[0], bufs[4]
        return pltpu.make_async_remote_copy(
            src_ref=sums.at[source],
            dst_ref=sums.at[source],
            send_sem=a_send.at[3 * s + 2, j],
            recv_sem=a_recv.at[3 * s + 2, j],
            device_id=device(mine * cube + within(j), core),
            device_id_type=MESH,
        )

    q_set = (0, q_parts, q_land, q_across, q_sums, q_other)
    v_set = (1, v_parts, v_land, v_across, v_sums, v_other)

    def start_scatter(bufs):
        for j in range(1, cube):
            scatter_copy(bufs, j).start()

    def start_across(bufs):
        total = bufs[1][spot].astype(f32)
        for j in range(1, cube):
            scatter_copy(bufs, j).wait_recv()
            total = total + bufs[2][j].astype(f32)
        bufs[3][mine] = total.astype(bf16)
        for j in range(1, cubes):
            across_copy(bufs, j, mine).start()

    def start_spread(bufs):
        for j in range(1, cubes):
            across_copy(bufs, j, lax.rem(mine + cubes - j, cubes)).wait_recv()
        total = bufs[3][0].astype(f32)
        for j in range(1, cubes):
            total = total + bufs[3][j].astype(f32)
        bufs[4][spot] = total.astype(bf16)
        for j in range(1, cube):
            spread_copy(bufs, j, spot).start()

    def hand_copy(bufs):
        return exchange(bufs[4], bufs[5], 14 + bufs[0])

    def start_hand(bufs):
        for j in range(1, cube):
            spread_copy(bufs, j, lax.rem(spot + cube - j, cube)).wait_recv()
        hand_copy(bufs).start()

    def finish(bufs, down_out, up_out, up_width, up_pieces):
        def write(source, at):
            for i in range(cube):
                lanes = pl.ds(pl.multiple_of(at * columns + i * each, each), each)
                down_out[:, lanes] = adapter_scale * source[i, :, :each].astype(f32)
                if i < up_pieces:
                    h, step = i // (up_pieces // 2), i % (up_pieces // 2)
                    size = up_width // (up_pieces // 2)
                    lanes = pl.ds(pl.multiple_of(at * up_width + step * size, size), size)
                    up_out[:, h, lanes] = adapter_scale * source[i, :, each:].astype(f32)

        write(bufs[4], core)
        hand_copy(bufs).wait_recv()
        write(bufs[5], other)
        for j in range(1, cube):
            scatter_copy(bufs, j).wait_send()
            spread_copy(bufs, j, spot).wait_send()
        for j in range(1, cubes):
            across_copy(bufs, j, mine).wait_send()
        hand_copy(bufs).wait_send()

    def project_down(parts, act):
        for i in range(cube):
            parts[i, :, :each] = jnp.dot(
                act, xb[:, i * each : (i + 1) * each], preferred_element_type=f32
            ).astype(bf16)

    def return_copy(which, h, d, to, head):
        return pltpu.make_async_remote_copy(
            src_ref=part_send.at[which, h, d, rows(to)],
            dst_ref=part_recv.at[which, h, d, head],
            send_sem=r_send.at[which, h, d, to],
            recv_sem=r_recv.at[which, h, d, head],
            device_id=device(behind(d), to),
            device_id_type=MESH,
        )

    def send_parts(which, total, h, slots, limit):
        for d in reversed(range(slots)):
            block = jnp.transpose(total[:, d * pair : (d + 1) * pair])
            if d == 0:
                acc[which, h, core] = jnp.where(core == 0, block[:tok], block[tok:])
                sib_part[which, h] = jnp.where(core == 0, block[tok:], block[:tok])
                part_swap(which, h).start()
            else:
                part_send[which, h, d] = block.astype(bf16)

                @pl.when(d < limit)
                def _():
                    for to in range(2):
                        return_copy(which, h, d, to, core).start()

    def stacked(ref, h):
        return jnp.concatenate(
            [ref[h, :, j * HEAD_SIZE : (j + 1) * HEAD_SIZE] for j in range(heads)], axis=0
        )

    def head_lanes(j):
        return pl.ds(pl.multiple_of(j * HEAD_SIZE, HEAD_SIZE), HEAD_SIZE)

    def head_rows(j):
        return pl.ds(pl.multiple_of(j * pair, pair), pair)

    def probabilities(h, p_ref, slots, limit):
        keys = slots * pair
        k = kb[h, :slots].reshape(keys, HEAD_SIZE)

        def one_head(j, inner):
            s = lax.dot_general(
                qb[h, :, head_lanes(j)], k, (((1,), (1,)), ((), ())), preferred_element_type=f32
            )
            t = s * exponent + bias[int(slots == span), :, :keys]
            e = jnp.exp2(t - jnp.max(t, axis=1, keepdims=True))
            w = e * (1.0 / jnp.sum(e, axis=1, keepdims=True))
            p_ref[head_rows(j)] = w.astype(bf16)
            return inner

        lax.fori_loop(0, heads, one_head, 0, unroll=heads)

    def value_part(h, p_ref, slots, limit):
        dv = lax.dot_general(
            stacked(dob, h), p_ref[...], (((0,), (0,)), ((), ())), preferred_element_type=f32
        )
        send_parts(1, dv, h, slots, limit)

    def score_gradients(h, p_ref, slots, first, last):
        keys = slots * pair
        k = kb[h, :slots].reshape(keys, HEAD_SIZE)
        v = vb[h, :slots].reshape(keys, HEAD_SIZE)

        def scores_of(j):
            dp = lax.dot_general(
                dob[h, :, head_lanes(j)], v, (((1,), (1,)), ((), ())), preferred_element_type=f32
            )
            w = p_ref[head_rows(j)].astype(f32)
            dot = jnp.sum(w * dp, axis=1, keepdims=True)
            p_ref[head_rows(j)] = (w * (dp - dot)).astype(bf16)

        def queries_of(j):
            dq = jnp.dot(p_ref[head_rows(j)], k, preferred_element_type=f32) * scaling
            dqb[h, :, head_lanes(j)] = dq.astype(bf16)

        def one_head(j, inner):
            scores_of(j)
            queries_of(j - 1)
            return inner

        scores_of(first)
        lax.fori_loop(first + 1, last, one_head, 0, unroll=last - first - 1)
        queries_of(last - 1)
        if last == heads:
            dq_swap(h).start()

    def query_adapter(h):
        dq = dqb[h]
        up_rows = q_up_ref[:, h, half_columns(core, width)]
        up = jnp.dot(acts[0], dq, preferred_element_type=f32).astype(bf16)
        return lax.dot_general(
            up_rows, dq, (((1,), (1,)), ((), ())), preferred_element_type=f32
        ), up

    def key_part(h, p_ref, slots, limit):
        dk = lax.dot_general(
            stacked(qb, h), p_ref[...], (((0,), (0,)), ((), ())), preferred_element_type=f32
        )
        send_parts(0, dk * scaling, h, slots, limit)

    def collect(which):
        for h in range(2):
            part_wait(which, h).wait_recv()
        for d in range(1, span):

            @pl.when(ps + d < span)
            def _():
                for head in range(2):
                    return_copy(which, small, d, head, head).wait_recv()
                    acc[which, small, head] += part_recv[which, small, d, head].astype(f32)

        for d in range(1, mid):

            @pl.when(ps + d < mid)
            def _():
                for head in range(2):
                    return_copy(which, big, d, head, head).wait_recv()
                    acc[which, big, head] += part_recv[which, big, d, head].astype(f32)

        return [
            jnp.concatenate([acc[which, h, 0], acc[which, h, 1]], axis=1).astype(bf16)
            for h in range(2)
        ]

    def wait_swap(h, i):
        swap_half(h, i, other).wait_recv()

    wait_swap(small, 0)
    gather_copy(0, small, 0, other, other).wait_recv()
    for d in range(1, mid):

        @pl.when(d <= ps)
        def _():
            gather_wait(0, small, d)

    probabilities(small, p_small, mid, ps + 1)
    wait_swap(small, 1)
    value_part(small, p_small, mid, ps + 1)

    for i in range(5, 10):
        staged[i].wait()
    swap_columns(other).wait_recv()
    for i, source in enumerate((q_down_ref, v_down_ref)):
        down_mine[i] = lax.dot_general(
            source[:, half_columns(core, columns)],
            xb[...],
            (((1,), (1,)), ((), ())),
            preferred_element_type=f32,
        )
    down_swap.start()

    wait_swap(big, 0)
    gather_copy(0, big, 0, other, other).wait_recv()
    for d in range(1, span):

        @pl.when(d <= ps + mid)
        def _():
            gather_wait(0, big, d)

    probabilities(big, p_big, span, ps + mid + 1)
    wait_swap(big, 1)
    value_part(big, p_big, span, ps + mid + 1)

    down_swap.wait()
    for i in range(2):
        acts[i] = (down_mine[i] + down_theirs[i]).astype(bf16)

    for h in (small, big):
        gather_copy(1, h, 0, other, other).wait_recv()
    for d in range(1, mid):

        @pl.when(d <= ps)
        def _():
            gather_wait(1, small, d)

    for d in range(1, span):

        @pl.when(d <= ps + mid)
        def _():
            gather_wait(1, big, d)

    score_gradients(small, p_small, mid, 0, heads)
    score_gradients(big, p_big, span, 0, heads // 2)

    gv = collect(1)
    v_act = jnp.zeros((rank, tok), f32)
    own_lanes = half_columns(core, tok)
    for h in range(2):
        v_act = v_act + lax.dot_general(
            v_up_ref[:, h, :], gv[h], (((1,), (1,)), ((), ())), preferred_element_type=f32
        )
        up = jnp.dot(acts[1, :, own_lanes], gv[h], preferred_element_type=f32)
        first, second = up[:, :HEAD_SIZE], up[:, HEAD_SIZE:]
        mixed_mine[1 + h] = jnp.where(core == 0, second, first)
        mixed_mine[3 + h] = jnp.where(core == 0, first, second)
    mixed_mine[0] = v_act
    mixed_swap.start()
    for h in range(2):
        gv_out[:, h, :] = gv[h]

    score_gradients(big, p_big, span, heads // 2, 3 * heads // 4)

    mixed_swap.wait()
    acts[2, :, own_lanes] = mixed_mine[0].astype(bf16)
    acts[2, :, half_columns(other, tok)] = mixed_theirs[0].astype(bf16)
    for i in range(cube):
        if i < 2:
            v_parts[i, :, each:] = (mixed_mine[3 + i] + mixed_theirs[1 + i]).astype(bf16)
        else:
            v_parts[i, :, each:] = jnp.zeros((rank, HEAD_SIZE), bf16)
    project_down(v_parts, acts[2])
    start_scatter(v_set)

    score_gradients(big, p_big, span, 3 * heads // 4, heads)

    act = jnp.zeros((rank, pair), f32)
    for h in range(2):
        more, up = query_adapter(h)
        act = act + more
        for i in range(cube // 2):
            q_parts[h * (cube // 2) + i, :, each:] = up[:, i * up_each : (i + 1) * up_each]
    act_mine[...] = act
    act_swap.start()
    act_swap.wait()
    project_down(q_parts, (act_mine[...] + act_theirs[...]).astype(bf16))
    start_scatter(q_set)

    key_part(big, p_big, span, ps + mid + 1)
    key_part(small, p_small, mid, ps + 1)

    start_across(v_set)
    start_across(q_set)
    start_spread(v_set)
    start_spread(q_set)
    gk = collect(0)
    for h in range(2):
        gk_out[:, h, :] = gk[h]
    for h in range(2):
        dq_out[:, h, half_columns(core, width)] = dqb[h, rows(core)]
        dq_swap(h).wait_recv()
        dq_out[:, h, half_columns(other, width)] = dq_land[h]
    start_hand(v_set)
    start_hand(q_set)
    finish(v_set, vd_out, vu_out, HEAD_SIZE, 2)
    finish(q_set, qd_out, qu_out, width, cube)

    for h in range(2):
        dq_swap(h).wait_send()
        for i in range(2):
            swap_half(h, i, core).wait_send()
            part_swap(i, h).wait_send()
            gather_copy(i, h, 0, other, core).wait_send()
    swap_columns(core).wait_send()
    for which in range(2):
        for d in range(1, span):

            @pl.when(ps + d < span)
            def _():
                gather_sent(which, small, d)

            @pl.when(d <= ps + mid)
            def _():
                for to in range(2):
                    return_copy(which, big, d, to, core).wait_send()

        for d in range(1, mid):

            @pl.when(ps + d < mid)
            def _():
                gather_sent(which, big, d)

            @pl.when(d <= ps)
            def _():
                for to in range(2):
                    return_copy(which, small, d, to, core).wait_send()


def deliver_kernel(*refs):
    count = (len(refs) - 1) // 2
    copies = [
        pltpu.make_async_copy(refs[i], refs[count + i], refs[-1].at[i]) for i in range(count)
    ]
    for copy in copies:
        copy.start()
    for copy in copies:
        copy.wait()


def deliver(arrays):
    vmem = pl.BlockSpec(memory_space=pltpu.VMEM)
    hbm = pl.BlockSpec(memory_space=pltpu.MemorySpace.HBM)
    return pl.pallas_call(
        deliver_kernel,
        out_shape=tuple(jax.ShapeDtypeStruct(a.shape, a.dtype) for a in arrays),
        in_specs=[vmem] * len(arrays),
        out_specs=(hbm,) * len(arrays),
        scratch_shapes=[pltpu.SemaphoreType.DMA((len(arrays),))],
        name="deliver",
    )(*arrays)


def paired_backward(q, do, k, v, seg, x, q_down, v_down, q_up, v_up, span):
    tok, width = q.shape[0], q.shape[2] // 2
    pair = 2 * tok
    heads = width // HEAD_SIZE
    chips = lax.axis_size("ctx") // 2
    rank = q_down.shape[0]
    columns = x.shape[1] // 2
    bf16, f32 = jnp.bfloat16, jnp.float32
    vmem = pl.BlockSpec(memory_space=pltpu.VMEM)
    hbm = pl.BlockSpec(memory_space=pltpu.MemorySpace.HBM)
    cube = 2 * span
    q_piece = columns // cube + 2 * width // cube
    v_piece = columns // cube + HEAD_SIZE
    scratch = [pltpu.VMEM(a.shape, a.dtype) for a in (q, do, k, v, seg, q_down, v_down, q_up, v_up)]
    scratch += [
        pltpu.VMEM((2, tok, width), bf16),
        pltpu.VMEM((2, tok, width), bf16),
        pltpu.VMEM((2, tok, 2 * HEAD_SIZE), bf16),
        pltpu.VMEM((2, tok, 2 * HEAD_SIZE), bf16),
        pltpu.VMEM((2, tok, width), bf16),
        pltpu.VMEM((2, pair, width), bf16),
        pltpu.VMEM((2, pair, width), bf16),
        pltpu.VMEM((2, span, pair, HEAD_SIZE), bf16),
        pltpu.VMEM((2, span, pair, HEAD_SIZE), bf16),
        pltpu.VMEM((pair, columns), bf16),
        pltpu.VMEM((2, pair, width), bf16),
        pltpu.VMEM((heads * pair, span // 2 * pair), bf16),
        pltpu.VMEM((heads * pair, span * pair), bf16),
        pltpu.VMEM((2, pair, span * pair), f32),
        pltpu.VMEM((2, 2, span, pair, HEAD_SIZE), bf16),
        pltpu.VMEM((2, 2, span, 2, tok, HEAD_SIZE), bf16),
        pltpu.VMEM((2, 2, 2, tok, HEAD_SIZE), f32),
        pltpu.VMEM((2, 2, tok, HEAD_SIZE), f32),
        pltpu.VMEM((2, rank, pair), f32),
        pltpu.VMEM((2, rank, pair), f32),
        pltpu.VMEM((rank, pair), f32),
        pltpu.VMEM((rank, pair), f32),
        pltpu.VMEM((5, rank, HEAD_SIZE), f32),
        pltpu.VMEM((5, rank, HEAD_SIZE), f32),
        pltpu.VMEM((3, rank, pair), bf16),
    ]
    for piece in (q_piece, v_piece):
        scratch += [
            pltpu.VMEM((n, rank, piece), bf16) for n in (cube, cube, chips // cube, cube, cube)
        ]
    scratch += [
        pltpu.SemaphoreType.DMA((10,)),
        pltpu.SemaphoreType.DMA((16,)),
        pltpu.SemaphoreType.DMA((16,)),
    ]
    scratch += [pltpu.SemaphoreType.DMA((2, 2, span, 2)) for _ in range(4)]
    scratch += [pltpu.SemaphoreType.DMA((6, max(cube, chips // cube))) for _ in range(2)]
    return pl.pallas_call(
        functools.partial(paired_kernel, chips, span),
        out_shape=tuple(
            [jax.ShapeDtypeStruct(a.shape, bf16) for a in (q, k, v)]
            + [jax.ShapeDtypeStruct(a.shape, f32) for a in (q_down, q_up, v_down, v_up)]
        ),
        in_specs=[hbm] * 10,
        out_specs=(vmem,) * 7,
        scratch_shapes=scratch,
        compiler_params=pltpu.CompilerParams(
            collective_id=1, has_side_effects=True, vmem_limit_bytes=61 * 1024 * 1024
        ),
        name="paired_backward",
    )(q, do, k, v, seg, x, q_down, v_down, q_up, v_up)


def on_device(
    projected_queries,
    projected_keys,
    projected_values,
    output_gradient,
    normed_layer_input,
    segment,
    query_adapter_down,
    query_adapter_up,
    value_adapter_down,
    value_adapter_up,
):
    tok_rows = projected_queries.shape[0]
    query_width = projected_queries.shape[2]
    key_width = projected_keys.shape[2]
    key_value_heads = key_width // HEAD_SIZE
    group_devs = GROUP // tok_rows
    ctx = lax.axis_size("ctx")
    paired = (
        lax.axis_size("fsdp") == 1
        and group_devs % 4 == 0
        and ctx % (2 * group_devs) == 0
        and key_value_heads == 2
        and tok_rows == HEAD_SIZE
        and query_width % (ctx * HEAD_SIZE // 2) == 0
        and normed_layer_input.shape[1] % (ctx * HEAD_SIZE) == 0
    )
    if paired:
        return deliver(
            paired_backward(
                projected_queries,
                output_gradient,
                projected_keys,
                projected_values,
                segment.reshape(-1, tok_rows),
                normed_layer_input,
                query_adapter_down,
                value_adapter_down,
                query_adapter_up,
                value_adapter_up,
                group_devs // 2,
            )
        )
    query_grad, key_grad, value_grad = attention_backward(
        projected_queries.transpose(1, 0, 2),
        output_gradient.transpose(1, 0, 2),
        projected_keys.transpose(1, 0, 2),
        projected_values.transpose(1, 0, 2),
        segment.reshape(-1, tok_rows),
        group_devs,
    )
    grad_query = query_grad.transpose(1, 0, 2)
    grad_key = key_grad.transpose(1, 0, 2)
    grad_value = value_grad.transpose(1, 0, 2)
    adapter_input = lax.psum(
        (
            jnp.dot(normed_layer_input, query_adapter_down.T, preferred_element_type=jnp.float32),
            jnp.dot(normed_layer_input, value_adapter_down.T, preferred_element_type=jnp.float32),
        ),
        "fsdp",
    )
    query_down_part = adapter_input[0].astype(jnp.bfloat16)
    value_down_part = adapter_input[1].astype(jnp.bfloat16)
    query_flattened_rows = grad_query.reshape(tok_rows, -1)
    value_flattened_rows = grad_value.reshape(tok_rows, -1)
    adapter_rank_rows = query_adapter_up.shape[0]
    adapter_output = lax.psum(
        (
            jnp.dot(
                query_flattened_rows,
                query_adapter_up.reshape(adapter_rank_rows, -1).T,
                preferred_element_type=jnp.float32,
            ),
            jnp.dot(
                value_flattened_rows,
                value_adapter_up.reshape(adapter_rank_rows, -1).T,
                preferred_element_type=jnp.float32,
            ),
        ),
        "fsdp",
    )
    query_up_part = adapter_output[0].astype(jnp.bfloat16)
    value_up_part = adapter_output[1].astype(jnp.bfloat16)
    local_down_query = jnp.dot(
        query_up_part.T, normed_layer_input, preferred_element_type=jnp.float32
    )
    local_up_query = jnp.dot(
        query_down_part.T, query_flattened_rows, preferred_element_type=jnp.float32
    ).reshape(adapter_rank_rows, 2, -1)
    local_down_value = jnp.dot(
        value_up_part.T, normed_layer_input, preferred_element_type=jnp.float32
    )
    local_up_value = jnp.dot(
        value_down_part.T, value_flattened_rows, preferred_element_type=jnp.float32
    ).reshape(adapter_rank_rows, 2, -1)
    gradient_totals = lax.psum(
        (local_down_query, local_up_query, local_down_value, local_up_value), "ctx"
    )
    return (
        grad_query,
        grad_key,
        grad_value,
        adapter_scale * gradient_totals[0],
        adapter_scale * gradient_totals[1],
        adapter_scale * gradient_totals[2],
        adapter_scale * gradient_totals[3],
    )


def solution(mesh):
    in_specs = (
        P(("rep", "ctx"), None, "fsdp"),
        P(("rep", "ctx"), None, "fsdp"),
        P(("rep", "ctx"), None, "fsdp"),
        P(("rep", "ctx"), None, "fsdp"),
        P(("rep", "ctx"), "fsdp"),
        P("rep"),
        P(None, "fsdp"),
        P(None, None, "fsdp"),
        P(None, "fsdp"),
        P(None, None, "fsdp"),
    )
    out_specs = (
        P(("rep", "ctx"), None, "fsdp"),
        P(("rep", "ctx"), None, "fsdp"),
        P(("rep", "ctx"), None, "fsdp"),
        P("rep", "fsdp"),
        P("rep", None, "fsdp"),
        P("rep", "fsdp"),
        P("rep", None, "fsdp"),
    )
    return jax.shard_map(
        on_device, mesh=mesh, in_specs=in_specs, out_specs=out_specs, check_vma=False
    )
```

```python
import functools
import math

import jax
import jax.numpy as jnp
from jax import lax
from jax.experimental import pallas as pl
from jax.experimental.pallas import tpu as pltpu
from jax.sharding import PartitionSpec as P

MESH = pl.DeviceIdType.MESH
MASKED = -1e30

QUERY_HEADS = 32
KEY_VALUE_HEADS = 4
HEAD_SIZE = 128
GROUP = 1024


adapter_scale = 2.0


def attention_kernel(
    ctx,
    devs,
    with_adapters,
    q_ref,
    do_ref,
    k_ref,
    v_ref,
    seg_ref,
    *refs,
):
    if with_adapters:
        x_ref, q_down_ref, v_down_ref, q_up_ref, v_up_ref = refs[:5]
        dq_ref, gk_ref, gv_ref, qd_out, qu_out, vd_out, vu_out = refs[5:12]
        refs = refs[12:]
    else:
        dq_ref, gk_ref, gv_ref = refs[:3]
        refs = refs[3:]
    kv_buf, part_send, part_recv, own_part, p_scr, w_scr, bias, g_send, g_recv, r_send, r_recv = (
        refs[:11]
    )
    if with_adapters:
        q_down, v_down, q_up, v_up, q_act = refs[11:16]
        q_bufs, v_bufs = refs[16:26], refs[26:]
    tok = k_ref.shape[1]
    kv_heads = k_ref.shape[2] // HEAD_SIZE
    repeat = q_ref.shape[2] // k_ref.shape[2]
    group_width = repeat * HEAD_SIZE
    mid = devs // 2
    scaling = HEAD_SIZE ** (-0.5)
    exponent = scaling * math.log2(math.e)
    me = lax.axis_index("ctx")
    p0 = lax.rem(me, devs)
    small = p0 // mid
    big = 1 - small
    ps = lax.rem(p0, mid)

    def ahead(d):
        return lax.rem(me + d, ctx)

    def behind(d):
        return lax.rem(me + ctx - d, ctx)

    for h in range(2):
        for g in range(kv_heads):
            lanes = slice(g * HEAD_SIZE, (g + 1) * HEAD_SIZE)
            kv_buf[h, 0, g, :, :HEAD_SIZE] = k_ref[h, :, lanes]
            kv_buf[h, 0, g, :, HEAD_SIZE:] = v_ref[h, :, lanes]

    barrier = pltpu.get_barrier_semaphore()
    for d in range(1, devs):
        pl.semaphore_signal(barrier, inc=1, device_id={"ctx": ahead(d)}, device_id_type=MESH)
        pl.semaphore_signal(barrier, inc=1, device_id={"ctx": behind(d)}, device_id_type=MESH)
    planes = ctx // devs
    plane = me // devs
    far = range(1, planes) if with_adapters else range(0)
    for j in far:
        pl.semaphore_signal(
            barrier,
            inc=1,
            device_id={"ctx": lax.rem(me + j * devs, ctx)},
            device_id_type=MESH,
        )
    pl.semaphore_wait(barrier, 2 * (devs - 1) + len(far))

    def gather_copy(h, d):
        return pltpu.make_async_remote_copy(
            src_ref=kv_buf.at[h, 0],
            dst_ref=kv_buf.at[h, d],
            send_sem=g_send.at[h, d],
            recv_sem=g_recv.at[h, d],
            device_id={"ctx": ahead(d)},
            device_id_type=MESH,
        )

    def return_copy(which, h, g, d):
        return pltpu.make_async_remote_copy(
            src_ref=part_send.at[which, h, g, d],
            dst_ref=part_recv.at[which, h, g, d],
            send_sem=r_send.at[which, h, g, d],
            recv_sem=r_recv.at[which, h, g, d],
            device_id={"ctx": behind(d)},
            device_id_type=MESH,
        )

    for d in range(1, mid):

        @pl.when(ps + d < mid)
        def _():
            gather_copy(small, d).start()

    for d in range(1, devs):

        @pl.when((ps + d >= mid) & (ps + d < devs))
        def _():
            gather_copy(small, d).start()

    for d in range(1, mid):

        @pl.when(ps + d < mid)
        def _():
            gather_copy(big, d).start()

    for d in range(1, mid):

        @pl.when(d > ps)
        def _():
            kv_buf[small, d] = jnp.zeros(kv_buf.shape[2:], kv_buf.dtype)

        @pl.when(d > ps)
        def _():
            kv_buf[big, mid + d] = jnp.zeros(kv_buf.shape[2:], kv_buf.dtype)

    own_ids = jnp.transpose(
        jnp.broadcast_to(seg_ref[pl.ds(me, 1), :].astype(jnp.float32), (tok, tok))
    )
    rows = lax.broadcasted_iota(jnp.int32, (tok, tok), 0)
    columns = lax.broadcasted_iota(jnp.int32, (tok, tok), 1)
    for d in range(devs):
        ids = seg_ref[pl.ds(behind(d), 1), :].astype(jnp.float32)
        block = jnp.where(own_ids == ids, 0.0, MASKED)
        if d == 0:
            block = jnp.where(columns <= rows, block, MASKED)
        bias[1, :, d * tok : (d + 1) * tok] = jnp.where(d <= ps + mid, block, MASKED)
        if d < mid:
            bias[0, :, d * tok : (d + 1) * tok] = jnp.where(d <= ps, block, MASKED)

    def within(j):
        return lax.rem(p0 + j, devs)

    def scatter_copy(bufs, j):
        part, landed, s_send, s_recv = bufs[0], bufs[1], bufs[4], bufs[5]
        return pltpu.make_async_remote_copy(
            src_ref=part.at[within(j)],
            dst_ref=landed.at[j],
            send_sem=s_send.at[j],
            recv_sem=s_recv.at[j],
            device_id={"ctx": plane * devs + within(j)},
            device_id_type=MESH,
        )

    def plane_copy(bufs, j):
        across, s_send, s_recv = bufs[2], bufs[6], bufs[7]
        return pltpu.make_async_remote_copy(
            src_ref=across.at[plane],
            dst_ref=across.at[plane],
            send_sem=s_send.at[j],
            recv_sem=s_recv.at[j],
            device_id={"ctx": lax.rem(me + j * devs, ctx)},
            device_id_type=MESH,
        )

    def spread_copy(bufs, j):
        whole, s_send, s_recv = bufs[3], bufs[8], bufs[9]
        return pltpu.make_async_remote_copy(
            src_ref=whole.at[p0],
            dst_ref=whole.at[p0],
            send_sem=s_send.at[j],
            recv_sem=s_recv.at[j],
            device_id={"ctx": plane * devs + within(j)},
            device_id_type=MESH,
        )

    def start_scatter(bufs):
        for j in range(1, devs):
            scatter_copy(bufs, j).start()

    def start_planes(bufs):
        total = bufs[0][p0].astype(jnp.float32)
        for j in range(1, devs):
            scatter_copy(bufs, j).wait_recv()
            total = total + bufs[1][j].astype(jnp.float32)
        bufs[2][plane] = total.astype(jnp.bfloat16)
        for j in range(1, planes):
            plane_copy(bufs, j).start()

    def start_spread(bufs):
        for j in range(1, planes):
            plane_copy(bufs, j).wait_recv()
        total = bufs[2][0].astype(jnp.float32)
        for j in range(1, planes):
            total = total + bufs[2][j].astype(jnp.float32)
        bufs[3][p0] = total.astype(jnp.bfloat16)
        for j in range(1, devs):
            spread_copy(bufs, j).start()

    def finish(bufs, down_out, up_out, up_pieces):
        for j in range(1, devs):
            spread_copy(bufs, j).wait_recv()
        width = down_out.shape[1] // devs
        up_width = 2 * up_out.shape[2] // up_pieces
        for p in range(devs):
            down_out[:, p * width : (p + 1) * width] = adapter_scale * bufs[3][
                p, :, :width
            ].astype(jnp.float32)
            if p < up_pieces:
                h, at = p // (up_pieces // 2), p % (up_pieces // 2)
                up_out[:, h, at * up_width : (at + 1) * up_width] = adapter_scale * bufs[3][
                    p, :, width:
                ].astype(jnp.float32)
        for j in range(1, devs):
            scatter_copy(bufs, j).wait_send()
            spread_copy(bufs, j).wait_send()
        for j in range(1, planes):
            plane_copy(bufs, j).wait_send()

    def project_down(bufs, act):
        width = x_ref.shape[1] // devs
        for p in range(devs):
            bufs[0][p, :, :width] = jnp.dot(
                act, x_ref[:, p * width : (p + 1) * width], preferred_element_type=jnp.float32
            ).astype(jnp.bfloat16)

    if with_adapters:
        for source, act in ((q_down_ref, q_down), (v_down_ref, v_down)):
            act[...] = lax.dot_general(
                source[...],
                x_ref[...],
                (((1,), (1,)), ((), ())),
                preferred_element_type=jnp.float32,
            ).astype(jnp.bfloat16)
        for h in range(2):
            q_up[h] = q_up_ref[:, h, :]
            v_up[h] = v_up_ref[:, h, :]
        q_act[...] = jnp.zeros_like(q_act)
        rank = q_act.shape[0]
        for p in range(2 * kv_heads, devs):
            v_bufs[0][p, :, x_ref.shape[1] // devs :] = jnp.zeros((rank, HEAD_SIZE), jnp.bfloat16)

    def stacked(ref, h, g):
        return jnp.concatenate(
            [
                ref[h, :, g * group_width + r * HEAD_SIZE : g * group_width + (r + 1) * HEAD_SIZE]
                for r in range(repeat)
            ],
            axis=0,
        )

    def send_parts(which, total, h, g, slots, limit):
        for d in range(slots):
            block = jnp.transpose(total[:, d * tok : (d + 1) * tok])
            if d == 0:
                own_part[which, h, g] = block
            else:
                part_send[which, h, g, d] = block.astype(jnp.bfloat16)
        for d in range(1, slots):

            @pl.when(d < limit)
            def _():
                return_copy(which, h, g, d).start()

    def probabilities(h, g, slots, limit):
        keys = slots * tok
        k = kv_buf[h, :slots, g, :, :HEAD_SIZE].reshape(keys, HEAD_SIZE)

        def one_head(r, inner):
            lanes = pl.ds(pl.multiple_of(g * group_width + r * HEAD_SIZE, HEAD_SIZE), HEAD_SIZE)
            at = pl.ds(pl.multiple_of(r * tok, tok), tok)
            s = lax.dot_general(
                q_ref[h, :, lanes],
                k,
                (((1,), (1,)), ((), ())),
                preferred_element_type=jnp.float32,
            )
            t = s * exponent + bias[int(slots == devs), :, :keys]
            e = jnp.exp2(t - jnp.max(t, axis=1, keepdims=True))
            w = e * (1.0 / jnp.sum(e, axis=1, keepdims=True))
            w_scr[g, at, :keys] = w
            p_scr[at, :keys] = w.astype(jnp.bfloat16)
            return inner

        lax.fori_loop(0, repeat, one_head, 0, unroll=8)
        dv = lax.dot_general(
            stacked(do_ref, h, g),
            p_scr[:, :keys],
            (((0,), (0,)), ((), ())),
            preferred_element_type=jnp.float32,
        )
        send_parts(1, dv, h, g, slots, limit)

    def score_gradients(h, g, slots, limit):
        keys = slots * tok
        k = kv_buf[h, :slots, g, :, :HEAD_SIZE].reshape(keys, HEAD_SIZE)
        v = kv_buf[h, :slots, g, :, HEAD_SIZE:].reshape(keys, HEAD_SIZE)

        def one_head(r, inner):
            lanes = pl.ds(pl.multiple_of(g * group_width + r * HEAD_SIZE, HEAD_SIZE), HEAD_SIZE)
            at = pl.ds(pl.multiple_of(r * tok, tok), tok)
            dp = lax.dot_general(
                do_ref[h, :, lanes],
                v,
                (((1,), (1,)), ((), ())),
                preferred_element_type=jnp.float32,
            )
            w = w_scr[g, at, :keys]
            low = w.astype(jnp.bfloat16).astype(jnp.float32)
            dot = jnp.sum(low * dp, axis=1, keepdims=True)
            ds = (w * (dp - dot)).astype(jnp.bfloat16)
            p_scr[at, :keys] = ds
            dq = jnp.dot(ds, k, preferred_element_type=jnp.float32) * scaling
            dq_ref[h, :, lanes] = dq.astype(jnp.bfloat16)
            return inner

        lax.fori_loop(0, repeat, one_head, 0, unroll=8)
        if with_adapters:
            lanes = slice(g * group_width, (g + 1) * group_width)
            dq_all = dq_ref[h, :, lanes]
            q_act[...] += lax.dot_general(
                q_up[h, :, lanes],
                dq_all,
                (((1,), (1,)), ((), ())),
                preferred_element_type=jnp.float32,
            )
            up = jnp.dot(q_down[...], dq_all, preferred_element_type=jnp.float32)
            up = up.astype(jnp.bfloat16)
            width = x_ref.shape[1] // devs
            each = group_width * 2 * kv_heads // devs
            pieces = group_width // each
            for i in range(pieces):
                q_bufs[0][(h * kv_heads + g) * pieces + i, :, width:] = up[
                    :, i * each : (i + 1) * each
                ]
        dk = lax.dot_general(
            stacked(q_ref, h, g),
            p_scr[:, :keys],
            (((0,), (0,)), ((), ())),
            preferred_element_type=jnp.float32,
        )
        send_parts(0, dk * scaling, h, g, slots, limit)

    def collect(which, out_ref):
        for d in range(1, devs):
            for g in range(kv_heads):

                @pl.when(ps + d < devs)
                def _():
                    return_copy(which, small, g, d).wait_recv()
                    own_part[which, small, g] += part_recv[which, small, g, d].astype(jnp.float32)

        for d in range(1, mid):
            for g in range(kv_heads):

                @pl.when(ps + d < mid)
                def _():
                    return_copy(which, big, g, d).wait_recv()
                    own_part[which, big, g] += part_recv[which, big, g, d].astype(jnp.float32)

        for h in range(2):
            for g in range(kv_heads):
                out_ref[h, :, g * HEAD_SIZE : (g + 1) * HEAD_SIZE] = own_part[which, h, g].astype(
                    jnp.bfloat16
                )

    def value_adapter():
        v_act = jnp.zeros(q_act.shape, jnp.float32)
        for h in range(2):
            v_act = v_act + lax.dot_general(
                v_up[h], gv_ref[h], (((1,), (1,)), ((), ())), preferred_element_type=jnp.float32
            )
            up = jnp.dot(v_down[...], gv_ref[h], preferred_element_type=jnp.float32)
            for g in range(kv_heads):
                v_bufs[0][h * kv_heads + g, :, x_ref.shape[1] // devs :] = up[
                    :, g * HEAD_SIZE : (g + 1) * HEAD_SIZE
                ].astype(jnp.bfloat16)
        project_down(v_bufs, v_act.astype(jnp.bfloat16))
        start_scatter(v_bufs)

    for d in range(1, mid):

        @pl.when(d <= ps)
        def _():
            gather_copy(small, d).wait_recv()

    for g in range(kv_heads):
        probabilities(small, g, mid, ps + 1)
    for g in range(kv_heads):
        score_gradients(small, g, mid, ps + 1)

    for d in range(1, devs):

        @pl.when(d <= ps + mid)
        def _():
            gather_copy(big, d).wait_recv()

    for g in range(kv_heads):
        probabilities(big, g, devs, ps + mid + 1)
    for g in range(kv_heads):
        score_gradients(big, g, devs, ps + mid + 1)
        if g == 0:
            collect(1, gv_ref)
            if with_adapters:
                value_adapter()

    if with_adapters:
        project_down(q_bufs, q_act[...].astype(jnp.bfloat16))
        start_scatter(q_bufs)
        start_planes(v_bufs)
        start_planes(q_bufs)
        start_spread(v_bufs)
        start_spread(q_bufs)
    collect(0, gk_ref)
    if with_adapters:
        finish(v_bufs, vd_out, vu_out, 2 * kv_heads)
        finish(q_bufs, qd_out, qu_out, devs)

    for d in range(1, devs):

        @pl.when(ps + d < devs)
        def _():
            gather_copy(small, d).wait_send()

        @pl.when(d <= ps + mid)
        def _():
            for which in range(2):
                for g in range(kv_heads):
                    return_copy(which, big, g, d).wait_send()

    for d in range(1, mid):

        @pl.when(ps + d < mid)
        def _():
            gather_copy(big, d).wait_send()

        @pl.when(d <= ps)
        def _():
            for which in range(2):
                for g in range(kv_heads):
                    return_copy(which, small, g, d).wait_send()


def attention_backward(q, do, k, v, seg, devs, adapters=None):
    tok, width = q.shape[1], q.shape[2]
    kv_heads = k.shape[2] // HEAD_SIZE
    repeat = width // k.shape[2]
    ctx = lax.axis_size("ctx")
    planes = ctx // devs
    bf16, f32 = jnp.bfloat16, jnp.float32
    vmem = pl.BlockSpec(memory_space=pltpu.VMEM)
    operands = (q, do, k, v, seg)
    results = [jax.ShapeDtypeStruct(a.shape, bf16) for a in (q, k, v)]
    scratch = [
        pltpu.VMEM((2, devs, kv_heads, tok, 2 * HEAD_SIZE), bf16),
        pltpu.VMEM((2, 2, kv_heads, devs, tok, HEAD_SIZE), bf16),
        pltpu.VMEM((2, 2, kv_heads, devs, tok, HEAD_SIZE), bf16),
        pltpu.VMEM((2, 2, kv_heads, tok, HEAD_SIZE), f32),
        pltpu.VMEM((repeat * tok, devs * tok), bf16),
        pltpu.VMEM((kv_heads, repeat * tok, devs * tok), f32),
        pltpu.VMEM((2, tok, devs * tok), f32),
        pltpu.SemaphoreType.DMA((2, devs)),
        pltpu.SemaphoreType.DMA((2, devs)),
        pltpu.SemaphoreType.DMA((2, 2, kv_heads, devs)),
        pltpu.SemaphoreType.DMA((2, 2, kv_heads, devs)),
    ]
    if adapters is not None:
        operands = operands + adapters
        x, q_down, v_down, q_up, v_up = adapters
        rank = q_down.shape[0]
        results += [jax.ShapeDtypeStruct(a.shape, f32) for a in (q_down, q_up, v_down, v_up)]
        scratch += [
            pltpu.VMEM((rank, tok), bf16),
            pltpu.VMEM((rank, tok), bf16),
            pltpu.VMEM((2, rank, q.shape[2]), bf16),
            pltpu.VMEM((2, rank, k.shape[2]), bf16),
            pltpu.VMEM((rank, tok), f32),
        ]
        for columns in ((x.shape[1] + 2 * width) // devs, x.shape[1] // devs + HEAD_SIZE):
            scratch += [
                pltpu.VMEM((n, rank, columns), bf16) for n in (devs, devs, planes, devs)
            ]
            scratch += [
                pltpu.SemaphoreType.DMA((n,)) for n in (devs, devs, planes, planes, devs, devs)
            ]
    return pl.pallas_call(
        functools.partial(attention_kernel, ctx, devs, adapters is not None),
        out_shape=tuple(results),
        in_specs=[vmem] * len(operands),
        out_specs=(vmem,) * len(results),
        scratch_shapes=scratch,
        compiler_params=pltpu.CompilerParams(
            collective_id=0, has_side_effects=True, vmem_limit_bytes=52 * 1024 * 1024
        ),
        name="attention_backward",
    )(*operands)


def paired_kernel(
    chips,
    span,
    q_hbm,
    do_hbm,
    k_hbm,
    v_hbm,
    seg_hbm,
    x_ref,
    q_down_hbm,
    v_down_hbm,
    q_up_hbm,
    v_up_hbm,
    dq_out,
    gk_out,
    gv_out,
    q_sums,
    q_other,
    v_sums,
    v_other,
    q_raw,
    do_raw,
    k_raw,
    v_raw,
    seg_ref,
    q_down_ref,
    v_down_ref,
    q_up_ref,
    v_up_ref,
    q_away,
    do_away,
    k_ref,
    v_ref,
    dq_land,
    q_up,
    x_away,
    qb,
    dob,
    kb,
    vb,
    xb,
    dqb,
    p_small,
    p_big,
    bias,
    part_send,
    part_recv,
    acc,
    sib_part,
    down_mine,
    down_theirs,
    act_mine,
    act_theirs,
    mixed_mine,
    mixed_theirs,
    acts,
    q_parts,
    q_land,
    q_across,
    v_parts,
    v_land,
    v_across,
    local_sem,
    swap_send,
    swap_recv,
    g_send,
    g_recv,
    r_send,
    r_recv,
    a_send,
    a_recv,
):
    bf16, f32 = jnp.bfloat16, jnp.float32
    tok = q_raw.shape[0]
    pair = 2 * tok
    width = qb.shape[2]
    heads = width // HEAD_SIZE
    columns = xb.shape[1]
    cube = q_parts.shape[0]
    cubes = chips // cube
    each = columns // cube
    up_each = 2 * width // cube
    rank = acts.shape[1]
    mid = span // 2
    scaling = HEAD_SIZE ** (-0.5)
    exponent = scaling * math.log2(math.e)
    me = lax.axis_index("ctx")
    chip = me // 2
    core = lax.rem(me, 2)
    spot = lax.rem(chip, cube)
    mine = chip // cube
    other = 1 - core
    place = lax.rem(chip, span)
    small = place // mid
    big = 1 - small
    ps = lax.rem(place, mid)

    def ahead(d):
        return lax.rem(chip + d, chips)

    def behind(d):
        return lax.rem(chip + chips - d, chips)

    def within(j):
        return lax.rem(spot + j, cube)

    def device(chip_at, core_at):
        return {"ctx": 2 * chip_at + core_at}

    sibling = device(chip, other)

    def rows(at):
        return pl.ds(pl.multiple_of(at * tok, tok), tok)

    def half_columns(at, size):
        return pl.ds(pl.multiple_of(at * size, size), size)

    barrier = pltpu.get_barrier_semaphore()
    pl.semaphore_signal(barrier, inc=1, device_id=sibling, device_id_type=MESH)
    for j in range(1, cube):
        pl.semaphore_signal(
            barrier, inc=1, device_id=device(mine * cube + within(j), core), device_id_type=MESH
        )
    for j in range(1, cubes):
        pl.semaphore_signal(
            barrier, inc=1, device_id=device(ahead(j * cube), core), device_id_type=MESH
        )
    for d in range(1, span):
        for to in range(2):
            pl.semaphore_signal(
                barrier, inc=1, device_id=device(ahead(d), to), device_id_type=MESH
            )
            pl.semaphore_signal(
                barrier, inc=1, device_id=device(behind(d), to), device_id_type=MESH
            )

    staged = [
        pltpu.make_async_copy(src, dst, local_sem.at[i])
        for i, (src, dst) in enumerate(
            (
                (k_hbm, k_raw),
                (v_hbm, v_raw),
                (q_hbm, q_raw),
                (do_hbm, do_raw),
                (seg_hbm, seg_ref),
                (x_ref.at[:, half_columns(core, columns)], xb.at[rows(core)]),
                (q_down_hbm, q_down_ref),
                (v_down_hbm, v_down_ref),
                (q_up_hbm, q_up_ref),
                (v_up_hbm, v_up_ref),
                (x_ref.at[:, half_columns(other, columns)], x_away),
            )
        )
    ]
    for copy in staged:
        copy.start()

    def swap_columns(row):
        return pltpu.make_async_remote_copy(
            src_ref=x_away,
            dst_ref=xb.at[rows(row)],
            send_sem=swap_send.at[4],
            recv_sem=swap_recv.at[4],
            device_id=sibling,
            device_id_type=MESH,
        )

    def swap_half(h, i, row):
        return pltpu.make_async_remote_copy(
            src_ref=(q_away, do_away)[i].at[h],
            dst_ref=(qb, dob)[i].at[h, rows(row)],
            send_sem=swap_send.at[2 * h + i],
            recv_sem=swap_recv.at[2 * h + i],
            device_id=sibling,
            device_id_type=MESH,
        )

    def gather_copy(which, h, d, to, row):
        src = (k_ref, v_ref)[which].at[h, :, half_columns(to, HEAD_SIZE)]
        return pltpu.make_async_remote_copy(
            src_ref=src,
            dst_ref=(kb, vb)[which].at[h, d, rows(row)],
            send_sem=g_send.at[which, h, d, to],
            recv_sem=g_recv.at[which, h, d, row],
            device_id=device(ahead(d), to),
            device_id_type=MESH,
        )

    def gather_start(which, h, d):
        for to in range(2):
            gather_copy(which, h, d, to, core).start()

    def gather_wait(which, h, d):
        for row in range(2):
            gather_copy(which, h, d, row, row).wait_recv()

    def gather_sent(which, h, d):
        for to in range(2):
            gather_copy(which, h, d, to, core).wait_send()

    @pl.when(ps == 0)
    def _():
        for buf in (kb, vb):
            buf[small, 1] = jnp.zeros(buf.shape[2:], bf16)
            buf[big, span - 1] = jnp.zeros(buf.shape[2:], bf16)

    to_row = lax.broadcasted_iota(jnp.int32, (pair, pair), 0)
    from_row = lax.broadcasted_iota(jnp.int32, (pair, pair), 1)
    parting = jnp.where(from_row == 2 * lax.rem(to_row, tok) + to_row // tok, 1.0, 0.0).astype(bf16)

    def parted(raw, lanes):
        return jnp.dot(
            parting, raw[:, :, lanes].reshape(pair, HEAD_SIZE), preferred_element_type=f32
        ).astype(bf16)

    for i, (raw, ref, buf) in enumerate(((k_raw, k_ref, kb), (v_raw, v_ref, vb))):
        staged[i].wait()
        for head in range(2):
            lanes = slice(head * HEAD_SIZE, (head + 1) * HEAD_SIZE)
            both = parted(raw, lanes)
            for h in range(2):
                ref[h, :, lanes] = both[h * tok : (h + 1) * tok]
        for h in range(2):
            buf[h, 0, rows(core)] = ref[h, :, half_columns(core, HEAD_SIZE)]
    def part_rows(i):
        raw, buf, away = ((q_raw, qb, q_away), (do_raw, dob, do_away))[i]
        staged[2 + i].wait()
        for j in range(heads):
            lanes = slice(j * HEAD_SIZE, (j + 1) * HEAD_SIZE)
            for at in (other, core):
                start = pl.multiple_of(at * width + j * HEAD_SIZE, HEAD_SIZE)
                both = parted(raw, pl.ds(start, HEAD_SIZE))
                for h in range(2):
                    block = both[h * tok : (h + 1) * tok]
                    if at is core:
                        buf[h, rows(core), lanes] = block
                    else:
                        away[h, :, lanes] = block

    part_rows(0)

    pl.semaphore_wait(barrier, cube + cubes - 1 + 4 * (span - 1))

    def gather_all(which):
        for d in range(1, mid):

            @pl.when(ps + d < mid)
            def _():
                gather_start(which, small, d)

        for d in range(1, span):

            @pl.when((ps + d >= mid) & (ps + d < span))
            def _():
                gather_start(which, small, d)

        for d in range(1, mid):

            @pl.when(ps + d < mid)
            def _():
                gather_start(which, big, d)

    gather_all(0)
    gather_copy(0, small, 0, other, core).start()
    swap_half(small, 0, core).start()
    gather_copy(0, big, 0, other, core).start()
    swap_half(big, 0, core).start()
    staged[10].wait()
    swap_columns(core).start()
    gather_all(1)
    part_rows(1)
    for h in (small, big):
        swap_half(h, 1, core).start()
        gather_copy(1, h, 0, other, core).start()

    staged[4].wait()

    def chip_ids(at):
        first = seg_ref[pl.ds(2 * at, 1), :]
        second = seg_ref[pl.ds(2 * at + 1, 1), :]
        return jnp.concatenate([first, second], axis=1).astype(f32)

    own_ids = jnp.transpose(jnp.broadcast_to(chip_ids(chip), (pair, pair)))
    row = lax.broadcasted_iota(jnp.int32, (pair, pair), 0)
    column = lax.broadcasted_iota(jnp.int32, (pair, pair), 1)
    for d in range(span):
        block = jnp.where(own_ids == chip_ids(behind(d)), 0.0, MASKED)
        if d == 0:
            block = jnp.where(column <= row, block, MASKED)
        bias[1, :, d * pair : (d + 1) * pair] = jnp.where(d <= ps + mid, block, MASKED)
        if d < mid:
            bias[0, :, d * pair : (d + 1) * pair] = jnp.where(d <= ps, block, MASKED)

    def exchange(src, dst, i):
        return pltpu.make_async_remote_copy(
            src_ref=src,
            dst_ref=dst,
            send_sem=swap_send.at[i],
            recv_sem=swap_recv.at[i],
            device_id=sibling,
            device_id_type=MESH,
        )

    down_swap = exchange(down_mine, down_theirs, 5)
    act_swap = exchange(act_mine, act_theirs, 6)
    mixed_swap = exchange(mixed_mine, mixed_theirs, 7)

    def part_swap(which, h):
        return pltpu.make_async_remote_copy(
            src_ref=sib_part.at[which, h],
            dst_ref=acc.at[which, h, core],
            send_sem=swap_send.at[8 + 2 * which + h],
            recv_sem=swap_recv.at[8 + 2 * which + h],
            device_id=sibling,
            device_id_type=MESH,
        )

    def part_wait(which, h):
        return pltpu.make_async_remote_copy(
            src_ref=sib_part.at[which, h],
            dst_ref=acc.at[which, h, other],
            send_sem=swap_send.at[8 + 2 * which + h],
            recv_sem=swap_recv.at[8 + 2 * which + h],
            device_id=sibling,
            device_id_type=MESH,
        )

    def dq_swap(h):
        return exchange(dqb.at[h, rows(other)], dq_land.at[h], 12 + h)

    def scatter_copy(bufs, j):
        s, parts, land = bufs[:3]
        return pltpu.make_async_remote_copy(
            src_ref=parts.at[within(j)],
            dst_ref=land.at[j],
            send_sem=a_send.at[3 * s, j],
            recv_sem=a_recv.at[3 * s, j],
            device_id=device(mine * cube + within(j), core),
            device_id_type=MESH,
        )

    def across_copy(bufs, j, source):
        s, across = bufs[0], bufs[3]
        return pltpu.make_async_remote_copy(
            src_ref=across.at[source],
            dst_ref=across.at[source],
            send_sem=a_send.at[3 * s + 1, j],
            recv_sem=a_recv.at[3 * s + 1, j],
            device_id=device(ahead(j * cube), core),
            device_id_type=MESH,
        )

    def spread_copy(bufs, j, source):
        s, sums = bufs[0], bufs[4]
        return pltpu.make_async_remote_copy(
            src_ref=sums.at[source],
            dst_ref=sums.at[source],
            send_sem=a_send.at[3 * s + 2, j],
            recv_sem=a_recv.at[3 * s + 2, j],
            device_id=device(mine * cube + within(j), core),
            device_id_type=MESH,
        )

    q_set = (0, q_parts, q_land, q_across, q_sums, q_other)
    v_set = (1, v_parts, v_land, v_across, v_sums, v_other)

    def start_scatter(bufs):
        for j in range(1, cube):
            scatter_copy(bufs, j).start()

    def start_across(bufs):
        total = bufs[1][spot].astype(f32)
        for j in range(1, cube):
            scatter_copy(bufs, j).wait_recv()
            total = total + bufs[2][j].astype(f32)
        bufs[3][mine] = total.astype(bf16)
        for j in range(1, cubes):
            across_copy(bufs, j, mine).start()

    def start_spread(bufs):
        for j in range(1, cubes):
            across_copy(bufs, j, lax.rem(mine + cubes - j, cubes)).wait_recv()
        total = bufs[3][0].astype(f32)
        for j in range(1, cubes):
            total = total + bufs[3][j].astype(f32)
        bufs[4][spot] = total.astype(bf16)
        for j in range(1, cube):
            spread_copy(bufs, j, spot).start()

    def hand_copy(bufs):
        return exchange(bufs[4], bufs[5], 14 + bufs[0])

    def start_hand(bufs):
        for j in range(1, cube):
            spread_copy(bufs, j, lax.rem(spot + cube - j, cube)).wait_recv()
        hand_copy(bufs).start()

    def finish(bufs):
        hand_copy(bufs).wait()
        for j in range(1, cube):
            scatter_copy(bufs, j).wait_send()
            spread_copy(bufs, j, spot).wait_send()
        for j in range(1, cubes):
            across_copy(bufs, j, mine).wait_send()

    def project_down(parts, act):
        for i in range(cube):
            parts[i, :, :each] = jnp.dot(
                act, xb[:, i * each : (i + 1) * each], preferred_element_type=f32
            ).astype(bf16)

    def return_copy(which, h, d, to, head):
        return pltpu.make_async_remote_copy(
            src_ref=part_send.at[which, h, d, rows(to)],
            dst_ref=part_recv.at[which, h, d, head],
            send_sem=r_send.at[which, h, d, to],
            recv_sem=r_recv.at[which, h, d, head],
            device_id=device(behind(d), to),
            device_id_type=MESH,
        )

    def send_parts(which, total, h, slots, limit):
        for d in reversed(range(slots)):
            block = jnp.transpose(total[:, d * pair : (d + 1) * pair])
            if d == 0:
                acc[which, h, core] = jnp.where(core == 0, block[:tok], block[tok:])
                sib_part[which, h] = jnp.where(core == 0, block[tok:], block[:tok])
                part_swap(which, h).start()
            else:
                part_send[which, h, d] = block.astype(bf16)

                @pl.when(d < limit)
                def _():
                    for to in range(2):
                        return_copy(which, h, d, to, core).start()

    def stacked(ref, h):
        return jnp.concatenate(
            [ref[h, :, j * HEAD_SIZE : (j + 1) * HEAD_SIZE] for j in range(heads)], axis=0
        )

    def head_lanes(j):
        return pl.ds(pl.multiple_of(j * HEAD_SIZE, HEAD_SIZE), HEAD_SIZE)

    def head_rows(j):
        return pl.ds(pl.multiple_of(j * pair, pair), pair)

    def probabilities(h, p_ref, slots, limit):
        keys = slots * pair
        k = kb[h, :slots].reshape(keys, HEAD_SIZE)

        def one_head(j, inner):
            s = lax.dot_general(
                qb[h, :, head_lanes(j)], k, (((1,), (1,)), ((), ())), preferred_element_type=f32
            )
            t = s * exponent + bias[int(slots == span), :, :keys]
            e = jnp.exp2(t - jnp.max(t, axis=1, keepdims=True))
            w = e * (1.0 / jnp.sum(e, axis=1, keepdims=True))
            p_ref[head_rows(j)] = w.astype(bf16)
            return inner

        lax.fori_loop(0, heads, one_head, 0, unroll=heads)

    def value_part(h, p_ref, slots, limit):
        dv = lax.dot_general(
            stacked(dob, h), p_ref[...], (((0,), (0,)), ((), ())), preferred_element_type=f32
        )
        send_parts(1, dv, h, slots, limit)

    def score_gradients(h, p_ref, slots, first, last):
        keys = slots * pair
        k = kb[h, :slots].reshape(keys, HEAD_SIZE)
        v = vb[h, :slots].reshape(keys, HEAD_SIZE)

        def scores_of(j):
            dp = lax.dot_general(
                dob[h, :, head_lanes(j)], v, (((1,), (1,)), ((), ())), preferred_element_type=f32
            )
            w = p_ref[head_rows(j)].astype(f32)
            dot = jnp.sum(w * dp, axis=1, keepdims=True)
            p_ref[head_rows(j)] = (w * (dp - dot)).astype(bf16)

        def queries_of(j):
            dq = jnp.dot(p_ref[head_rows(j)], k, preferred_element_type=f32) * scaling
            dqb[h, :, head_lanes(j)] = dq.astype(bf16)

        def one_head(j, inner):
            scores_of(j)
            queries_of(j - 1)
            return inner

        scores_of(first)
        lax.fori_loop(first + 1, last, one_head, 0, unroll=last - first - 1)
        queries_of(last - 1)
        if last == heads:
            dq_swap(h).start()

    def query_adapter(h):
        return lax.dot_general(
            q_up[h],
            dqb[h],
            (((1,), (1,)), ((), ())),
            preferred_element_type=f32,
        )

    def key_part(h, p_ref, slots, limit):
        dk = lax.dot_general(
            stacked(qb, h), p_ref[...], (((0,), (0,)), ((), ())), preferred_element_type=f32
        )
        send_parts(0, dk * scaling, h, slots, limit)

    def collect(which):
        for h in range(2):
            part_wait(which, h).wait_recv()
        for d in range(1, span):

            @pl.when(ps + d < span)
            def _():
                for head in range(2):
                    return_copy(which, small, d, head, head).wait_recv()
                    acc[which, small, head] += part_recv[which, small, d, head].astype(f32)

        for d in range(1, mid):

            @pl.when(ps + d < mid)
            def _():
                for head in range(2):
                    return_copy(which, big, d, head, head).wait_recv()
                    acc[which, big, head] += part_recv[which, big, d, head].astype(f32)

        return [
            jnp.concatenate([acc[which, h, 0], acc[which, h, 1]], axis=1).astype(bf16)
            for h in range(2)
        ]

    def wait_swap(h, i):
        swap_half(h, i, other).wait_recv()

    for i in range(5, 10):
        staged[i].wait()
    for h in range(2):
        q_up[h] = q_up_ref[:, h, half_columns(core, width)]
    swap_columns(other).wait_recv()
    for i, source in enumerate((q_down_ref, v_down_ref)):
        down_mine[i] = lax.dot_general(
            source[:, half_columns(core, columns)],
            xb[...],
            (((1,), (1,)), ((), ())),
            preferred_element_type=f32,
        )
    down_swap.start()

    wait_swap(small, 0)
    gather_copy(0, small, 0, other, other).wait_recv()
    for d in range(1, mid):

        @pl.when(d <= ps)
        def _():
            gather_wait(0, small, d)

    probabilities(small, p_small, mid, ps + 1)
    wait_swap(small, 1)
    value_part(small, p_small, mid, ps + 1)

    wait_swap(big, 0)
    gather_copy(0, big, 0, other, other).wait_recv()
    for d in range(1, span):

        @pl.when(d <= ps + mid)
        def _():
            gather_wait(0, big, d)

    probabilities(big, p_big, span, ps + mid + 1)
    wait_swap(big, 1)
    value_part(big, p_big, span, ps + mid + 1)

    down_swap.wait()
    for i in range(2):
        acts[i] = (down_mine[i] + down_theirs[i]).astype(bf16)

    for h in (small, big):
        gather_copy(1, h, 0, other, other).wait_recv()
    for d in range(1, mid):

        @pl.when(d <= ps)
        def _():
            gather_wait(1, small, d)

    for d in range(1, span):

        @pl.when(d <= ps + mid)
        def _():
            gather_wait(1, big, d)

    score_gradients(small, p_small, mid, 0, heads)
    act_small = query_adapter(small)
    score_gradients(big, p_big, span, 0, heads)
    act_mine[...] = act_small + query_adapter(big)
    act_swap.start()
    for h in range(2):
        up = jnp.dot(acts[0], dqb[h], preferred_element_type=f32).astype(bf16)
        for i in range(cube // 2):
            q_parts[h * (cube // 2) + i, :, each:] = up[:, i * up_each : (i + 1) * up_each]
    act_swap.wait()
    project_down(q_parts, (act_mine[...] + act_theirs[...]).astype(bf16))
    start_scatter(q_set)

    gv = collect(1)
    v_act = jnp.zeros((rank, tok), f32)
    own_lanes = half_columns(core, tok)
    for h in range(2):
        v_act = v_act + lax.dot_general(
            v_up_ref[:, h, :], gv[h], (((1,), (1,)), ((), ())), preferred_element_type=f32
        )
        up = jnp.dot(acts[1, :, own_lanes], gv[h], preferred_element_type=f32)
        first, second = up[:, :HEAD_SIZE], up[:, HEAD_SIZE:]
        mixed_mine[1 + h] = jnp.where(core == 0, second, first)
        mixed_mine[3 + h] = jnp.where(core == 0, first, second)
    mixed_mine[0] = v_act
    mixed_swap.start()
    for h in range(2):
        gv_out[:, h, :] = gv[h]

    key_part(big, p_big, span, ps + mid + 1)

    mixed_swap.wait()
    acts[2, :, own_lanes] = mixed_mine[0].astype(bf16)
    acts[2, :, half_columns(other, tok)] = mixed_theirs[0].astype(bf16)
    for i in range(cube):
        if i < 2:
            v_parts[i, :, each:] = (mixed_mine[3 + i] + mixed_theirs[1 + i]).astype(bf16)
        else:
            v_parts[i, :, each:] = jnp.zeros((rank, HEAD_SIZE), bf16)
    project_down(v_parts, acts[2])
    start_scatter(v_set)

    key_part(small, p_small, mid, ps + 1)

    start_across(q_set)
    start_across(v_set)
    start_spread(q_set)
    start_spread(v_set)
    for h in range(2):
        dq_out[:, h, half_columns(core, width)] = dqb[h, rows(core)]
        dq_swap(h).wait_recv()
        dq_out[:, h, half_columns(other, width)] = dq_land[h]
    gk = collect(0)
    for h in range(2):
        gk_out[:, h, :] = gk[h]
    start_hand(q_set)
    start_hand(v_set)
    finish(q_set)
    finish(v_set)

    for h in range(2):
        dq_swap(h).wait_send()
        for i in range(2):
            swap_half(h, i, core).wait_send()
            part_swap(i, h).wait_send()
            gather_copy(i, h, 0, other, core).wait_send()
    swap_columns(core).wait_send()
    for which in range(2):
        for d in range(1, span):

            @pl.when(ps + d < span)
            def _():
                gather_sent(which, small, d)

            @pl.when(d <= ps + mid)
            def _():
                for to in range(2):
                    return_copy(which, big, d, to, core).wait_send()

        for d in range(1, mid):

            @pl.when(ps + d < mid)
            def _():
                gather_sent(which, big, d)

            @pl.when(d <= ps)
            def _():
                for to in range(2):
                    return_copy(which, small, d, to, core).wait_send()


def deliver_kernel(
    dq, gk, gv, q_sums, q_other, v_sums, v_other, *refs
):
    outs, totals, sems = refs[:7], refs[7:11], refs[11]
    core = lax.rem(lax.axis_index("ctx"), 2)
    copies = []

    def send(src, i):
        copies.append(pltpu.make_async_copy(src, outs[i], sems.at[i]))
        copies[-1].start()

    for i, src in enumerate((dq, gk, gv)):
        send(src, i)
    for i, (pair, pieces) in enumerate((((q_sums, q_other), None), ((v_sums, v_other), 2))):
        down, up = totals[2 * i], totals[2 * i + 1]
        cube = pair[0].shape[0]
        pieces = pieces or cube
        columns, width = down.shape[1] // 2, up.shape[2] // 2
        each, size = columns // cube, 2 * width // pieces
        for source, at in zip(pair, (core, 1 - core)):
            for p in range(cube):
                lanes = pl.ds(pl.multiple_of(at * columns + p * each, each), each)
                down[:, lanes] = adapter_scale * source[p, :, :each].astype(jnp.float32)
        send(down, 3 + 2 * i)
        for source, at in zip(pair, (core, 1 - core)):
            for p in range(pieces):
                h, step = p // (pieces // 2), p % (pieces // 2)
                lanes = pl.ds(pl.multiple_of(at * width + step * size, size), size)
                up[:, h, lanes] = adapter_scale * source[p, :, each:].astype(jnp.float32)
        send(up, 4 + 2 * i)
    for copy in copies:
        copy.wait()


def deliver(arrays, outs):
    vmem = pl.BlockSpec(memory_space=pltpu.VMEM)
    hbm = pl.BlockSpec(memory_space=pltpu.MemorySpace.HBM)
    return pl.pallas_call(
        deliver_kernel,
        out_shape=tuple(outs),
        in_specs=[vmem] * len(arrays),
        out_specs=(hbm,) * len(outs),
        scratch_shapes=[pltpu.VMEM(a.shape, a.dtype) for a in outs[3:]]
        + [pltpu.SemaphoreType.DMA((len(outs),))],
        name="deliver",
    )(*arrays)


def paired_backward(q, do, k, v, seg, x, q_down, v_down, q_up, v_up, span):
    tok, width = q.shape[0], q.shape[2] // 2
    pair = 2 * tok
    heads = width // HEAD_SIZE
    chips = lax.axis_size("ctx") // 2
    rank = q_down.shape[0]
    columns = x.shape[1] // 2
    bf16, f32 = jnp.bfloat16, jnp.float32
    vmem = pl.BlockSpec(memory_space=pltpu.VMEM)
    hbm = pl.BlockSpec(memory_space=pltpu.MemorySpace.HBM)
    cube = 2 * span
    q_piece = columns // cube + 2 * width // cube
    v_piece = columns // cube + HEAD_SIZE
    scratch = [pltpu.VMEM(a.shape, a.dtype) for a in (q, do, k, v, seg, q_down, v_down, q_up, v_up)]
    scratch += [
        pltpu.VMEM((2, tok, width), bf16),
        pltpu.VMEM((2, tok, width), bf16),
        pltpu.VMEM((2, tok, 2 * HEAD_SIZE), bf16),
        pltpu.VMEM((2, tok, 2 * HEAD_SIZE), bf16),
        pltpu.VMEM((2, tok, width), bf16),
        pltpu.VMEM((2, rank, width), bf16),
        pltpu.VMEM((tok, columns), bf16),
        pltpu.VMEM((2, pair, width), bf16),
        pltpu.VMEM((2, pair, width), bf16),
        pltpu.VMEM((2, span, pair, HEAD_SIZE), bf16),
        pltpu.VMEM((2, span, pair, HEAD_SIZE), bf16),
        pltpu.VMEM((pair, columns), bf16),
        pltpu.VMEM((2, pair, width), bf16),
        pltpu.VMEM((heads * pair, span // 2 * pair), bf16),
        pltpu.VMEM((heads * pair, span * pair), bf16),
        pltpu.VMEM((2, pair, span * pair), f32),
        pltpu.VMEM((2, 2, span, pair, HEAD_SIZE), bf16),
        pltpu.VMEM((2, 2, span, 2, tok, HEAD_SIZE), bf16),
        pltpu.VMEM((2, 2, 2, tok, HEAD_SIZE), f32),
        pltpu.VMEM((2, 2, tok, HEAD_SIZE), f32),
        pltpu.VMEM((2, rank, pair), f32),
        pltpu.VMEM((2, rank, pair), f32),
        pltpu.VMEM((rank, pair), f32),
        pltpu.VMEM((rank, pair), f32),
        pltpu.VMEM((5, rank, HEAD_SIZE), f32),
        pltpu.VMEM((5, rank, HEAD_SIZE), f32),
        pltpu.VMEM((3, rank, pair), bf16),
    ]
    for piece in (q_piece, v_piece):
        scratch += [
            pltpu.VMEM((n, rank, piece), bf16) for n in (cube, cube, chips // cube)
        ]
    scratch += [
        pltpu.SemaphoreType.DMA((11,)),
        pltpu.SemaphoreType.DMA((16,)),
        pltpu.SemaphoreType.DMA((16,)),
    ]
    scratch += [pltpu.SemaphoreType.DMA((2, 2, span, 2)) for _ in range(4)]
    scratch += [pltpu.SemaphoreType.DMA((6, max(cube, chips // cube))) for _ in range(2)]
    return pl.pallas_call(
        functools.partial(paired_kernel, chips, span),
        out_shape=tuple(
            [jax.ShapeDtypeStruct(a.shape, bf16) for a in (q, k, v)]
            + [
                jax.ShapeDtypeStruct((cube, rank, piece), bf16)
                for piece in (q_piece, q_piece, v_piece, v_piece)
            ]
        ),
        in_specs=[hbm] * 10,
        out_specs=(vmem,) * 7,
        scratch_shapes=scratch,
        compiler_params=pltpu.CompilerParams(
            collective_id=1, has_side_effects=True, vmem_limit_bytes=61 * 1024 * 1024
        ),
        name="paired_backward",
    )(q, do, k, v, seg, x, q_down, v_down, q_up, v_up)


def on_device(
    projected_queries,
    projected_keys,
    projected_values,
    output_gradient,
    normed_layer_input,
    segment,
    query_adapter_down,
    query_adapter_up,
    value_adapter_down,
    value_adapter_up,
):
    tok_rows = projected_queries.shape[0]
    query_width = projected_queries.shape[2]
    key_width = projected_keys.shape[2]
    key_value_heads = key_width // HEAD_SIZE
    group_devs = GROUP // tok_rows
    ctx = lax.axis_size("ctx")
    paired = (
        lax.axis_size("fsdp") == 1
        and group_devs % 4 == 0
        and ctx % (2 * group_devs) == 0
        and key_value_heads == 2
        and tok_rows == HEAD_SIZE
        and query_width % (ctx * HEAD_SIZE // 2) == 0
        and normed_layer_input.shape[1] % (ctx * HEAD_SIZE) == 0
    )
    if paired:
        results = paired_backward(
            projected_queries,
            output_gradient,
            projected_keys,
            projected_values,
            segment.reshape(-1, tok_rows),
            normed_layer_input,
            query_adapter_down,
            value_adapter_down,
            query_adapter_up,
            value_adapter_up,
            group_devs // 2,
        )
        outs = [
            jax.ShapeDtypeStruct(a.shape, jnp.bfloat16)
            for a in (projected_queries, projected_keys, projected_values)
        ] + [
            jax.ShapeDtypeStruct(a.shape, jnp.float32)
            for a in (
                query_adapter_down,
                query_adapter_up,
                value_adapter_down,
                value_adapter_up,
            )
        ]
        return deliver(results, outs)
    query_grad, key_grad, value_grad = attention_backward(
        projected_queries.transpose(1, 0, 2),
        output_gradient.transpose(1, 0, 2),
        projected_keys.transpose(1, 0, 2),
        projected_values.transpose(1, 0, 2),
        segment.reshape(-1, tok_rows),
        group_devs,
    )
    grad_query = query_grad.transpose(1, 0, 2)
    grad_key = key_grad.transpose(1, 0, 2)
    grad_value = value_grad.transpose(1, 0, 2)
    adapter_input = lax.psum(
        (
            jnp.dot(normed_layer_input, query_adapter_down.T, preferred_element_type=jnp.float32),
            jnp.dot(normed_layer_input, value_adapter_down.T, preferred_element_type=jnp.float32),
        ),
        "fsdp",
    )
    query_down_part = adapter_input[0].astype(jnp.bfloat16)
    value_down_part = adapter_input[1].astype(jnp.bfloat16)
    query_flattened_rows = grad_query.reshape(tok_rows, -1)
    value_flattened_rows = grad_value.reshape(tok_rows, -1)
    adapter_rank_rows = query_adapter_up.shape[0]
    adapter_output = lax.psum(
        (
            jnp.dot(
                query_flattened_rows,
                query_adapter_up.reshape(adapter_rank_rows, -1).T,
                preferred_element_type=jnp.float32,
            ),
            jnp.dot(
                value_flattened_rows,
                value_adapter_up.reshape(adapter_rank_rows, -1).T,
                preferred_element_type=jnp.float32,
            ),
        ),
        "fsdp",
    )
    query_up_part = adapter_output[0].astype(jnp.bfloat16)
    value_up_part = adapter_output[1].astype(jnp.bfloat16)
    local_down_query = jnp.dot(
        query_up_part.T, normed_layer_input, preferred_element_type=jnp.float32
    )
    local_up_query = jnp.dot(
        query_down_part.T, query_flattened_rows, preferred_element_type=jnp.float32
    ).reshape(adapter_rank_rows, 2, -1)
    local_down_value = jnp.dot(
        value_up_part.T, normed_layer_input, preferred_element_type=jnp.float32
    )
    local_up_value = jnp.dot(
        value_down_part.T, value_flattened_rows, preferred_element_type=jnp.float32
    ).reshape(adapter_rank_rows, 2, -1)
    gradient_totals = lax.psum(
        (local_down_query, local_up_query, local_down_value, local_up_value), "ctx"
    )
    return (
        grad_query,
        grad_key,
        grad_value,
        adapter_scale * gradient_totals[0],
        adapter_scale * gradient_totals[1],
        adapter_scale * gradient_totals[2],
        adapter_scale * gradient_totals[3],
    )


def solution(mesh):
    in_specs = (
        P(("rep", "ctx"), None, "fsdp"),
        P(("rep", "ctx"), None, "fsdp"),
        P(("rep", "ctx"), None, "fsdp"),
        P(("rep", "ctx"), None, "fsdp"),
        P(("rep", "ctx"), "fsdp"),
        P("rep"),
        P(None, "fsdp"),
        P(None, None, "fsdp"),
        P(None, "fsdp"),
        P(None, None, "fsdp"),
    )
    out_specs = (
        P(("rep", "ctx"), None, "fsdp"),
        P(("rep", "ctx"), None, "fsdp"),
        P(("rep", "ctx"), None, "fsdp"),
        P("rep", "fsdp"),
        P("rep", None, "fsdp"),
        P("rep", "fsdp"),
        P("rep", None, "fsdp"),
    )
    return jax.shard_map(
        on_device, mesh=mesh, in_specs=in_specs, out_specs=out_specs, check_vma=False
    )
```

```python
import functools
import math

import jax
import jax.numpy as jnp
from jax import lax
from jax.experimental import pallas as pl
from jax.experimental.pallas import tpu as pltpu
from jax.sharding import PartitionSpec as P

MESH = pl.DeviceIdType.MESH
MASKED = -1e30

QUERY_HEADS = 32
KEY_VALUE_HEADS = 4
HEAD_SIZE = 128
GROUP = 1024


adapter_scale = 2.0


def attention_kernel(
    ctx,
    devs,
    with_adapters,
    q_ref,
    do_ref,
    k_ref,
    v_ref,
    seg_ref,
    *refs,
):
    if with_adapters:
        x_ref, q_down_ref, v_down_ref, q_up_ref, v_up_ref = refs[:5]
        dq_ref, gk_ref, gv_ref, qd_out, qu_out, vd_out, vu_out = refs[5:12]
        refs = refs[12:]
    else:
        dq_ref, gk_ref, gv_ref = refs[:3]
        refs = refs[3:]
    kv_buf, part_send, part_recv, own_part, p_scr, w_scr, bias, g_send, g_recv, r_send, r_recv = (
        refs[:11]
    )
    if with_adapters:
        q_down, v_down, q_up, v_up, q_act = refs[11:16]
        q_bufs, v_bufs = refs[16:26], refs[26:]
    tok = k_ref.shape[1]
    kv_heads = k_ref.shape[2] // HEAD_SIZE
    repeat = q_ref.shape[2] // k_ref.shape[2]
    group_width = repeat * HEAD_SIZE
    mid = devs // 2
    scaling = HEAD_SIZE ** (-0.5)
    exponent = scaling * math.log2(math.e)
    me = lax.axis_index("ctx")
    p0 = lax.rem(me, devs)
    small = p0 // mid
    big = 1 - small
    ps = lax.rem(p0, mid)

    def ahead(d):
        return lax.rem(me + d, ctx)

    def behind(d):
        return lax.rem(me + ctx - d, ctx)

    for h in range(2):
        for g in range(kv_heads):
            lanes = slice(g * HEAD_SIZE, (g + 1) * HEAD_SIZE)
            kv_buf[h, 0, g, :, :HEAD_SIZE] = k_ref[h, :, lanes]
            kv_buf[h, 0, g, :, HEAD_SIZE:] = v_ref[h, :, lanes]

    barrier = pltpu.get_barrier_semaphore()
    for d in range(1, devs):
        pl.semaphore_signal(barrier, inc=1, device_id={"ctx": ahead(d)}, device_id_type=MESH)
        pl.semaphore_signal(barrier, inc=1, device_id={"ctx": behind(d)}, device_id_type=MESH)
    planes = ctx // devs
    plane = me // devs
    far = range(1, planes) if with_adapters else range(0)
    for j in far:
        pl.semaphore_signal(
            barrier,
            inc=1,
            device_id={"ctx": lax.rem(me + j * devs, ctx)},
            device_id_type=MESH,
        )
    pl.semaphore_wait(barrier, 2 * (devs - 1) + len(far))

    def gather_copy(h, d):
        return pltpu.make_async_remote_copy(
            src_ref=kv_buf.at[h, 0],
            dst_ref=kv_buf.at[h, d],
            send_sem=g_send.at[h, d],
            recv_sem=g_recv.at[h, d],
            device_id={"ctx": ahead(d)},
            device_id_type=MESH,
        )

    def return_copy(which, h, g, d):
        return pltpu.make_async_remote_copy(
            src_ref=part_send.at[which, h, g, d],
            dst_ref=part_recv.at[which, h, g, d],
            send_sem=r_send.at[which, h, g, d],
            recv_sem=r_recv.at[which, h, g, d],
            device_id={"ctx": behind(d)},
            device_id_type=MESH,
        )

    for d in range(1, mid):

        @pl.when(ps + d < mid)
        def _():
            gather_copy(small, d).start()

    for d in range(1, devs):

        @pl.when((ps + d >= mid) & (ps + d < devs))
        def _():
            gather_copy(small, d).start()

    for d in range(1, mid):

        @pl.when(ps + d < mid)
        def _():
            gather_copy(big, d).start()

    for d in range(1, mid):

        @pl.when(d > ps)
        def _():
            kv_buf[small, d] = jnp.zeros(kv_buf.shape[2:], kv_buf.dtype)

        @pl.when(d > ps)
        def _():
            kv_buf[big, mid + d] = jnp.zeros(kv_buf.shape[2:], kv_buf.dtype)

    own_ids = jnp.transpose(
        jnp.broadcast_to(seg_ref[pl.ds(me, 1), :].astype(jnp.float32), (tok, tok))
    )
    rows = lax.broadcasted_iota(jnp.int32, (tok, tok), 0)
    columns = lax.broadcasted_iota(jnp.int32, (tok, tok), 1)
    for d in range(devs):
        ids = seg_ref[pl.ds(behind(d), 1), :].astype(jnp.float32)
        block = jnp.where(own_ids == ids, 0.0, MASKED)
        if d == 0:
            block = jnp.where(columns <= rows, block, MASKED)
        bias[1, :, d * tok : (d + 1) * tok] = jnp.where(d <= ps + mid, block, MASKED)
        if d < mid:
            bias[0, :, d * tok : (d + 1) * tok] = jnp.where(d <= ps, block, MASKED)

    def within(j):
        return lax.rem(p0 + j, devs)

    def scatter_copy(bufs, j):
        part, landed, s_send, s_recv = bufs[0], bufs[1], bufs[4], bufs[5]
        return pltpu.make_async_remote_copy(
            src_ref=part.at[within(j)],
            dst_ref=landed.at[j],
            send_sem=s_send.at[j],
            recv_sem=s_recv.at[j],
            device_id={"ctx": plane * devs + within(j)},
            device_id_type=MESH,
        )

    def plane_copy(bufs, j):
        across, s_send, s_recv = bufs[2], bufs[6], bufs[7]
        return pltpu.make_async_remote_copy(
            src_ref=across.at[plane],
            dst_ref=across.at[plane],
            send_sem=s_send.at[j],
            recv_sem=s_recv.at[j],
            device_id={"ctx": lax.rem(me + j * devs, ctx)},
            device_id_type=MESH,
        )

    def spread_copy(bufs, j):
        whole, s_send, s_recv = bufs[3], bufs[8], bufs[9]
        return pltpu.make_async_remote_copy(
            src_ref=whole.at[p0],
            dst_ref=whole.at[p0],
            send_sem=s_send.at[j],
            recv_sem=s_recv.at[j],
            device_id={"ctx": plane * devs + within(j)},
            device_id_type=MESH,
        )

    def start_scatter(bufs):
        for j in range(1, devs):
            scatter_copy(bufs, j).start()

    def start_planes(bufs):
        total = bufs[0][p0].astype(jnp.float32)
        for j in range(1, devs):
            scatter_copy(bufs, j).wait_recv()
            total = total + bufs[1][j].astype(jnp.float32)
        bufs[2][plane] = total.astype(jnp.bfloat16)
        for j in range(1, planes):
            plane_copy(bufs, j).start()

    def start_spread(bufs):
        for j in range(1, planes):
            plane_copy(bufs, j).wait_recv()
        total = bufs[2][0].astype(jnp.float32)
        for j in range(1, planes):
            total = total + bufs[2][j].astype(jnp.float32)
        bufs[3][p0] = total.astype(jnp.bfloat16)
        for j in range(1, devs):
            spread_copy(bufs, j).start()

    def finish(bufs, down_out, up_out, up_pieces):
        for j in range(1, devs):
            spread_copy(bufs, j).wait_recv()
        width = down_out.shape[1] // devs
        up_width = 2 * up_out.shape[2] // up_pieces
        for p in range(devs):
            down_out[:, p * width : (p + 1) * width] = adapter_scale * bufs[3][
                p, :, :width
            ].astype(jnp.float32)
            if p < up_pieces:
                h, at = p // (up_pieces // 2), p % (up_pieces // 2)
                up_out[:, h, at * up_width : (at + 1) * up_width] = adapter_scale * bufs[3][
                    p, :, width:
                ].astype(jnp.float32)
        for j in range(1, devs):
            scatter_copy(bufs, j).wait_send()
            spread_copy(bufs, j).wait_send()
        for j in range(1, planes):
            plane_copy(bufs, j).wait_send()

    def project_down(bufs, act):
        width = x_ref.shape[1] // devs
        for p in range(devs):
            bufs[0][p, :, :width] = jnp.dot(
                act, x_ref[:, p * width : (p + 1) * width], preferred_element_type=jnp.float32
            ).astype(jnp.bfloat16)

    if with_adapters:
        for source, act in ((q_down_ref, q_down), (v_down_ref, v_down)):
            act[...] = lax.dot_general(
                source[...],
                x_ref[...],
                (((1,), (1,)), ((), ())),
                preferred_element_type=jnp.float32,
            ).astype(jnp.bfloat16)
        for h in range(2):
            q_up[h] = q_up_ref[:, h, :]
            v_up[h] = v_up_ref[:, h, :]
        q_act[...] = jnp.zeros_like(q_act)
        rank = q_act.shape[0]
        for p in range(2 * kv_heads, devs):
            v_bufs[0][p, :, x_ref.shape[1] // devs :] = jnp.zeros((rank, HEAD_SIZE), jnp.bfloat16)

    def stacked(ref, h, g):
        return jnp.concatenate(
            [
                ref[h, :, g * group_width + r * HEAD_SIZE : g * group_width + (r + 1) * HEAD_SIZE]
                for r in range(repeat)
            ],
            axis=0,
        )

    def send_parts(which, total, h, g, slots, limit):
        for d in range(slots):
            block = jnp.transpose(total[:, d * tok : (d + 1) * tok])
            if d == 0:
                own_part[which, h, g] = block
            else:
                part_send[which, h, g, d] = block.astype(jnp.bfloat16)
        for d in range(1, slots):

            @pl.when(d < limit)
            def _():
                return_copy(which, h, g, d).start()

    def probabilities(h, g, slots, limit):
        keys = slots * tok
        k = kv_buf[h, :slots, g, :, :HEAD_SIZE].reshape(keys, HEAD_SIZE)

        def one_head(r, inner):
            lanes = pl.ds(pl.multiple_of(g * group_width + r * HEAD_SIZE, HEAD_SIZE), HEAD_SIZE)
            at = pl.ds(pl.multiple_of(r * tok, tok), tok)
            s = lax.dot_general(
                q_ref[h, :, lanes],
                k,
                (((1,), (1,)), ((), ())),
                preferred_element_type=jnp.float32,
            )
            t = s * exponent + bias[int(slots == devs), :, :keys]
            e = jnp.exp2(t - jnp.max(t, axis=1, keepdims=True))
            w = e * (1.0 / jnp.sum(e, axis=1, keepdims=True))
            w_scr[g, at, :keys] = w
            p_scr[at, :keys] = w.astype(jnp.bfloat16)
            return inner

        lax.fori_loop(0, repeat, one_head, 0, unroll=8)
        dv = lax.dot_general(
            stacked(do_ref, h, g),
            p_scr[:, :keys],
            (((0,), (0,)), ((), ())),
            preferred_element_type=jnp.float32,
        )
        send_parts(1, dv, h, g, slots, limit)

    def score_gradients(h, g, slots, limit):
        keys = slots * tok
        k = kv_buf[h, :slots, g, :, :HEAD_SIZE].reshape(keys, HEAD_SIZE)
        v = kv_buf[h, :slots, g, :, HEAD_SIZE:].reshape(keys, HEAD_SIZE)

        def one_head(r, inner):
            lanes = pl.ds(pl.multiple_of(g * group_width + r * HEAD_SIZE, HEAD_SIZE), HEAD_SIZE)
            at = pl.ds(pl.multiple_of(r * tok, tok), tok)
            dp = lax.dot_general(
                do_ref[h, :, lanes],
                v,
                (((1,), (1,)), ((), ())),
                preferred_element_type=jnp.float32,
            )
            w = w_scr[g, at, :keys]
            low = w.astype(jnp.bfloat16).astype(jnp.float32)
            dot = jnp.sum(low * dp, axis=1, keepdims=True)
            ds = (w * (dp - dot)).astype(jnp.bfloat16)
            p_scr[at, :keys] = ds
            dq = jnp.dot(ds, k, preferred_element_type=jnp.float32) * scaling
            dq_ref[h, :, lanes] = dq.astype(jnp.bfloat16)
            return inner

        lax.fori_loop(0, repeat, one_head, 0, unroll=8)
        if with_adapters:
            lanes = slice(g * group_width, (g + 1) * group_width)
            dq_all = dq_ref[h, :, lanes]
            q_act[...] += lax.dot_general(
                q_up[h, :, lanes],
                dq_all,
                (((1,), (1,)), ((), ())),
                preferred_element_type=jnp.float32,
            )
            up = jnp.dot(q_down[...], dq_all, preferred_element_type=jnp.float32)
            up = up.astype(jnp.bfloat16)
            width = x_ref.shape[1] // devs
            each = group_width * 2 * kv_heads // devs
            pieces = group_width // each
            for i in range(pieces):
                q_bufs[0][(h * kv_heads + g) * pieces + i, :, width:] = up[
                    :, i * each : (i + 1) * each
                ]
        dk = lax.dot_general(
            stacked(q_ref, h, g),
            p_scr[:, :keys],
            (((0,), (0,)), ((), ())),
            preferred_element_type=jnp.float32,
        )
        send_parts(0, dk * scaling, h, g, slots, limit)

    def collect(which, out_ref):
        for d in range(1, devs):
            for g in range(kv_heads):

                @pl.when(ps + d < devs)
                def _():
                    return_copy(which, small, g, d).wait_recv()
                    own_part[which, small, g] += part_recv[which, small, g, d].astype(jnp.float32)

        for d in range(1, mid):
            for g in range(kv_heads):

                @pl.when(ps + d < mid)
                def _():
                    return_copy(which, big, g, d).wait_recv()
                    own_part[which, big, g] += part_recv[which, big, g, d].astype(jnp.float32)

        for h in range(2):
            for g in range(kv_heads):
                out_ref[h, :, g * HEAD_SIZE : (g + 1) * HEAD_SIZE] = own_part[which, h, g].astype(
                    jnp.bfloat16
                )

    def value_adapter():
        v_act = jnp.zeros(q_act.shape, jnp.float32)
        for h in range(2):
            v_act = v_act + lax.dot_general(
                v_up[h], gv_ref[h], (((1,), (1,)), ((), ())), preferred_element_type=jnp.float32
            )
            up = jnp.dot(v_down[...], gv_ref[h], preferred_element_type=jnp.float32)
            for g in range(kv_heads):
                v_bufs[0][h * kv_heads + g, :, x_ref.shape[1] // devs :] = up[
                    :, g * HEAD_SIZE : (g + 1) * HEAD_SIZE
                ].astype(jnp.bfloat16)
        project_down(v_bufs, v_act.astype(jnp.bfloat16))
        start_scatter(v_bufs)

    for d in range(1, mid):

        @pl.when(d <= ps)
        def _():
            gather_copy(small, d).wait_recv()

    for g in range(kv_heads):
        probabilities(small, g, mid, ps + 1)
    for g in range(kv_heads):
        score_gradients(small, g, mid, ps + 1)

    for d in range(1, devs):

        @pl.when(d <= ps + mid)
        def _():
            gather_copy(big, d).wait_recv()

    for g in range(kv_heads):
        probabilities(big, g, devs, ps + mid + 1)
    for g in range(kv_heads):
        score_gradients(big, g, devs, ps + mid + 1)
        if g == 0:
            collect(1, gv_ref)
            if with_adapters:
                value_adapter()

    if with_adapters:
        project_down(q_bufs, q_act[...].astype(jnp.bfloat16))
        start_scatter(q_bufs)
        start_planes(v_bufs)
        start_planes(q_bufs)
        start_spread(v_bufs)
        start_spread(q_bufs)
    collect(0, gk_ref)
    if with_adapters:
        finish(v_bufs, vd_out, vu_out, 2 * kv_heads)
        finish(q_bufs, qd_out, qu_out, devs)

    for d in range(1, devs):

        @pl.when(ps + d < devs)
        def _():
            gather_copy(small, d).wait_send()

        @pl.when(d <= ps + mid)
        def _():
            for which in range(2):
                for g in range(kv_heads):
                    return_copy(which, big, g, d).wait_send()

    for d in range(1, mid):

        @pl.when(ps + d < mid)
        def _():
            gather_copy(big, d).wait_send()

        @pl.when(d <= ps)
        def _():
            for which in range(2):
                for g in range(kv_heads):
                    return_copy(which, small, g, d).wait_send()


def attention_backward(q, do, k, v, seg, devs, adapters=None):
    tok, width = q.shape[1], q.shape[2]
    kv_heads = k.shape[2] // HEAD_SIZE
    repeat = width // k.shape[2]
    ctx = lax.axis_size("ctx")
    planes = ctx // devs
    bf16, f32 = jnp.bfloat16, jnp.float32
    vmem = pl.BlockSpec(memory_space=pltpu.VMEM)
    operands = (q, do, k, v, seg)
    results = [jax.ShapeDtypeStruct(a.shape, bf16) for a in (q, k, v)]
    scratch = [
        pltpu.VMEM((2, devs, kv_heads, tok, 2 * HEAD_SIZE), bf16),
        pltpu.VMEM((2, 2, kv_heads, devs, tok, HEAD_SIZE), bf16),
        pltpu.VMEM((2, 2, kv_heads, devs, tok, HEAD_SIZE), bf16),
        pltpu.VMEM((2, 2, kv_heads, tok, HEAD_SIZE), f32),
        pltpu.VMEM((repeat * tok, devs * tok), bf16),
        pltpu.VMEM((kv_heads, repeat * tok, devs * tok), f32),
        pltpu.VMEM((2, tok, devs * tok), f32),
        pltpu.SemaphoreType.DMA((2, devs)),
        pltpu.SemaphoreType.DMA((2, devs)),
        pltpu.SemaphoreType.DMA((2, 2, kv_heads, devs)),
        pltpu.SemaphoreType.DMA((2, 2, kv_heads, devs)),
    ]
    if adapters is not None:
        operands = operands + adapters
        x, q_down, v_down, q_up, v_up = adapters
        rank = q_down.shape[0]
        results += [jax.ShapeDtypeStruct(a.shape, f32) for a in (q_down, q_up, v_down, v_up)]
        scratch += [
            pltpu.VMEM((rank, tok), bf16),
            pltpu.VMEM((rank, tok), bf16),
            pltpu.VMEM((2, rank, q.shape[2]), bf16),
            pltpu.VMEM((2, rank, k.shape[2]), bf16),
            pltpu.VMEM((rank, tok), f32),
        ]
        for columns in ((x.shape[1] + 2 * width) // devs, x.shape[1] // devs + HEAD_SIZE):
            scratch += [
                pltpu.VMEM((n, rank, columns), bf16) for n in (devs, devs, planes, devs)
            ]
            scratch += [
                pltpu.SemaphoreType.DMA((n,)) for n in (devs, devs, planes, planes, devs, devs)
            ]
    return pl.pallas_call(
        functools.partial(attention_kernel, ctx, devs, adapters is not None),
        out_shape=tuple(results),
        in_specs=[vmem] * len(operands),
        out_specs=(vmem,) * len(results),
        scratch_shapes=scratch,
        compiler_params=pltpu.CompilerParams(
            collective_id=0, has_side_effects=True, vmem_limit_bytes=52 * 1024 * 1024
        ),
        name="attention_backward",
    )(*operands)


def paired_kernel(
    chips,
    span,
    q_hbm,
    do_hbm,
    k_hbm,
    v_hbm,
    seg_hbm,
    x_ref,
    q_down_hbm,
    v_down_hbm,
    q_up_hbm,
    v_up_hbm,
    dq_out,
    gk_out,
    gv_out,
    q_sums,
    q_other,
    v_sums,
    v_other,
    q_raw,
    do_raw,
    k_raw,
    v_raw,
    seg_ref,
    q_down_ref,
    v_down_ref,
    q_up_ref,
    v_up_ref,
    q_away,
    do_away,
    k_ref,
    v_ref,
    dq_land,
    q_up,
    x_away,
    qb,
    dob,
    kb,
    vb,
    xb,
    dqb,
    p_small,
    p_big,
    bias,
    part_send,
    part_recv,
    acc,
    sib_part,
    down_mine,
    down_theirs,
    act_mine,
    act_theirs,
    mixed_mine,
    mixed_theirs,
    acts,
    q_parts,
    q_land,
    q_across,
    v_parts,
    v_land,
    v_across,
    local_sem,
    swap_send,
    swap_recv,
    g_send,
    g_recv,
    r_send,
    r_recv,
    a_send,
    a_recv,
):
    bf16, f32 = jnp.bfloat16, jnp.float32
    tok = q_raw.shape[0]
    pair = 2 * tok
    width = qb.shape[2]
    heads = width // HEAD_SIZE
    columns = xb.shape[1]
    cube = q_parts.shape[0]
    cubes = chips // cube
    each = columns // cube
    up_each = 2 * width // cube
    rank = acts.shape[1]
    mid = span // 2
    scaling = HEAD_SIZE ** (-0.5)
    exponent = scaling * math.log2(math.e)
    me = lax.axis_index("ctx")
    chip = me // 2
    core = lax.rem(me, 2)
    spot = lax.rem(chip, cube)
    mine = chip // cube
    other = 1 - core
    place = lax.rem(chip, span)
    small = place // mid
    big = 1 - small
    ps = lax.rem(place, mid)

    def ahead(d):
        return lax.rem(chip + d, chips)

    def behind(d):
        return lax.rem(chip + chips - d, chips)

    def within(j):
        return lax.rem(spot + j, cube)

    def device(chip_at, core_at):
        return {"ctx": 2 * chip_at + core_at}

    sibling = device(chip, other)

    def rows(at):
        return pl.ds(pl.multiple_of(at * tok, tok), tok)

    def half_columns(at, size):
        return pl.ds(pl.multiple_of(at * size, size), size)

    barrier = pltpu.get_barrier_semaphore()
    pl.semaphore_signal(barrier, inc=1, device_id=sibling, device_id_type=MESH)
    for j in range(1, cube):
        pl.semaphore_signal(
            barrier, inc=1, device_id=device(mine * cube + within(j), core), device_id_type=MESH
        )
    for j in range(1, cubes):
        pl.semaphore_signal(
            barrier, inc=1, device_id=device(ahead(j * cube), core), device_id_type=MESH
        )
    for d in range(1, span):
        for to in range(2):
            pl.semaphore_signal(
                barrier, inc=1, device_id=device(ahead(d), to), device_id_type=MESH
            )
            pl.semaphore_signal(
                barrier, inc=1, device_id=device(behind(d), to), device_id_type=MESH
            )

    staged = [
        pltpu.make_async_copy(src, dst, local_sem.at[i])
        for i, (src, dst) in enumerate(
            (
                (k_hbm, k_raw),
                (v_hbm, v_raw),
                (q_hbm, q_raw),
                (do_hbm, do_raw),
                (seg_hbm, seg_ref),
                (x_ref.at[:, half_columns(core, columns)], xb.at[rows(core)]),
                (q_down_hbm, q_down_ref),
                (v_down_hbm, v_down_ref),
                (q_up_hbm, q_up_ref),
                (v_up_hbm, v_up_ref),
                (x_ref.at[:, half_columns(other, columns)], x_away),
            )
        )
    ]
    for copy in staged:
        copy.start()

    def swap_columns(row):
        return pltpu.make_async_remote_copy(
            src_ref=x_away,
            dst_ref=xb.at[rows(row)],
            send_sem=swap_send.at[4],
            recv_sem=swap_recv.at[4],
            device_id=sibling,
            device_id_type=MESH,
        )

    def swap_half(h, i, row):
        return pltpu.make_async_remote_copy(
            src_ref=(q_away, do_away)[i].at[h],
            dst_ref=(qb, dob)[i].at[h, rows(row)],
            send_sem=swap_send.at[2 * h + i],
            recv_sem=swap_recv.at[2 * h + i],
            device_id=sibling,
            device_id_type=MESH,
        )

    def gather_copy(which, h, d, to, row):
        src = (k_ref, v_ref)[which].at[h, :, half_columns(to, HEAD_SIZE)]
        return pltpu.make_async_remote_copy(
            src_ref=src,
            dst_ref=(kb, vb)[which].at[h, d, rows(row)],
            send_sem=g_send.at[which, h, d, to],
            recv_sem=g_recv.at[which, h, d, row],
            device_id=device(ahead(d), to),
            device_id_type=MESH,
        )

    def gather_start(which, h, d):
        for to in range(2):
            gather_copy(which, h, d, to, core).start()

    def gather_wait(which, h, d):
        for row in range(2):
            gather_copy(which, h, d, row, row).wait_recv()

    def gather_sent(which, h, d):
        for to in range(2):
            gather_copy(which, h, d, to, core).wait_send()

    @pl.when(ps == 0)
    def _():
        for buf in (kb, vb):
            buf[small, 1] = jnp.zeros(buf.shape[2:], bf16)
            buf[big, span - 1] = jnp.zeros(buf.shape[2:], bf16)

    to_row = lax.broadcasted_iota(jnp.int32, (pair, pair), 0)
    from_row = lax.broadcasted_iota(jnp.int32, (pair, pair), 1)
    parting = jnp.where(from_row == 2 * lax.rem(to_row, tok) + to_row // tok, 1.0, 0.0).astype(bf16)

    def parted(raw, lanes):
        return jnp.dot(
            parting, raw[:, :, lanes].reshape(pair, HEAD_SIZE), preferred_element_type=f32
        ).astype(bf16)

    for i, (raw, ref, buf) in enumerate(((k_raw, k_ref, kb), (v_raw, v_ref, vb))):
        staged[i].wait()
        for head in range(2):
            lanes = slice(head * HEAD_SIZE, (head + 1) * HEAD_SIZE)
            both = parted(raw, lanes)
            for h in range(2):
                ref[h, :, lanes] = both[h * tok : (h + 1) * tok]
        for h in range(2):
            buf[h, 0, rows(core)] = ref[h, :, half_columns(core, HEAD_SIZE)]
    def part_rows(i):
        raw, buf, away = ((q_raw, qb, q_away), (do_raw, dob, do_away))[i]
        staged[2 + i].wait()
        for j in range(heads):
            lanes = slice(j * HEAD_SIZE, (j + 1) * HEAD_SIZE)
            for at in (other, core):
                start = pl.multiple_of(at * width + j * HEAD_SIZE, HEAD_SIZE)
                both = parted(raw, pl.ds(start, HEAD_SIZE))
                for h in range(2):
                    block = both[h * tok : (h + 1) * tok]
                    if at is core:
                        buf[h, rows(core), lanes] = block
                    else:
                        away[h, :, lanes] = block

    part_rows(0)

    pl.semaphore_wait(barrier, cube + cubes - 1 + 4 * (span - 1))

    def gather_all(which):
        for d in range(1, mid):

            @pl.when(ps + d < mid)
            def _():
                gather_start(which, small, d)

        for d in range(1, span):

            @pl.when((ps + d >= mid) & (ps + d < span))
            def _():
                gather_start(which, small, d)

        for d in range(1, mid):

            @pl.when(ps + d < mid)
            def _():
                gather_start(which, big, d)

    gather_all(0)
    gather_copy(0, small, 0, other, core).start()
    swap_half(small, 0, core).start()
    gather_copy(0, big, 0, other, core).start()
    swap_half(big, 0, core).start()
    staged[10].wait()
    swap_columns(core).start()
    gather_all(1)
    part_rows(1)
    for h in (small, big):
        swap_half(h, 1, core).start()
        gather_copy(1, h, 0, other, core).start()

    staged[4].wait()

    def chip_ids(at):
        first = seg_ref[pl.ds(2 * at, 1), :]
        second = seg_ref[pl.ds(2 * at + 1, 1), :]
        return jnp.concatenate([first, second], axis=1).astype(f32)

    own_ids = jnp.transpose(jnp.broadcast_to(chip_ids(chip), (pair, pair)))
    row = lax.broadcasted_iota(jnp.int32, (pair, pair), 0)
    column = lax.broadcasted_iota(jnp.int32, (pair, pair), 1)
    for d in range(span):
        block = jnp.where(own_ids == chip_ids(behind(d)), 0.0, MASKED)
        if d == 0:
            block = jnp.where(column <= row, block, MASKED)
        bias[1, :, d * pair : (d + 1) * pair] = jnp.where(d <= ps + mid, block, MASKED)
        if d < mid:
            bias[0, :, d * pair : (d + 1) * pair] = jnp.where(d <= ps, block, MASKED)

    def exchange(src, dst, i):
        return pltpu.make_async_remote_copy(
            src_ref=src,
            dst_ref=dst,
            send_sem=swap_send.at[i],
            recv_sem=swap_recv.at[i],
            device_id=sibling,
            device_id_type=MESH,
        )

    down_swap = exchange(down_mine, down_theirs, 5)
    act_swap = exchange(act_mine, act_theirs, 6)
    mixed_swap = exchange(mixed_mine, mixed_theirs, 7)

    def part_swap(which, h):
        return pltpu.make_async_remote_copy(
            src_ref=sib_part.at[which, h],
            dst_ref=acc.at[which, h, core],
            send_sem=swap_send.at[8 + 2 * which + h],
            recv_sem=swap_recv.at[8 + 2 * which + h],
            device_id=sibling,
            device_id_type=MESH,
        )

    def part_wait(which, h):
        return pltpu.make_async_remote_copy(
            src_ref=sib_part.at[which, h],
            dst_ref=acc.at[which, h, other],
            send_sem=swap_send.at[8 + 2 * which + h],
            recv_sem=swap_recv.at[8 + 2 * which + h],
            device_id=sibling,
            device_id_type=MESH,
        )

    def dq_swap(h):
        return exchange(dqb.at[h, rows(other)], dq_land.at[h], 12 + h)

    def scatter_copy(bufs, j):
        s, parts, land = bufs[:3]
        return pltpu.make_async_remote_copy(
            src_ref=parts.at[within(j)],
            dst_ref=land.at[j],
            send_sem=a_send.at[3 * s, j],
            recv_sem=a_recv.at[3 * s, j],
            device_id=device(mine * cube + within(j), core),
            device_id_type=MESH,
        )

    def across_copy(bufs, j, source):
        s, across = bufs[0], bufs[3]
        return pltpu.make_async_remote_copy(
            src_ref=across.at[source],
            dst_ref=across.at[source],
            send_sem=a_send.at[3 * s + 1, j],
            recv_sem=a_recv.at[3 * s + 1, j],
            device_id=device(ahead(j * cube), core),
            device_id_type=MESH,
        )

    def spread_copy(bufs, j, source):
        s, sums = bufs[0], bufs[4]
        return pltpu.make_async_remote_copy(
            src_ref=sums.at[source],
            dst_ref=sums.at[source],
            send_sem=a_send.at[3 * s + 2, j],
            recv_sem=a_recv.at[3 * s + 2, j],
            device_id=device(mine * cube + within(j), core),
            device_id_type=MESH,
        )

    q_set = (0, q_parts, q_land, q_across, q_sums, q_other)
    v_set = (1, v_parts, v_land, v_across, v_sums, v_other)

    def start_scatter(bufs):
        for j in range(1, cube):
            scatter_copy(bufs, j).start()

    def start_across(bufs):
        total = bufs[1][spot].astype(f32)
        for j in range(1, cube):
            scatter_copy(bufs, j).wait_recv()
            total = total + bufs[2][j].astype(f32)
        bufs[3][mine] = total.astype(bf16)
        for j in range(1, cubes):
            across_copy(bufs, j, mine).start()

    def start_spread(bufs):
        for j in range(1, cubes):
            across_copy(bufs, j, lax.rem(mine + cubes - j, cubes)).wait_recv()
        total = bufs[3][0].astype(f32)
        for j in range(1, cubes):
            total = total + bufs[3][j].astype(f32)
        bufs[4][spot] = total.astype(bf16)
        for j in range(1, cube):
            spread_copy(bufs, j, spot).start()

    def hand_copy(bufs):
        return exchange(bufs[4], bufs[5], 14 + bufs[0])

    def start_hand(bufs):
        for j in range(1, cube):
            spread_copy(bufs, j, lax.rem(spot + cube - j, cube)).wait_recv()
        hand_copy(bufs).start()

    def finish(bufs):
        hand_copy(bufs).wait()
        for j in range(1, cube):
            scatter_copy(bufs, j).wait_send()
            spread_copy(bufs, j, spot).wait_send()
        for j in range(1, cubes):
            across_copy(bufs, j, mine).wait_send()

    def project_down(parts, act):
        for i in range(cube):
            parts[i, :, :each] = jnp.dot(
                act, xb[:, i * each : (i + 1) * each], preferred_element_type=f32
            ).astype(bf16)

    def return_copy(which, h, d, to, head):
        return pltpu.make_async_remote_copy(
            src_ref=part_send.at[which, h, d, rows(to)],
            dst_ref=part_recv.at[which, h, d, head],
            send_sem=r_send.at[which, h, d, to],
            recv_sem=r_recv.at[which, h, d, head],
            device_id=device(behind(d), to),
            device_id_type=MESH,
        )

    def send_parts(which, total, h, slots, limit):
        for d in reversed(range(slots)):
            block = jnp.transpose(total[:, d * pair : (d + 1) * pair])
            if d == 0:
                acc[which, h, core] = jnp.where(core == 0, block[:tok], block[tok:])
                sib_part[which, h] = jnp.where(core == 0, block[tok:], block[:tok])
                part_swap(which, h).start()
            else:
                part_send[which, h, d] = block.astype(bf16)

                @pl.when(d < limit)
                def _():
                    for to in range(2):
                        return_copy(which, h, d, to, core).start()

    def stacked(ref, h):
        return jnp.concatenate(
            [ref[h, :, j * HEAD_SIZE : (j + 1) * HEAD_SIZE] for j in range(heads)], axis=0
        )

    def head_lanes(j):
        return pl.ds(pl.multiple_of(j * HEAD_SIZE, HEAD_SIZE), HEAD_SIZE)

    def head_rows(j):
        return pl.ds(pl.multiple_of(j * pair, pair), pair)

    def probabilities(h, p_ref, slots, limit):
        keys = slots * pair
        k = kb[h, :slots].reshape(keys, HEAD_SIZE)

        def one_head(j, inner):
            s = lax.dot_general(
                qb[h, :, head_lanes(j)], k, (((1,), (1,)), ((), ())), preferred_element_type=f32
            )
            t = s * exponent + bias[int(slots == span), :, :keys]
            e = jnp.exp2(t - jnp.max(t, axis=1, keepdims=True))
            w = e * (1.0 / jnp.sum(e, axis=1, keepdims=True))
            p_ref[head_rows(j)] = w.astype(bf16)
            return inner

        lax.fori_loop(0, heads, one_head, 0, unroll=heads)

    def value_part(h, p_ref, slots, limit):
        dv = lax.dot_general(
            stacked(dob, h), p_ref[...], (((0,), (0,)), ((), ())), preferred_element_type=f32
        )
        send_parts(1, dv, h, slots, limit)

    def score_gradients(h, p_ref, slots, first, last):
        keys = slots * pair
        k = kb[h, :slots].reshape(keys, HEAD_SIZE)
        v = vb[h, :slots].reshape(keys, HEAD_SIZE)

        def scores_of(j):
            dp = lax.dot_general(
                dob[h, :, head_lanes(j)], v, (((1,), (1,)), ((), ())), preferred_element_type=f32
            )
            w = p_ref[head_rows(j)].astype(f32)
            dot = jnp.sum(w * dp, axis=1, keepdims=True)
            p_ref[head_rows(j)] = (w * (dp - dot)).astype(bf16)

        def queries_of(j):
            dq = jnp.dot(p_ref[head_rows(j)], k, preferred_element_type=f32) * scaling
            dqb[h, :, head_lanes(j)] = dq.astype(bf16)

        def one_head(j, inner):
            scores_of(j)
            queries_of(j - 1)
            return inner

        scores_of(first)
        lax.fori_loop(first + 1, last, one_head, 0, unroll=last - first - 1)
        queries_of(last - 1)
        if last == heads:
            dq_swap(h).start()

    def query_adapter(h):
        return lax.dot_general(
            q_up[h],
            dqb[h],
            (((1,), (1,)), ((), ())),
            preferred_element_type=f32,
        )

    def key_part(h, p_ref, slots, limit):
        dk = lax.dot_general(
            stacked(qb, h), p_ref[...], (((0,), (0,)), ((), ())), preferred_element_type=f32
        )
        send_parts(0, dk * scaling, h, slots, limit)

    def collect(which):
        for h in range(2):
            part_wait(which, h).wait_recv()
        for d in range(1, span):

            @pl.when(ps + d < span)
            def _():
                for head in range(2):
                    return_copy(which, small, d, head, head).wait_recv()
                    acc[which, small, head] += part_recv[which, small, d, head].astype(f32)

        for d in range(1, mid):

            @pl.when(ps + d < mid)
            def _():
                for head in range(2):
                    return_copy(which, big, d, head, head).wait_recv()
                    acc[which, big, head] += part_recv[which, big, d, head].astype(f32)

        return [
            jnp.concatenate([acc[which, h, 0], acc[which, h, 1]], axis=1).astype(bf16)
            for h in range(2)
        ]

    def wait_swap(h, i):
        swap_half(h, i, other).wait_recv()

    for i in range(5, 10):
        staged[i].wait()
    for h in range(2):
        q_up[h] = q_up_ref[:, h, half_columns(core, width)]
    swap_columns(other).wait_recv()
    both_down = jnp.concatenate(
        [source[:, half_columns(core, columns)] for source in (q_down_ref, v_down_ref)], axis=0
    )
    both_acts = lax.dot_general(
        both_down, xb[...], (((1,), (1,)), ((), ())), preferred_element_type=f32
    )
    for i in range(2):
        down_mine[i] = both_acts[i * rank : (i + 1) * rank]
    down_swap.start()

    wait_swap(small, 0)
    gather_copy(0, small, 0, other, other).wait_recv()
    for d in range(1, mid):

        @pl.when(d <= ps)
        def _():
            gather_wait(0, small, d)

    probabilities(small, p_small, mid, ps + 1)
    wait_swap(small, 1)
    value_part(small, p_small, mid, ps + 1)

    wait_swap(big, 0)
    gather_copy(0, big, 0, other, other).wait_recv()
    for d in range(1, span):

        @pl.when(d <= ps + mid)
        def _():
            gather_wait(0, big, d)

    probabilities(big, p_big, span, ps + mid + 1)
    wait_swap(big, 1)
    value_part(big, p_big, span, ps + mid + 1)

    down_swap.wait()
    for i in range(2):
        acts[i] = (down_mine[i] + down_theirs[i]).astype(bf16)

    for h in (small, big):
        gather_copy(1, h, 0, other, other).wait_recv()
    for d in range(1, mid):

        @pl.when(d <= ps)
        def _():
            gather_wait(1, small, d)

    for d in range(1, span):

        @pl.when(d <= ps + mid)
        def _():
            gather_wait(1, big, d)

    score_gradients(small, p_small, mid, 0, heads)
    act_small = query_adapter(small)
    score_gradients(big, p_big, span, 0, heads)
    act_mine[...] = act_small + query_adapter(big)
    act_swap.start()
    for h in range(2):
        up = jnp.dot(acts[0], dqb[h], preferred_element_type=f32).astype(bf16)
        for i in range(cube // 2):
            q_parts[h * (cube // 2) + i, :, each:] = up[:, i * up_each : (i + 1) * up_each]
    act_swap.wait()
    project_down(q_parts, (act_mine[...] + act_theirs[...]).astype(bf16))
    start_scatter(q_set)

    gv = collect(1)
    v_act = jnp.zeros((rank, tok), f32)
    own_lanes = half_columns(core, tok)
    for h in range(2):
        v_act = v_act + lax.dot_general(
            v_up_ref[:, h, :], gv[h], (((1,), (1,)), ((), ())), preferred_element_type=f32
        )
        up = jnp.dot(acts[1, :, own_lanes], gv[h], preferred_element_type=f32)
        first, second = up[:, :HEAD_SIZE], up[:, HEAD_SIZE:]
        mixed_mine[1 + h] = jnp.where(core == 0, second, first)
        mixed_mine[3 + h] = jnp.where(core == 0, first, second)
    mixed_mine[0] = v_act
    mixed_swap.start()
    for h in range(2):
        gv_out[:, h, :] = gv[h]

    key_part(big, p_big, span, ps + mid + 1)

    mixed_swap.wait()
    acts[2, :, own_lanes] = mixed_mine[0].astype(bf16)
    acts[2, :, half_columns(other, tok)] = mixed_theirs[0].astype(bf16)
    for i in range(cube):
        if i < 2:
            v_parts[i, :, each:] = (mixed_mine[3 + i] + mixed_theirs[1 + i]).astype(bf16)
        else:
            v_parts[i, :, each:] = jnp.zeros((rank, HEAD_SIZE), bf16)
    project_down(v_parts, acts[2])
    start_scatter(v_set)

    start_across(q_set)
    key_part(small, p_small, mid, ps + 1)

    start_across(v_set)
    start_spread(q_set)
    start_spread(v_set)
    for h in range(2):
        dq_out[:, h, half_columns(core, width)] = dqb[h, rows(core)]
        dq_swap(h).wait_recv()
        dq_out[:, h, half_columns(other, width)] = dq_land[h]
    gk = collect(0)
    for h in range(2):
        gk_out[:, h, :] = gk[h]
    start_hand(q_set)
    start_hand(v_set)
    finish(q_set)
    finish(v_set)

    for h in range(2):
        dq_swap(h).wait_send()
        for i in range(2):
            swap_half(h, i, core).wait_send()
            part_swap(i, h).wait_send()
            gather_copy(i, h, 0, other, core).wait_send()
    swap_columns(core).wait_send()
    for which in range(2):
        for d in range(1, span):

            @pl.when(ps + d < span)
            def _():
                gather_sent(which, small, d)

            @pl.when(d <= ps + mid)
            def _():
                for to in range(2):
                    return_copy(which, big, d, to, core).wait_send()

        for d in range(1, mid):

            @pl.when(ps + d < mid)
            def _():
                gather_sent(which, big, d)

            @pl.when(d <= ps)
            def _():
                for to in range(2):
                    return_copy(which, small, d, to, core).wait_send()


def deliver_kernel(
    dq, gk, gv, q_sums, q_other, v_sums, v_other, *refs
):
    outs, totals, sems = refs[:7], refs[7:11], refs[11]
    core = lax.rem(lax.axis_index("ctx"), 2)
    copies = []

    def send(src, i):
        copies.append(pltpu.make_async_copy(src, outs[i], sems.at[i]))
        copies[-1].start()

    for i, src in enumerate((dq, gk, gv)):
        send(src, i)
    for i, (pair, pieces) in enumerate((((q_sums, q_other), None), ((v_sums, v_other), 2))):
        down, up = totals[2 * i], totals[2 * i + 1]
        cube = pair[0].shape[0]
        pieces = pieces or cube
        columns, width = down.shape[1] // 2, up.shape[2] // 2
        each, size = columns // cube, 2 * width // pieces
        for source, at in zip(pair, (core, 1 - core)):
            for p in range(cube):
                lanes = pl.ds(pl.multiple_of(at * columns + p * each, each), each)
                down[:, lanes] = adapter_scale * source[p, :, :each].astype(jnp.float32)
        send(down, 3 + 2 * i)
        for source, at in zip(pair, (core, 1 - core)):
            for p in range(pieces):
                h, step = p // (pieces // 2), p % (pieces // 2)
                lanes = pl.ds(pl.multiple_of(at * width + step * size, size), size)
                up[:, h, lanes] = adapter_scale * source[p, :, each:].astype(jnp.float32)
        send(up, 4 + 2 * i)
    for copy in copies:
        copy.wait()


def deliver(arrays, outs):
    vmem = pl.BlockSpec(memory_space=pltpu.VMEM)
    hbm = pl.BlockSpec(memory_space=pltpu.MemorySpace.HBM)
    return pl.pallas_call(
        deliver_kernel,
        out_shape=tuple(outs),
        in_specs=[vmem] * len(arrays),
        out_specs=(hbm,) * len(outs),
        scratch_shapes=[pltpu.VMEM(a.shape, a.dtype) for a in outs[3:]]
        + [pltpu.SemaphoreType.DMA((len(outs),))],
        name="deliver",
    )(*arrays)


def paired_backward(q, do, k, v, seg, x, q_down, v_down, q_up, v_up, span):
    tok, width = q.shape[0], q.shape[2] // 2
    pair = 2 * tok
    heads = width // HEAD_SIZE
    chips = lax.axis_size("ctx") // 2
    rank = q_down.shape[0]
    columns = x.shape[1] // 2
    bf16, f32 = jnp.bfloat16, jnp.float32
    vmem = pl.BlockSpec(memory_space=pltpu.VMEM)
    hbm = pl.BlockSpec(memory_space=pltpu.MemorySpace.HBM)
    cube = 2 * span
    q_piece = columns // cube + 2 * width // cube
    v_piece = columns // cube + HEAD_SIZE
    scratch = [pltpu.VMEM(a.shape, a.dtype) for a in (q, do, k, v, seg, q_down, v_down, q_up, v_up)]
    scratch += [
        pltpu.VMEM((2, tok, width), bf16),
        pltpu.VMEM((2, tok, width), bf16),
        pltpu.VMEM((2, tok, 2 * HEAD_SIZE), bf16),
        pltpu.VMEM((2, tok, 2 * HEAD_SIZE), bf16),
        pltpu.VMEM((2, tok, width), bf16),
        pltpu.VMEM((2, rank, width), bf16),
        pltpu.VMEM((tok, columns), bf16),
        pltpu.VMEM((2, pair, width), bf16),
        pltpu.VMEM((2, pair, width), bf16),
        pltpu.VMEM((2, span, pair, HEAD_SIZE), bf16),
        pltpu.VMEM((2, span, pair, HEAD_SIZE), bf16),
        pltpu.VMEM((pair, columns), bf16),
        pltpu.VMEM((2, pair, width), bf16),
        pltpu.VMEM((heads * pair, span // 2 * pair), bf16),
        pltpu.VMEM((heads * pair, span * pair), bf16),
        pltpu.VMEM((2, pair, span * pair), f32),
        pltpu.VMEM((2, 2, span, pair, HEAD_SIZE), bf16),
        pltpu.VMEM((2, 2, span, 2, tok, HEAD_SIZE), bf16),
        pltpu.VMEM((2, 2, 2, tok, HEAD_SIZE), f32),
        pltpu.VMEM((2, 2, tok, HEAD_SIZE), f32),
        pltpu.VMEM((2, rank, pair), f32),
        pltpu.VMEM((2, rank, pair), f32),
        pltpu.VMEM((rank, pair), f32),
        pltpu.VMEM((rank, pair), f32),
        pltpu.VMEM((5, rank, HEAD_SIZE), f32),
        pltpu.VMEM((5, rank, HEAD_SIZE), f32),
        pltpu.VMEM((3, rank, pair), bf16),
    ]
    for piece in (q_piece, v_piece):
        scratch += [
            pltpu.VMEM((n, rank, piece), bf16) for n in (cube, cube, chips // cube)
        ]
    scratch += [
        pltpu.SemaphoreType.DMA((11,)),
        pltpu.SemaphoreType.DMA((16,)),
        pltpu.SemaphoreType.DMA((16,)),
    ]
    scratch += [pltpu.SemaphoreType.DMA((2, 2, span, 2)) for _ in range(4)]
    scratch += [pltpu.SemaphoreType.DMA((6, max(cube, chips // cube))) for _ in range(2)]
    return pl.pallas_call(
        functools.partial(paired_kernel, chips, span),
        out_shape=tuple(
            [jax.ShapeDtypeStruct(a.shape, bf16) for a in (q, k, v)]
            + [
                jax.ShapeDtypeStruct((cube, rank, piece), bf16)
                for piece in (q_piece, q_piece, v_piece, v_piece)
            ]
        ),
        in_specs=[hbm] * 10,
        out_specs=(vmem,) * 7,
        scratch_shapes=scratch,
        compiler_params=pltpu.CompilerParams(
            collective_id=1, has_side_effects=True, vmem_limit_bytes=61 * 1024 * 1024
        ),
        name="paired_backward",
    )(q, do, k, v, seg, x, q_down, v_down, q_up, v_up)


def on_device(
    projected_queries,
    projected_keys,
    projected_values,
    output_gradient,
    normed_layer_input,
    segment,
    query_adapter_down,
    query_adapter_up,
    value_adapter_down,
    value_adapter_up,
):
    tok_rows = projected_queries.shape[0]
    query_width = projected_queries.shape[2]
    key_width = projected_keys.shape[2]
    key_value_heads = key_width // HEAD_SIZE
    group_devs = GROUP // tok_rows
    ctx = lax.axis_size("ctx")
    paired = (
        lax.axis_size("fsdp") == 1
        and group_devs % 4 == 0
        and ctx % (2 * group_devs) == 0
        and key_value_heads == 2
        and tok_rows == HEAD_SIZE
        and query_width % (ctx * HEAD_SIZE // 2) == 0
        and normed_layer_input.shape[1] % (ctx * HEAD_SIZE) == 0
    )
    if paired:
        results = paired_backward(
            projected_queries,
            output_gradient,
            projected_keys,
            projected_values,
            segment.reshape(-1, tok_rows),
            normed_layer_input,
            query_adapter_down,
            value_adapter_down,
            query_adapter_up,
            value_adapter_up,
            group_devs // 2,
        )
        outs = [
            jax.ShapeDtypeStruct(a.shape, jnp.bfloat16)
            for a in (projected_queries, projected_keys, projected_values)
        ] + [
            jax.ShapeDtypeStruct(a.shape, jnp.float32)
            for a in (
                query_adapter_down,
                query_adapter_up,
                value_adapter_down,
                value_adapter_up,
            )
        ]
        return deliver(results, outs)
    query_grad, key_grad, value_grad = attention_backward(
        projected_queries.transpose(1, 0, 2),
        output_gradient.transpose(1, 0, 2),
        projected_keys.transpose(1, 0, 2),
        projected_values.transpose(1, 0, 2),
        segment.reshape(-1, tok_rows),
        group_devs,
    )
    grad_query = query_grad.transpose(1, 0, 2)
    grad_key = key_grad.transpose(1, 0, 2)
    grad_value = value_grad.transpose(1, 0, 2)
    adapter_input = lax.psum(
        (
            jnp.dot(normed_layer_input, query_adapter_down.T, preferred_element_type=jnp.float32),
            jnp.dot(normed_layer_input, value_adapter_down.T, preferred_element_type=jnp.float32),
        ),
        "fsdp",
    )
    query_down_part = adapter_input[0].astype(jnp.bfloat16)
    value_down_part = adapter_input[1].astype(jnp.bfloat16)
    query_flattened_rows = grad_query.reshape(tok_rows, -1)
    value_flattened_rows = grad_value.reshape(tok_rows, -1)
    adapter_rank_rows = query_adapter_up.shape[0]
    adapter_output = lax.psum(
        (
            jnp.dot(
                query_flattened_rows,
                query_adapter_up.reshape(adapter_rank_rows, -1).T,
                preferred_element_type=jnp.float32,
            ),
            jnp.dot(
                value_flattened_rows,
                value_adapter_up.reshape(adapter_rank_rows, -1).T,
                preferred_element_type=jnp.float32,
            ),
        ),
        "fsdp",
    )
    query_up_part = adapter_output[0].astype(jnp.bfloat16)
    value_up_part = adapter_output[1].astype(jnp.bfloat16)
    local_down_query = jnp.dot(
        query_up_part.T, normed_layer_input, preferred_element_type=jnp.float32
    )
    local_up_query = jnp.dot(
        query_down_part.T, query_flattened_rows, preferred_element_type=jnp.float32
    ).reshape(adapter_rank_rows, 2, -1)
    local_down_value = jnp.dot(
        value_up_part.T, normed_layer_input, preferred_element_type=jnp.float32
    )
    local_up_value = jnp.dot(
        value_down_part.T, value_flattened_rows, preferred_element_type=jnp.float32
    ).reshape(adapter_rank_rows, 2, -1)
    gradient_totals = lax.psum(
        (local_down_query, local_up_query, local_down_value, local_up_value), "ctx"
    )
    return (
        grad_query,
        grad_key,
        grad_value,
        adapter_scale * gradient_totals[0],
        adapter_scale * gradient_totals[1],
        adapter_scale * gradient_totals[2],
        adapter_scale * gradient_totals[3],
    )


def solution(mesh):
    in_specs = (
        P(("rep", "ctx"), None, "fsdp"),
        P(("rep", "ctx"), None, "fsdp"),
        P(("rep", "ctx"), None, "fsdp"),
        P(("rep", "ctx"), None, "fsdp"),
        P(("rep", "ctx"), "fsdp"),
        P("rep"),
        P(None, "fsdp"),
        P(None, None, "fsdp"),
        P(None, "fsdp"),
        P(None, None, "fsdp"),
    )
    out_specs = (
        P(("rep", "ctx"), None, "fsdp"),
        P(("rep", "ctx"), None, "fsdp"),
        P(("rep", "ctx"), None, "fsdp"),
        P("rep", "fsdp"),
        P("rep", None, "fsdp"),
        P("rep", "fsdp"),
        P("rep", None, "fsdp"),
    )
    return jax.shard_map(
        on_device, mesh=mesh, in_specs=in_specs, out_specs=out_specs, check_vma=False
    )
```
